32 devices in a mesh: batch: 2 (over x), ctx: 16 (over z, y, core).
Axes of the slice: x: 2, y: 2, z: 4, core: 2. Of those that a mesh axis runs over, the one named last changes fastest.
Arguments:
- layer_input: bfloat16 [4, 2, 1536, 768], P('batch', None, 'ctx'), may hold values from -6 to 6
- cotangent: bfloat16 [4, 2, 1536, 768], P('batch', None, 'ctx'), may hold values from -6 to 6
- prefix: int32 [4], P('batch'), may hold values from 153 to 768, as said below
- block_size: int32 [4], P('batch'), may hold values from 4 to 16, as said below
- ln1_gain: bfloat16 [768], P(('batch', 'ctx')), may hold values from 0.5 to 1.5
- ln1_bias: bfloat16 [768], P(('batch', 'ctx')), may hold values from -1.75 to 1.75
- qkv_weight: bfloat16 [768, 2304], P(('batch', 'ctx')), may hold values from -0.21875 to 0.21875
- qkv_bias: bfloat16 [2304], P(('batch', 'ctx')), may hold values from -0.1875 to 0.1875
- out_weight: bfloat16 [768, 768], P(('batch', 'ctx')), may hold values from -0.625 to 0.625
- out_bias: bfloat16 [768], P(('batch', 'ctx')), may hold values from -0.625 to 0.625
- ln2_gain: bfloat16 [768], P(('batch', 'ctx')), may hold values from 0.5 to 1.5
- ln2_bias: bfloat16 [768], P(('batch', 'ctx')), may hold values from -1.75 to 1.75
- up_weight: bfloat16 [768, 3072], P(('batch', 'ctx')), may hold values from -0.21875 to 0.21875
- up_bias: bfloat16 [3072], P(('batch', 'ctx')), may hold values from -1.75 to 1.75
- down_weight: bfloat16 [3072, 768], P(('batch', 'ctx')), may hold values from -0.109375 to 0.109375
- down_bias: bfloat16 [768], P(('batch', 'ctx')), may hold values from -1.75 to 1.75
Outputs:
- block_out: bfloat16 [4, 2, 1536, 768], P('batch', None, 'ctx')
- grad_input: bfloat16 [4, 2, 1536, 768], P('batch', None, 'ctx')
- grad_ln1_gain: float32 [768], P(('batch', 'ctx'))
- grad_ln1_bias: float32 [768], P(('batch', 'ctx'))
- grad_qkv_weight: float32 [768, 2304], P(('batch', 'ctx'))
- grad_qk_bias: float32 [1536], P(('batch', 'ctx'))
- grad_value_bias: float32 [768], P(('batch', 'ctx'))
- grad_out_weight: float32 [768, 768], P(('batch', 'ctx'))
- grad_out_bias: float32 [768], P(('batch', 'ctx'))
- grad_ln2_gain: float32 [768], P(('batch', 'ctx'))
- grad_ln2_bias: float32 [768], P(('batch', 'ctx'))
- grad_up_weight: float32 [768, 3072], P(('batch', 'ctx'))
- grad_up_bias: float32 [3072], P(('batch', 'ctx'))
- grad_down_weight: float32 [3072, 768], P(('batch', 'ctx'))
- grad_down_bias: float32 [768], P(('batch', 'ctx'))
The draws below stay inside these ranges and needn't reach their ends.
Inputs may be any that keep to these rules, and one draw needn't show every extreme that they name: `prefix`: per sequence, from a tenth to a half of 1536; in every draw some sequence has exactly 153 and some exactly 768. `block_size`: each value is 4, 8 or 16, and all three occur in every draw.
All inputs are finite; a program needn't handle non-finite values.
Results may differ from the reference program's by a relative error of at most 0.019.
Values may be sent and summed in bfloat16 or wider, within the bound.
No kernel may reach another device: no remote copies, remote signals or barrier semaphores. Data moves between devices by JAX's collectives and lax.ppermute only.
A program may use at most 256 MiB of HBM per device.

```python
import jax
import jax.numpy as jnp
from jax import lax

D = 768
HEADS = 12
HEAD_DIM = 64
FF = 3072
SEQS = 4
LENGTH = 1536


def draw_prefix(key, part):
    values = jax.random.randint(key, (SEQS,), LENGTH // 10, LENGTH // 2 + 1, dtype=jnp.int32)
    shuffled = jax.random.permutation(jax.random.fold_in(key, 7), SEQS)
    values = values.at[shuffled[0]].set(LENGTH // 2)
    values = values.at[shuffled[1]].set(LENGTH // 10)
    return values.astype(jnp.int32)


def draw_block_size(key, part):
    offset = jax.random.randint(jax.random.fold_in(key, 11), (), 0, 3, dtype=jnp.int32)
    levels = (offset + jnp.arange(SEQS, dtype=jnp.int32)) % 3
    return jnp.where(levels == 0, 4, jnp.where(levels == 1, 8, 16)).astype(jnp.int32)


def shard_levels(key, dims, cuts, least, top_value):
    def one(position, shards_of):
        heights = jax.random.uniform(jax.random.fold_in(jax.random.fold_in(key, 6), position), (shards_of,), jnp.float32, least / len(cuts), top_value / len(cuts))
        return jnp.repeat(jnp.exp(heights), dims[position] // shards_of).reshape((-1,) + (1,) * (len(dims) - position - 1))

    loudness = one(*cuts[0])
    for cut in cuts[1:]:
        loudness = loudness * one(*cut)
    return loudness


def bell_draw(rng, shape, scale, reach, cuts=(), kind=jnp.bfloat16):
    array = jax.random.normal(rng, shape, jnp.float32) * scale
    if len(cuts) > 0:
        array = shard_levels(rng, shape, cuts, -0.22, 0.18) * array
    return jnp.clip(array, min=-reach, max=reach).astype(kind)


def setup_inputs(seed: int = 0) -> dict:
    key_list = jax.random.split(jax.random.key(seed), 17)
    return {
        "layer_input": bell_draw(key_list[0], (SEQS, 2, LENGTH, D), 1.0, 6.0, ((0, 2), (2, 16))),
        "cotangent": bell_draw(key_list[1], (SEQS, 2, LENGTH, D), 1.0, 6.0, ((0, 2), (2, 16))),
        "prefix": draw_prefix(jax.random.fold_in(key_list[16], 71), 0),
        "block_size": draw_block_size(jax.random.fold_in(key_list[16], 71), 0),
        "ln1_gain": jnp.clip(1.0 + 0.1 * jax.random.normal(key_list[4], (D,), jnp.float32), 0.5, 1.5).astype(jnp.bfloat16),
        "ln1_bias": bell_draw(key_list[5], (D,), 0.3, 1.75, ((0, 32),)),
        "qkv_weight": bell_draw(key_list[6], (D, 3 * D), D ** -0.5, 0.21875, ((0, 32),)),
        "qkv_bias": bell_draw(key_list[7], (3 * D,), 0.03, 0.1875, ((0, 32),)),
        "out_weight": bell_draw(key_list[8], (D, D), (D // 8) ** -0.5, 0.625, ((0, 32),)),
        "out_bias": bell_draw(key_list[9], (D,), 0.1, 0.625, ((0, 32),)),
        "ln2_gain": jnp.clip(1.0 + 0.1 * jax.random.normal(key_list[10], (D,), jnp.float32), 0.5, 1.5).astype(jnp.bfloat16),
        "ln2_bias": bell_draw(key_list[11], (D,), 0.3, 1.75, ((0, 32),)),
        "up_weight": bell_draw(key_list[12], (D, FF), D ** -0.5, 0.21875, ((0, 32),)),
        "up_bias": bell_draw(key_list[13], (FF,), 0.3, 1.75, ((0, 32),)),
        "down_weight": bell_draw(key_list[14], (FF, D), FF ** -0.5, 0.109375, ((0, 32),)),
        "down_bias": bell_draw(key_list[15], (D,), 0.3, 1.75, ((0, 32),)),
    }


SCALE = 0.125
NEGATIVE = -1e+30
EPSILON = 1e-05
THETA = 10000.0
HIGHEST = lax.Precision.HIGHEST

@jax.custom_vjp
def low(v):
    return lax.optimization_barrier(v.astype(jnp.bfloat16)).astype(jnp.float32)

@jax.custom_vjp
def low_back(v):
    return v

def low_keep(v):
    return (low(v), None)

def low_pass(kept, grad):
    return (grad,)

def back_keep(v):
    return (v, None)

def back_low(kept, grad):
    return (low(grad),)
low.defvjp(low_keep, low_pass)
low_back.defvjp(back_keep, back_low)

def layer_norm(values, gain_vec, bias_add):
    center = values - lax.optimization_barrier(jnp.mean(values, -1, keepdims=True))
    spread = lax.optimization_barrier(jnp.mean(center * center, -1, keepdims=True))
    return center * lax.rsqrt(spread + EPSILON) * gain_vec + bias_add

def rotary_tables(positions):
    half_dim = HEAD_DIM // 2
    inverse = 1.0 / THETA ** (jnp.arange(half_dim, dtype=jnp.float32) / half_dim)
    angles = positions.astype(jnp.float32)[:, None] * inverse[None, :]
    return (jnp.cos(angles)[:, None, :], jnp.sin(angles)[:, None, :])

def rotate(values, cos_tab, sin_tab):
    half_dim = values.shape[-1] // 2
    first_half = values[..., :half_dim]
    second = values[..., half_dim:]
    return jnp.concatenate([first_half * cos_tab - second * sin_tab, second * cos_tab + first_half * sin_tab], -1)

def allowed_pairs(query_copy, query_pos, key_copy, key_pos, prefix_len, block_len):
    query_block = (query_pos // block_len)[:, None]
    key_block = (key_pos // block_len)[None, :]
    query_at = query_pos[:, None]
    key_at = key_pos[None, :]
    noisy_key = (key_copy == 0)[None, :]
    for_noisy = jnp.where(noisy_key, key_block == query_block, (key_block < query_block) | (key_at < prefix_len))
    clean_rule = (query_at < prefix_len) & (key_at < prefix_len) | (query_at >= prefix_len) & (key_block <= query_block)
    for_clean = jnp.logical_not(noisy_key) & clean_rule
    return jnp.where((query_copy == 0)[:, None], for_noisy, for_clean)

def layer(inputs, params, prefix_len, block_len):
    gain_one, bias_one, qkv_mat, qkv_add, out_mat, out_add, gain_two, bias_two, up_mat, up_add, down_mat, down_add = params
    seq_len = inputs.shape[1]
    width = inputs.shape[2]
    total_rows = 2 * seq_len
    rows = inputs.reshape(total_rows, width)
    normed = low(layer_norm(rows, gain_one, bias_one))
    projected = low_back(jnp.dot(normed, qkv_mat, precision=HIGHEST)) + qkv_add
    positions = jnp.arange(total_rows, dtype=jnp.int32) % seq_len
    copies = jnp.arange(total_rows, dtype=jnp.int32) // seq_len
    cos_tab, sin_tab = rotary_tables(positions)
    query_rows = low(rotate(projected[:, :width].reshape(total_rows, HEADS, HEAD_DIM), cos_tab, sin_tab))
    key_rows = low(rotate(projected[:, width:2 * width].reshape(total_rows, HEADS, HEAD_DIM), cos_tab, sin_tab))
    value_rows = low(projected[:, 2 * width:].reshape(total_rows, HEADS, HEAD_DIM))
    block_rows = min(512, total_rows)

    def attend(block_index):
        first_row = block_index * block_rows
        query_block = lax.dynamic_slice_in_dim(query_rows, first_row, block_rows, 0)
        block_pos = lax.dynamic_slice_in_dim(positions, first_row, block_rows, 0)
        block_copy = lax.dynamic_slice_in_dim(copies, first_row, block_rows, 0)
        allowed = allowed_pairs(block_copy, block_pos, copies, positions, prefix_len, block_len)[:, None, :]
        raw_scores = low_back(jnp.einsum('rhd,khd->rhk', query_block, key_rows, precision=HIGHEST))
        scores = jnp.where(allowed, raw_scores * SCALE, NEGATIVE)
        shifted = jnp.exp(scores - lax.optimization_barrier(jnp.max(scores, -1, keepdims=True)))
        probs_low = low(shifted / lax.optimization_barrier(jnp.sum(shifted, -1, keepdims=True)))
        return jnp.einsum('rhk,khd->rhd', probs_low, value_rows, precision=HIGHEST)
    attn = lax.map(jax.checkpoint(attend), jnp.arange(total_rows // block_rows, dtype=jnp.int32))
    attn_low = low(low_back(attn.reshape(total_rows, width)))
    hidden = rows + low_back(jnp.dot(attn_low, out_mat, precision=HIGHEST)) + out_add
    normed_two = low(layer_norm(hidden, gain_two, bias_two))
    upper = low_back(jnp.dot(normed_two, up_mat, precision=HIGHEST)) + up_add
    activ = low(jax.nn.gelu(upper, approximate=True))
    output = hidden + low_back(jnp.dot(activ, down_mat, precision=HIGHEST)) + down_add
    return output.reshape(2, seq_len, width)

def reference(layer_input, cotangent, prefix, block_size, ln1_gain, ln1_bias, qkv_weight, qkv_bias, out_weight, out_bias, ln2_gain, ln2_bias, up_weight, up_bias, down_weight, down_bias):
    params = tuple((weight_in.astype(jnp.float32) for weight_in in (ln1_gain, ln1_bias, qkv_weight, qkv_bias, out_weight, out_bias, ln2_gain, ln2_bias, up_weight, up_bias, down_weight, down_bias)))

    def per_sequence(running, seq_item):
        seq_in, seq_cot, prefix_len, block_len = seq_item

        def forward(seq_rows, *weights_in):
            return layer(seq_rows, weights_in, prefix_len, block_len)
        output, backward = jax.vjp(forward, seq_in.astype(jnp.float32), *params)
        all_grads = backward(seq_cot.astype(jnp.float32))
        running = tuple((summed + fresh for summed, fresh in zip(running, all_grads[1:])))
        return (running, (output.astype(jnp.bfloat16), all_grads[0].astype(jnp.bfloat16)))
    start_grads = tuple((jnp.zeros_like(weight_in) for weight_in in params))
    weight_grads, (outputs, input_grads) = lax.scan(per_sequence, start_grads, (layer_input, cotangent, prefix, block_size))
    split_at = 2 * D
    bias_grad = weight_grads[3]
    return (outputs, input_grads, weight_grads[0], weight_grads[1], weight_grads[2], bias_grad[:split_at], bias_grad[split_at:]) + tuple(weight_grads[4:])
```

```python
import functools

import jax
import jax.numpy as jnp
from jax import lax
from jax.experimental import pallas as pl
from jax.experimental.pallas import tpu as pltpu
from jax.sharding import PartitionSpec as P

HEADS = 12
HEAD_DIM = 64
SCALE = 0.125
NEGATIVE = -1e30
EPSILON = 1e-05
THETA = 10000.0
LANES = 128
BF16 = jnp.bfloat16
F32 = jnp.float32
VMEM_LIMIT = 56 * 1024 * 1024
NT = (((1,), (1,)), ((), ()))


def swap_halves(tile):
    lane = lax.broadcasted_iota(jnp.int32, tile.shape, 1)
    return jnp.where(lane % 64 < 32, pltpu.roll(tile, LANES - 32, 1), pltpu.roll(tile, 32, 1))


def project_kernel(x_ref, gain_ref, bias_ref, w_ref, add_ref, cos_ref, sin_ref, out_ref, unit_ref, *, start, turned):
    x = x_ref[...].astype(F32)
    center = x - jnp.mean(x, -1, keepdims=True)
    spread = jnp.mean(center * center, -1, keepdims=True)
    unit = center * lax.rsqrt(spread + EPSILON)
    unit_ref[...] = unit.astype(BF16)
    normed = (unit * gain_ref[...] + bias_ref[...]).astype(BF16)
    cos_tab, sin_tab = cos_ref[...], sin_ref[...]
    total = jnp.dot(normed, w_ref[:, start:], preferred_element_type=F32) + add_ref[:, start:]
    for tile in range(total.shape[1] // LANES):
        part = total[:, tile * LANES : (tile + 1) * LANES]
        if tile * LANES < turned:
            part = part * cos_tab + swap_halves(part) * sin_tab
        out_ref[:, tile * LANES : (tile + 1) * LANES] = part.astype(BF16)


def project(x, gain, bias, weight, add, cos_tab, sin_tab, start, turned, block):
    rows, width = x.shape
    columns = weight.shape[1] - start
    row_map = lambda i: (i, 0)
    fixed = lambda i: (0, 0)
    return pl.pallas_call(
        functools.partial(project_kernel, start=start, turned=turned),
        grid=(rows // block,),
        in_specs=[
            pl.BlockSpec((block, width), row_map),
            pl.BlockSpec((1, width), fixed),
            pl.BlockSpec((1, width), fixed),
            pl.BlockSpec(weight.shape, fixed),
            pl.BlockSpec((1, weight.shape[1]), fixed),
            pl.BlockSpec((block, LANES), row_map),
            pl.BlockSpec((block, LANES), row_map),
        ],
        out_specs=[pl.BlockSpec((block, columns), row_map), pl.BlockSpec((block, width), row_map)],
        out_shape=[jax.ShapeDtypeStruct((rows, columns), BF16), jax.ShapeDtypeStruct((rows, width), BF16)],
        compiler_params=pltpu.CompilerParams(vmem_limit_bytes=VMEM_LIMIT),
        cost_estimate=pl.CostEstimate(
            flops=2 * rows * width * columns,
            bytes_accessed=2 * (rows * (2 * width + columns) + width * columns),
            transcendentals=rows,
        ),
        name="project",
    )(x, gain, bias, weight, add, cos_tab, sin_tab)


def head_parts(rows, factor):
    rows = rows.astype(F32) * factor
    lane = lax.broadcasted_iota(jnp.int32, rows.shape, 1)
    first = lane < HEAD_DIM
    return (jnp.where(first, rows, 0.0).astype(BF16), jnp.where(first, 0.0, rows).astype(BF16))


def flipped(tile):
    return tile.astype(F32).T.astype(BF16)


def nt_dot(a, b):
    return lax.dot_general(a, b, NT, preferred_element_type=F32)


def own_mask(limit_ref, noisy_rows, rows):
    at = lax.broadcasted_iota(jnp.int32, (noisy_rows, rows), 0)
    return (at >= limit_ref[1:2, :]) & (at < limit_ref[2:3, :])


def attend_kernel(count_ref, q_ref, kn_ref, vn_ref, kc_ref, vc_ref, limit_ref, o_ref, log_ref, *, block):
    rows = q_ref.shape[0]
    queries = head_parts(q_ref[...], SCALE)
    limit = limit_ref[0:1, :]

    def fold(state, keys, values, mask):
        values_flipped = flipped(values)
        out = []
        for h in range(2):
            best, total, acc = state[h]
            scores = jnp.where(mask, nt_dot(keys, queries[h]), NEGATIVE)
            new_best = jnp.maximum(best, jnp.max(scores, 0, keepdims=True))
            weights = jnp.exp(scores - new_best)
            factor = jnp.exp(best - new_best)
            total = total * factor + jnp.sum(weights, 0, keepdims=True)
            acc = acc * factor + jnp.dot(
                values_flipped[h * HEAD_DIM : (h + 1) * HEAD_DIM], weights.astype(BF16), preferred_element_type=F32
            )
            out.append((new_best, total, acc))
        return tuple(out)

    def step(index, state):
        first = pl.multiple_of(index * block, block)
        at = lax.broadcasted_iota(jnp.int32, (block, rows), 0) + index * block
        return fold(state, kc_ref[pl.ds(first, block), :], vc_ref[pl.ds(first, block), :], at < limit)

    start = (
        jnp.full((1, rows), NEGATIVE, F32),
        jnp.zeros((1, rows), F32),
        jnp.zeros((HEAD_DIM, rows), F32),
    )
    state = lax.fori_loop(0, count_ref[0], step, (start, start))
    state = fold(state, kn_ref[...], vn_ref[...], own_mask(limit_ref, kn_ref.shape[0], rows))
    o_ref[...] = jnp.concatenate([acc / total for _, total, acc in state], 0).T.astype(BF16)
    for h in range(2):
        log_ref[0, h : h + 1, :] = state[h][0] + jnp.log(state[h][1])


def attend(count, own, clean, limits, block):
    rows = own.shape[0]
    length = clean.shape[0]
    pairs = own.shape[1] // (3 * LANES)
    spec = pltpu.PrefetchScalarGridSpec(
        num_scalar_prefetch=1,
        grid=(pairs,),
        in_specs=[
            pl.BlockSpec((rows, LANES), lambda p, c: (0, p)),
            pl.BlockSpec((rows // 2, LANES), lambda p, c: (0, pairs + p)),
            pl.BlockSpec((rows // 2, LANES), lambda p, c: (0, 2 * pairs + p)),
            pl.BlockSpec((length, LANES), lambda p, c: (0, p)),
            pl.BlockSpec((length, LANES), lambda p, c: (0, pairs + p)),
            pl.BlockSpec((8, rows), lambda p, c: (0, 0)),
        ],
        out_specs=[
            pl.BlockSpec((rows, LANES), lambda p, c: (0, p)),
            pl.BlockSpec((1, 8, rows), lambda p, c: (p, 0, 0)),
        ],
    )
    return pl.pallas_call(
        functools.partial(attend_kernel, block=block),
        grid_spec=spec,
        out_shape=[
            jax.ShapeDtypeStruct((rows, pairs * LANES), BF16),
            jax.ShapeDtypeStruct((pairs, 8, rows), F32),
        ],
        compiler_params=pltpu.CompilerParams(vmem_limit_bytes=VMEM_LIMIT),
        cost_estimate=pl.CostEstimate(
            flops=pairs * rows * (length + rows // 2) * 2048,
            bytes_accessed=2 * pairs * LANES * (2 * length + 3 * rows),
            transcendentals=2 * pairs * rows * length,
        ),
        name="attend",
    )(count, own, own, own, clean, clean, limits)


def attend_back_kernel(
    count_ref, q_ref, kn_ref, vn_ref, kc_ref, vc_ref, limit_ref, o_ref, do_ref, log_ref,
    cos_own_ref, sin_own_ref, cos_ref, sin_ref, dkv_ref, down_ref, sum_ref, *, block
):
    rows = q_ref.shape[0]
    noisy = kn_ref.shape[0]
    width = dkv_ref.shape[1] // 2
    length = kc_ref.shape[0]
    here = pl.multiple_of(pl.program_id(0) * LANES, LANES)
    queries = head_parts(q_ref[...], SCALE)
    grads = head_parts(do_ref[...], 1.0)
    limit = limit_ref[0:1, :]
    product = do_ref[...].astype(F32) * o_ref[...].astype(F32)
    lane = lax.broadcasted_iota(jnp.int32, (8, LANES), 1)
    deltas = []
    for h in range(2):
        ones = jnp.where((lane < HEAD_DIM) == (h == 0), 1.0, 0.0)
        deltas.append(
            lax.dot_general(ones, product, NT, precision=lax.Precision.HIGHEST, preferred_element_type=F32)[0:1]
        )

    def fold(dq, keys, values, mask):
        keys_flipped = flipped(keys)
        dk = dv = None
        out = []
        for h in range(2):
            scores = nt_dot(keys, queries[h])
            probs = jnp.where(mask, jnp.exp(scores - log_ref[0, h : h + 1, :]), 0.0)
            inner = nt_dot(values, grads[h])
            slopes = (probs * (inner - deltas[h])).astype(BF16)
            dv_new = jnp.dot(probs.astype(BF16), grads[h], preferred_element_type=F32)
            dk_new = jnp.dot(slopes, queries[h], preferred_element_type=F32)
            dv = dv_new if dv is None else dv + dv_new
            dk = dk_new if dk is None else dk + dk_new
            out.append(
                dq[h]
                + jnp.dot(keys_flipped[h * HEAD_DIM : (h + 1) * HEAD_DIM], slopes, preferred_element_type=F32)
            )
        return tuple(out), dk, dv

    def unturn(grad, cos_tab, sin_tab):
        return grad * cos_tab - swap_halves(grad) * sin_tab

    def step(index, carry):
        dq, sum_k, sum_v = carry
        first = pl.multiple_of(index * block, block)
        where = pl.ds(first, block)
        at = lax.broadcasted_iota(jnp.int32, (block, rows), 0) + index * block
        dq, dk, dv = fold(dq, kc_ref[where, :], vc_ref[where, :], at < limit)
        dk = unturn(dk, cos_ref[where, :], sin_ref[where, :])
        dkv_ref[where, pl.ds(here, LANES)] = dk.astype(BF16)
        dkv_ref[where, pl.ds(width + here, LANES)] = dv.astype(BF16)
        return dq, sum_k + jnp.sum(dk, 0, keepdims=True), sum_v + jnp.sum(dv, 0, keepdims=True)

    zero_q = jnp.zeros((HEAD_DIM, rows), F32)
    zero_sum = jnp.zeros((1, LANES), F32)
    dq, sum_k, sum_v = lax.fori_loop(0, count_ref[0], step, ((zero_q, zero_q), zero_sum, zero_sum))

    def blank(index, carry):
        where = pl.ds(pl.multiple_of(index * block, block), block)
        dkv_ref[where, pl.ds(here, LANES)] = jnp.zeros((block, LANES), BF16)
        dkv_ref[where, pl.ds(width + here, LANES)] = jnp.zeros((block, LANES), BF16)
        return carry

    lax.fori_loop(count_ref[0], length // block, blank, 0)
    dq, dk, dv = fold(dq, kn_ref[...], vn_ref[...], own_mask(limit_ref, noisy, rows))
    dk = unturn(dk, cos_own_ref[:noisy, :], sin_own_ref[:noisy, :])
    dq = unturn(jnp.concatenate(dq, 0).T * SCALE, cos_own_ref[...], sin_own_ref[...])
    zeros = jnp.zeros((rows - noisy, LANES), BF16)
    for part, grad in enumerate((dq, dk, dv)):
        down_ref[: grad.shape[0], pl.ds(part * width + here, LANES)] = grad.astype(BF16)
        if part > 0:
            down_ref[noisy:, pl.ds(part * width + here, LANES)] = zeros
    sums = (
        jnp.sum(dq, 0, keepdims=True),
        sum_k + jnp.sum(dk, 0, keepdims=True),
        sum_v + jnp.sum(dv, 0, keepdims=True),
    )
    for part in range(3):
        sum_ref[:, pl.ds(part * width + here, LANES)] = jnp.broadcast_to(sums[part], (8, LANES))


def attend_back(count, own, clean, limits, attn, grad, log_total, cos_own, sin_own, cos_tab, sin_tab, block):
    rows = own.shape[0]
    length, both = clean.shape
    pairs = own.shape[1] // (3 * LANES)
    spec = pltpu.PrefetchScalarGridSpec(
        num_scalar_prefetch=1,
        grid=(pairs,),
        in_specs=[
            pl.BlockSpec((rows, LANES), lambda p, c: (0, p)),
            pl.BlockSpec((rows // 2, LANES), lambda p, c: (0, pairs + p)),
            pl.BlockSpec((rows // 2, LANES), lambda p, c: (0, 2 * pairs + p)),
            pl.BlockSpec((length, LANES), lambda p, c: (0, p)),
            pl.BlockSpec((length, LANES), lambda p, c: (0, pairs + p)),
            pl.BlockSpec((8, rows), lambda p, c: (0, 0)),
            pl.BlockSpec((rows, LANES), lambda p, c: (0, p)),
            pl.BlockSpec((rows, LANES), lambda p, c: (0, p)),
            pl.BlockSpec((1, 8, rows), lambda p, c: (p, 0, 0)),
            pl.BlockSpec((rows, LANES), lambda p, c: (0, 0)),
            pl.BlockSpec((rows, LANES), lambda p, c: (0, 0)),
            pl.BlockSpec((length, LANES), lambda p, c: (0, 0)),
            pl.BlockSpec((length, LANES), lambda p, c: (0, 0)),
        ],
        out_specs=[
            pl.BlockSpec((length, both), lambda p, c: (0, 0)),
            pl.BlockSpec((rows, own.shape[1]), lambda p, c: (0, 0)),
            pl.BlockSpec((8, own.shape[1]), lambda p, c: (0, 0)),
        ],
    )
    return pl.pallas_call(
        functools.partial(attend_back_kernel, block=block),
        grid_spec=spec,
        out_shape=[
            jax.ShapeDtypeStruct((length, both), BF16),
            jax.ShapeDtypeStruct(own.shape, BF16),
            jax.ShapeDtypeStruct((8, own.shape[1]), F32),
        ],
        compiler_params=pltpu.CompilerParams(vmem_limit_bytes=VMEM_LIMIT),
        cost_estimate=pl.CostEstimate(
            flops=pairs * rows * (length + rows // 2) * 5120,
            bytes_accessed=2 * pairs * LANES * (5 * length + 8 * rows),
            transcendentals=2 * pairs * rows * length,
        ),
        name="attend_back",
    )(count, own, own, own, clean, clean, limits, attn, grad, log_total, cos_own, sin_own, cos_tab, sin_tab)


def feed_forward_kernel(
    attn_ref, x_ref, top_ref, up_ref, down_ref, out_ref, vec_ref,
    block_out_ref, hidden_grad_ref, attn_grad_ref, weights_ref,
    hidden, unit, inverse, normed, normed_flipped, lowered, grad_normed,
    up_grads, down_grads, out_grads, vec_grads, sums, up_sems, down_sems, last_sems
):
    chunk = pl.program_id(0)
    chunks = pl.num_programs(0)
    width = x_ref.shape[1]

    @pl.when(chunk == 0)
    def _():
        value = (
            x_ref[...].astype(F32)
            + jnp.dot(attn_ref[...], out_ref[...], preferred_element_type=F32)
            + vec_ref[0:1, :]
        )
        hidden[...] = value
        center = value - jnp.mean(value, -1, keepdims=True)
        scale = lax.rsqrt(jnp.mean(center * center, -1, keepdims=True) + EPSILON)
        inverse[...] = scale
        unit[...] = center * scale
        scaled = unit[...] * vec_ref[1:2, :] + vec_ref[2:3, :]
        normed[...] = scaled.astype(BF16)
        normed_flipped[...] = scaled.T.astype(BF16)
        lowered[...] = jnp.zeros_like(lowered)
        grad_normed[...] = jnp.zeros_like(grad_normed)
        sums[...] = jnp.zeros_like(sums)

    upper = jnp.dot(normed[...], up_ref[...], preferred_element_type=F32) + vec_ref[pl.ds(4 + chunk, 1), :]
    grad_activ = nt_dot(top_ref[...], down_ref[...])
    inner = jnp.tanh(0.7978845608028654 * (upper + 0.044715 * upper * upper * upper))
    activ = 0.5 * upper * (1.0 + inner)
    slope = 0.5 * (1.0 + inner) + 0.5 * upper * (1.0 - inner * inner) * 0.7978845608028654 * (
        1.0 + 0.134145 * upper * upper
    )
    grad_upper = grad_activ * slope
    grad_low = grad_upper.astype(BF16)
    sums[pl.ds(4 + chunk, 1), :] = jnp.sum(grad_upper, 0, keepdims=True)
    lowered[...] += jnp.dot(activ.astype(BF16), down_ref[...], preferred_element_type=F32)
    grad_normed[...] += nt_dot(grad_low, up_ref[...])
    up_grads[chunk] = jnp.dot(normed_flipped[...], grad_low, preferred_element_type=F32).astype(BF16)
    down_grads[chunk] = jnp.dot(activ.T.astype(BF16), top_ref[...], preferred_element_type=F32).astype(BF16)

    def copy_up(index):
        columns = pl.ds(pl.multiple_of(index * width, width), width)
        return pltpu.make_async_copy(up_grads.at[index], weights_ref.at[:, columns], up_sems.at[index])

    def copy_down(index):
        columns = pl.ds(pl.multiple_of((chunks + index) * width, width), width)
        return pltpu.make_async_copy(down_grads.at[index], weights_ref.at[:, columns], down_sems.at[index])

    copy_up(chunk).start()
    copy_down(chunk).start()

    @pl.when(chunk == chunks - 1)
    def _():
        top = top_ref[...].astype(F32)
        block_out_ref[...] = (hidden[...] + lowered[...] + vec_ref[3:4, :]).astype(BF16)
        grad = grad_normed[...]
        rows_unit = unit[...]
        sums[1:2, :] = jnp.sum(grad * rows_unit, 0, keepdims=True)
        sums[2:3, :] = jnp.sum(grad, 0, keepdims=True)
        sums[3:4, :] = jnp.sum(top, 0, keepdims=True)
        grad = grad * vec_ref[1:2, :]
        grad = inverse[...] * (
            grad - jnp.mean(grad, -1, keepdims=True) - rows_unit * jnp.mean(grad * rows_unit, -1, keepdims=True)
        )
        grad = top + grad
        hidden_grad_ref[...] = grad
        sums[0:1, :] = jnp.sum(grad, 0, keepdims=True)
        low = grad.astype(BF16)
        attn_grad_ref[...] = nt_dot(low, out_ref[...]).astype(BF16)
        out_grads[...] = jnp.dot(
            attn_ref[...].astype(F32).T.astype(BF16), low, preferred_element_type=F32
        ).astype(BF16)
        vec_grads[...] = sums[...].T.astype(BF16)
        first = 2 * chunks * width
        copies = [
            pltpu.make_async_copy(out_grads, weights_ref.at[:, pl.ds(first, width)], last_sems.at[0]),
            pltpu.make_async_copy(vec_grads, weights_ref.at[:, pl.ds(first + width, LANES)], last_sems.at[1]),
        ]
        for copy in copies:
            copy.start()
        for index in range(up_grads.shape[0]):
            copy_up(index).wait()
            copy_down(index).wait()
        for copy in copies:
            copy.wait()


def feed_forward(attn, x, top, weights, vectors, chunks):
    rows, width = x.shape
    fixed = lambda b: (0, 0)
    whole = pl.BlockSpec((rows, width), fixed)
    return pl.pallas_call(
        feed_forward_kernel,
        grid=(chunks,),
        in_specs=[
            whole,
            whole,
            whole,
            pl.BlockSpec((width, width), lambda b: (0, b)),
            pl.BlockSpec((width, width), lambda b: (0, chunks + b)),
            pl.BlockSpec((width, width), lambda b: (0, 2 * chunks)),
            pl.BlockSpec(vectors.shape, fixed),
        ],
        out_specs=[whole, whole, whole, pl.BlockSpec(memory_space=pl.ANY)],
        out_shape=[
            jax.ShapeDtypeStruct((rows, width), BF16),
            jax.ShapeDtypeStruct((rows, width), F32),
            jax.ShapeDtypeStruct((rows, width), BF16),
            jax.ShapeDtypeStruct(weights.shape, BF16),
        ],
        scratch_shapes=[
            pltpu.VMEM((rows, width), F32),
            pltpu.VMEM((rows, width), F32),
            pltpu.VMEM((rows, 1), F32),
            pltpu.VMEM((rows, width), BF16),
            pltpu.VMEM((width, rows), BF16),
            pltpu.VMEM((rows, width), F32),
            pltpu.VMEM((rows, width), F32),
            pltpu.VMEM((chunks, width, width), BF16),
            pltpu.VMEM((chunks, width, width), BF16),
            pltpu.VMEM((width, width), BF16),
            pltpu.VMEM((width, LANES), BF16),
            pltpu.VMEM((LANES, width), F32),
            pltpu.SemaphoreType.DMA((chunks,)),
            pltpu.SemaphoreType.DMA((chunks,)),
            pltpu.SemaphoreType.DMA((2,)),
        ],
        compiler_params=pltpu.CompilerParams(vmem_limit_bytes=VMEM_LIMIT),
        cost_estimate=pl.CostEstimate(
            flops=2 * rows * width * width * (6 * chunks + 3),
            bytes_accessed=4 * width * weights.shape[1] + 12 * rows * width,
            transcendentals=rows * width * chunks,
        ),
        name="feed_forward",
    )(attn, x, top, weights, weights, weights, vectors)


def pick(array, index, axis=0):
    return lax.dynamic_index_in_dim(array, index, axis, keepdims=False)


def ordered(flag, own, other, axis):
    return jnp.stack([jnp.where(flag == 0, own, other), jnp.where(flag == 0, other, own)], axis)


class Links:
    def __init__(self):
        self.count = lax.axis_size("ctx")
        self.deep = self.count // 4
        at = lax.axis_index("ctx")
        self.x = lax.axis_index("batch")
        self.core = at % 2
        self.y = (at // 2) % 2
        self.z = at // 4
        self.chip = at // 2

    def over_core(self, array):
        return lax.ppermute(array, "ctx", [(i, i ^ 1) for i in range(self.count)])

    def over_y(self, array):
        return lax.ppermute(array, "ctx", [(i, i ^ 2) for i in range(self.count)])

    def over_x(self, array):
        return lax.ppermute(array, "batch", [(0, 1), (1, 0)])

    def along_z(self, array, hop):
        count = self.count
        return lax.ppermute(array, "ctx", [(i, (i + 4 * hop) % count) for i in range(count)])

    def gather_z(self, piece):
        deep = self.deep
        whole = jnp.broadcast_to(piece[None], (deep,) + piece.shape)
        for hop in range(1, deep):
            whole = lax.dynamic_update_index_in_dim(whole, self.along_z(piece, hop), (self.z - hop) % deep, 0)
        return whole

    def gather_plane(self, piece):
        column = self.gather_z(piece)
        return ordered(self.y, column, self.over_y(column), 1)

    def gather(self, piece):
        plane = self.gather_plane(piece)
        return ordered(self.x, plane, self.over_x(plane), 0)

    def reduce_z(self, parts):
        total = pick(parts, self.z).astype(F32)
        for hop in range(1, self.deep):
            total = total + self.along_z(pick(parts, (self.z + hop) % self.deep), hop).astype(F32)
        return total

    def reduce_plane(self, parts):
        got = self.over_y(pick(parts, 1 - self.y, 1))
        mine = pick(parts, self.y, 1)
        return self.reduce_z((mine.astype(F32) + got.astype(F32)).astype(BF16))

    def reduce(self, parts):
        got = self.over_x(pick(parts, 1 - self.x))
        mine = pick(parts, self.x)
        return self.reduce_plane((mine.astype(F32) + got.astype(F32)).astype(BF16))


def unit_rows(values):
    center = values - jnp.mean(values, -1, keepdims=True)
    spread = jnp.mean(center * center, -1, keepdims=True)
    inverse = lax.rsqrt(spread + EPSILON)
    return center * inverse, inverse


def unit_back(grad, unit, inverse):
    return inverse * (
        grad - jnp.mean(grad, -1, keepdims=True) - unit * jnp.mean(grad * unit, -1, keepdims=True)
    )


def rotary_tables(positions):
    half_dim = HEAD_DIM // 2
    inverse = 1.0 / THETA ** (jnp.arange(half_dim, dtype=F32) / half_dim)
    angles = positions.astype(F32)[:, None] * jnp.tile(inverse, LANES // half_dim)[None, :]
    sign = jnp.where(jnp.arange(LANES) % HEAD_DIM < half_dim, -1.0, 1.0)
    return jnp.cos(angles), jnp.sin(angles) * sign[None, :]


def key_block(length):
    for block in (256, 128, 64, 32, 16):
        if length % block == 0:
            return block
    return length


def row_block(rows):
    for block in (512, 384, 256, 128, 64, 32, 16):
        if rows % block == 0:
            return block
    return rows


def dot(a, b):
    return jnp.dot(a, b, preferred_element_type=F32)


def dot_left(a, b):
    return lax.dot_general(a, b, (((0,), (0,)), ((), ())), preferred_element_type=F32)


def on_device(
    layer_input, cotangent, prefix, block_size, ln1_gain, ln1_bias, qkv_weight, qkv_bias, out_weight, out_bias,
    ln2_gain, ln2_bias, up_weight, up_bias, down_weight, down_bias,
):
    links = Links()
    core = links.core
    seqs, _, pos_dev, width = layer_input.shape
    devices = 2 * links.count
    length = links.count * pos_dev
    half = width // 2
    rows = 4 * pos_dev
    shard = ln1_gain.shape[0]
    hidden_shard = up_bias.shape[0]

    folds = hidden_shard // shard
    up_piece = up_weight.reshape(shard, devices, folds, shard).transpose(0, 2, 1, 3).reshape(shard, -1)
    down_piece = down_weight.reshape(folds, shard, width).transpose(1, 0, 2).reshape(shard, -1)
    vec_piece = jnp.stack(
        [out_bias, ln2_gain, ln2_bias, down_bias] + [up_bias[i * shard : (i + 1) * shard] for i in range(folds)], 1
    )
    vec_piece = jnp.pad(vec_piece, ((0, 0), (0, LANES - vec_piece.shape[1])))
    packed = jnp.concatenate([up_piece, down_piece, out_weight, vec_piece], 1)
    weights = lax.all_gather(packed, ("batch", "ctx"), axis=0, tiled=True)
    vectors = weights[:, -LANES:].T[: 4 + folds].astype(F32)

    split = qkv_weight.reshape(shard, 3, 2, half)
    vec_one = jnp.stack([ln1_gain, ln1_bias] + [qkv_bias[i * shard : (i + 1) * shard] for i in range(3)], 1)
    vec_one = jnp.pad(vec_one, ((0, 0), (0, LANES - vec_one.shape[1])))
    mine = jnp.concatenate([pick(split, core, 2).reshape(shard, 3 * half), vec_one], 1)
    theirs = jnp.concatenate([pick(split, 1 - core, 2).reshape(shard, 3 * half), vec_one], 1)
    piece = ordered(core, mine, links.over_core(theirs), 0).reshape(2 * shard, -1)
    qkv_mat = links.gather(piece).reshape(width, -1)
    vec_one = qkv_mat[:, 3 * half :].T.astype(F32)
    gain_one, bias_one = vec_one[0:1], vec_one[1:2]
    qkv_add = vec_one[2:5].reshape(3, devices, shard).transpose(1, 0, 2).reshape(3, 2, half)
    qkv_add = pick(qkv_add, core, 1).reshape(1, 3 * half)
    qkv_mat = qkv_mat[:, : 3 * half]

    lane_rows = links.gather_plane(layer_input[:, 1])
    lane_rows = ordered(core, lane_rows, links.over_core(lane_rows), 3)
    clean_inputs = lane_rows.transpose(2, 0, 1, 3, 4, 5).reshape(seqs, length, width)

    inputs_pair = ordered(core, layer_input, links.over_core(layer_input), 2).reshape(seqs, rows, width)

    cos_tab, sin_tab = rotary_tables(jnp.arange(length, dtype=jnp.int32))
    first_pos = links.chip * 2 * pos_dev
    cos_own = jnp.tile(lax.dynamic_slice_in_dim(cos_tab, first_pos, 2 * pos_dev, 0), (2, 1))
    sin_own = jnp.tile(lax.dynamic_slice_in_dim(sin_tab, first_pos, 2 * pos_dev, 0), (2, 1))
    block = key_block(length)
    at = jnp.arange(2 * pos_dev, dtype=jnp.int32)
    position = first_pos + at
    own_qkv, own_unit, clean_kv, clean_unit, limit_list, counts, attn_list, log_list = ([] for _ in range(8))
    for s in range(seqs):
        near = (position // block_size[s]) * block_size[s]
        after = near + block_size[s]
        noisy_limit = jnp.maximum(near, prefix[s])
        clean_limit = jnp.where(position < prefix[s], prefix[s], after)
        limit = jnp.concatenate([noisy_limit, clean_limit])
        none = jnp.zeros_like(at)
        limits = jnp.stack(
            [limit, jnp.concatenate([near - first_pos, none]), jnp.concatenate([after - first_pos, none])]
            + [jnp.zeros_like(limit)] * 5
        )
        count = jnp.minimum((jnp.max(limit) + block - 1) // block, length // block).reshape(1)
        own, unit = project(
            inputs_pair[s], gain_one, bias_one, qkv_mat, qkv_add, cos_own, sin_own, 0, width, row_block(rows)
        )
        clean, all_unit = project(
            clean_inputs[s], gain_one, bias_one, qkv_mat, qkv_add, cos_tab, sin_tab, half, half, row_block(length)
        )
        attn, log_total = attend(count, own, clean, limits, block)
        for kept, value in zip(
            (own_qkv, own_unit, clean_kv, clean_unit, limit_list, counts, attn_list, log_list),
            (own, unit, clean, all_unit, limits, count, attn, log_total),
        ):
            kept.append(value)

    attn_rows = jnp.stack(attn_list).reshape(seqs, 2, 2, pos_dev, half)
    attn_got = links.over_core(pick(attn_rows, 1 - core, 2))
    attn_low = ordered(core, pick(attn_rows, core, 2), attn_got, 3).reshape(-1, width)
    flat_inputs = layer_input.reshape(-1, width)
    output, grad_hidden, grad_attn, weight_grads = feed_forward(
        attn_low, flat_inputs, cotangent.reshape(-1, width), weights, vectors, folds
    )
    output = output.reshape(layer_input.shape)
    packed = lax.psum_scatter(weight_grads, ("batch", "ctx"), scatter_dimension=0, tiled=True).astype(F32)

    grad_split = grad_attn.reshape(-1, 2, half)
    grad_got = links.over_core(pick(grad_split, 1 - core, 1))
    grad_rows = ordered(
        core,
        pick(grad_split, core, 1).reshape(seqs, 2, pos_dev, half),
        grad_got.reshape(seqs, 2, pos_dev, half),
        2,
    ).reshape(seqs, rows, half)
    clean_grads, own_grads, column_sums = [], [], 0.0
    for s in range(seqs):
        clean_grad, own_grad, sums = attend_back(
            counts[s], own_qkv[s], clean_kv[s], limit_list[s], attn_list[s], grad_rows[s], log_list[s],
            cos_own, sin_own, cos_tab, sin_tab, block,
        )
        clean_grads.append(clean_grad)
        own_grads.append(own_grad)
        column_sums = column_sums + sums[0]

    kv_mat = qkv_mat[:, half:]
    spread, local = [], []
    for s in range(seqs):
        spread.append(lax.dot_general(clean_grads[s], kv_mat, NT, preferred_element_type=F32).astype(BF16))
        local.append(lax.dot_general(own_grads[s], qkv_mat, NT, preferred_element_type=F32).astype(BF16))
    spread = jnp.stack([part.reshape(links.deep, 2, 2, pos_dev, width) for part in spread], 2)
    local = jnp.stack([part.reshape(2, 2, pos_dev, width) for part in local])
    spread = pick(spread, core, 3).astype(F32) + links.over_core(pick(spread, 1 - core, 3)).astype(F32)
    local = pick(local, core, 2).astype(F32) + links.over_core(pick(local, 1 - core, 2)).astype(F32)
    total = links.reduce_plane(spread.astype(BF16))
    grad_normed_one = jnp.stack([local[:, 0], local[:, 1] + total], 1).reshape(-1, width)
    unit_one, inverse_one = unit_rows(flat_inputs.astype(F32))
    grad_input = grad_hidden + unit_back(grad_normed_one * gain_one, unit_one, inverse_one)
    grad_input = grad_input.astype(BF16).reshape(layer_input.shape)

    unit_part = jnp.zeros((width, 3 * half), F32)
    kv_part = jnp.zeros((width, 2 * half), F32)
    for s in range(seqs):
        unit_part = unit_part + dot_left(own_unit[s], own_grads[s])
        kv_part = kv_part + dot_left(clean_unit[s], clean_grads[s])
    unit_part = unit_part + jnp.pad(kv_part, ((0, 0), (half, 0)))
    wide = qkv_mat.astype(F32)
    gain_part = jnp.sum(wide * unit_part, -1)
    bias_part = jnp.sum(wide * column_sums[None, :], -1)
    qkv_part = gain_one.reshape(-1, 1) * unit_part + bias_one.reshape(-1, 1) * column_sums[None, :]
    column_sums = ordered(core, column_sums.reshape(3, half), jnp.zeros((3, half), F32), 1).reshape(3 * width)
    qk_part = column_sums[: 2 * width].reshape(devices, 2, shard).transpose(0, 2, 1).reshape(width, 2)
    vec_part = jnp.concatenate(
        [jnp.stack([gain_part, bias_part, column_sums[2 * width :]], 1), qk_part], 1
    )
    vec_part = jnp.pad(vec_part, ((0, 0), (0, LANES - vec_part.shape[1])))
    qkv_part = jnp.concatenate([qkv_part, vec_part], 1).astype(BF16)
    qkv_sum = links.reduce(qkv_part.reshape(2, links.deep, 2, 2 * shard, -1)).reshape(2, shard, -1)
    qkv_mine = pick(qkv_sum, core)
    qkv_got = links.over_core(pick(qkv_sum, 1 - core))
    grad_qkv = ordered(
        core, qkv_mine[:, : 3 * half].reshape(shard, 3, half), qkv_got[:, : 3 * half].reshape(shard, 3, half), 2
    ).reshape(shard, 3 * width)
    vec_sum = (qkv_mine[:, 3 * half :] + qkv_got[:, 3 * half :]).T

    hidden_width = devices * hidden_shard
    grad_up = packed[:, :hidden_width].reshape(shard, folds, devices, shard).transpose(0, 2, 1, 3)
    grad_up = grad_up.reshape(shard, hidden_width)
    grad_down = packed[:, hidden_width : hidden_width + folds * width].reshape(shard, folds, width)
    grad_down = grad_down.transpose(1, 0, 2).reshape(hidden_shard, width)
    grad_out = packed[:, hidden_width + folds * width : -LANES]
    late = packed[:, -LANES:].T

    return (
        output, grad_input, vec_sum[0], vec_sum[1], grad_qkv, vec_sum[3:5].reshape(-1), vec_sum[2], grad_out,
        late[0], late[1], late[2], grad_up, late[4 : 4 + folds].reshape(-1), grad_down, late[3],
    )


def solution(mesh):
    every = P(("batch", "ctx"))
    matrix = P(("batch", "ctx"), None)
    acts = P("batch", None, "ctx", None)
    return jax.shard_map(
        on_device,
        mesh=mesh,
        in_specs=(
            acts, acts, P("batch"), P("batch"), every, every, matrix, every, matrix, every, every, every, matrix,
            every, matrix, every,
        ),
        out_specs=(
            acts, acts, every, every, matrix, every, every, matrix, every, every, every, matrix, every, matrix, every,
        ),
        check_vma=False,
    )
```

```python
import functools

import jax
import jax.numpy as jnp
from jax import lax
from jax.experimental import pallas as pl
from jax.experimental.pallas import tpu as pltpu
from jax.sharding import PartitionSpec as P

HEADS = 12
HEAD_DIM = 64
SCALE = 0.125
NEGATIVE = -1e30
EPSILON = 1e-05
THETA = 10000.0
LANES = 128
BF16 = jnp.bfloat16
F32 = jnp.float32
VMEM_LIMIT = 56 * 1024 * 1024
NT = (((1,), (1,)), ((), ()))


def swap_halves(tile):
    lane = lax.broadcasted_iota(jnp.int32, tile.shape, 1)
    return jnp.where(lane % 64 < 32, pltpu.roll(tile, LANES - 32, 1), pltpu.roll(tile, 32, 1))


def project_kernel(x_ref, gain_ref, bias_ref, w_ref, add_ref, cos_ref, sin_ref, out_ref, unit_ref, *, start, turned):
    x = x_ref[...].astype(F32)
    center = x - jnp.mean(x, -1, keepdims=True)
    spread = jnp.mean(center * center, -1, keepdims=True)
    unit = center * lax.rsqrt(spread + EPSILON)
    unit_ref[...] = unit.astype(BF16)
    normed = (unit * gain_ref[...] + bias_ref[...]).astype(BF16)
    cos_tab, sin_tab = cos_ref[...], sin_ref[...]
    total = jnp.dot(normed, w_ref[:, start:], preferred_element_type=F32) + add_ref[:, start:]
    for tile in range(total.shape[1] // LANES):
        part = total[:, tile * LANES : (tile + 1) * LANES]
        if tile * LANES < turned:
            part = part * cos_tab + swap_halves(part) * sin_tab
        out_ref[:, tile * LANES : (tile + 1) * LANES] = part.astype(BF16)


def project(x, gain, bias, weight, add, cos_tab, sin_tab, start, turned, block):
    rows, width = x.shape
    columns = weight.shape[1] - start
    row_map = lambda i: (i, 0)
    fixed = lambda i: (0, 0)
    return pl.pallas_call(
        functools.partial(project_kernel, start=start, turned=turned),
        grid=(rows // block,),
        in_specs=[
            pl.BlockSpec((block, width), row_map),
            pl.BlockSpec((1, width), fixed),
            pl.BlockSpec((1, width), fixed),
            pl.BlockSpec(weight.shape, fixed),
            pl.BlockSpec((1, weight.shape[1]), fixed),
            pl.BlockSpec((block, LANES), row_map),
            pl.BlockSpec((block, LANES), row_map),
        ],
        out_specs=[pl.BlockSpec((block, columns), row_map), pl.BlockSpec((block, width), row_map)],
        out_shape=[jax.ShapeDtypeStruct((rows, columns), BF16), jax.ShapeDtypeStruct((rows, width), BF16)],
        compiler_params=pltpu.CompilerParams(vmem_limit_bytes=VMEM_LIMIT),
        cost_estimate=pl.CostEstimate(
            flops=2 * rows * width * columns,
            bytes_accessed=2 * (rows * (2 * width + columns) + width * columns),
            transcendentals=rows,
        ),
        name="project",
    )(x, gain, bias, weight, add, cos_tab, sin_tab)


def head_parts(rows, factor):
    rows = rows.astype(F32) * factor
    lane = lax.broadcasted_iota(jnp.int32, rows.shape, 1)
    first = lane < HEAD_DIM
    return (jnp.where(first, rows, 0.0).astype(BF16), jnp.where(first, 0.0, rows).astype(BF16))


def flipped(tile):
    return tile.astype(F32).T.astype(BF16)


def nt_dot(a, b):
    return lax.dot_general(a, b, NT, preferred_element_type=F32)


def own_mask(limit_ref, noisy_rows, rows):
    at = lax.broadcasted_iota(jnp.int32, (noisy_rows, rows), 0)
    return (at >= limit_ref[1:2, :]) & (at < limit_ref[2:3, :])


def attend_kernel(count_ref, q_ref, kn_ref, vn_ref, kc_ref, vc_ref, limit_ref, o_ref, log_ref, *, block):
    rows = q_ref.shape[0]
    queries = head_parts(q_ref[...], SCALE)
    limit = limit_ref[0:1, :]

    def fold(state, parts):
        values = [flipped(part_values) for _, part_values, _ in parts]
        out = []
        for h in range(2):
            best, total, acc = state[h]
            heads = slice(h * HEAD_DIM, (h + 1) * HEAD_DIM)
            scores = [jnp.where(mask, nt_dot(keys, queries[h]), NEGATIVE) for keys, _, mask in parts]
            tops = [jnp.max(part, 0, keepdims=True) for part in scores]
            new_best = functools.reduce(jnp.maximum, tops, best)
            factor = jnp.exp(best - new_best)
            total = total * factor
            acc = acc * factor
            for part, part_values in zip(scores, values):
                weights = jnp.exp(part - new_best)
                total = total + jnp.sum(weights, 0, keepdims=True)
                acc = acc + jnp.dot(part_values[heads], weights.astype(BF16), preferred_element_type=F32)
            out.append((new_best, total, acc))
        return tuple(out)

    def clean_parts(index):
        parts = []
        for offset in range(0, block, piece):
            first = index * block + offset
            at = lax.broadcasted_iota(jnp.int32, (piece, rows), 0) + first
            if not isinstance(first, int):
                first = pl.multiple_of(first, piece)
            parts.append((kc_ref[pl.ds(first, piece), :], vc_ref[pl.ds(first, piece), :], at < limit))
        return parts

    piece = key_block(block, 512)
    own_part = (kn_ref[...], vn_ref[...], own_mask(limit_ref, kn_ref.shape[0], rows))
    start = (
        jnp.full((1, rows), NEGATIVE, F32),
        jnp.zeros((1, rows), F32),
        jnp.zeros((HEAD_DIM, rows), F32),
    )
    if block == kc_ref.shape[0]:
        state = fold((start, start), clean_parts(0) + [own_part])
    else:
        state = lax.fori_loop(0, count_ref[0], lambda i, state: fold(state, clean_parts(i)), (start, start))
        state = fold(state, [own_part])
    o_ref[...] = jnp.concatenate([acc / total for _, total, acc in state], 0).T.astype(BF16)
    for h in range(2):
        log_ref[0, h : h + 1, :] = state[h][0] + jnp.log(state[h][1])


def attend(count, own, clean, limits, block):
    rows = own.shape[0]
    length = clean.shape[0]
    pairs = own.shape[1] // (3 * LANES)
    spec = pltpu.PrefetchScalarGridSpec(
        num_scalar_prefetch=1,
        grid=(pairs,),
        in_specs=[
            pl.BlockSpec((rows, LANES), lambda p, c: (0, p)),
            pl.BlockSpec((rows // 2, LANES), lambda p, c: (0, pairs + p)),
            pl.BlockSpec((rows // 2, LANES), lambda p, c: (0, 2 * pairs + p)),
            pl.BlockSpec((length, LANES), lambda p, c: (0, p)),
            pl.BlockSpec((length, LANES), lambda p, c: (0, pairs + p)),
            pl.BlockSpec((8, rows), lambda p, c: (0, 0)),
        ],
        out_specs=[
            pl.BlockSpec((rows, LANES), lambda p, c: (0, p)),
            pl.BlockSpec((1, 8, rows), lambda p, c: (p, 0, 0)),
        ],
    )
    return pl.pallas_call(
        functools.partial(attend_kernel, block=block),
        grid_spec=spec,
        out_shape=[
            jax.ShapeDtypeStruct((rows, pairs * LANES), BF16),
            jax.ShapeDtypeStruct((pairs, 8, rows), F32),
        ],
        compiler_params=pltpu.CompilerParams(vmem_limit_bytes=VMEM_LIMIT),
        cost_estimate=pl.CostEstimate(
            flops=pairs * rows * (length + rows // 2) * 2048,
            bytes_accessed=2 * pairs * LANES * (2 * length + 3 * rows),
            transcendentals=2 * pairs * rows * length,
        ),
        name="attend",
    )(count, own, own, own, clean, clean, limits)


def attend_back_kernel(
    count_ref, q_ref, kn_ref, vn_ref, kc_ref, vc_ref, limit_ref, o_ref, do_ref, log_ref,
    cos_own_ref, sin_own_ref, cos_ref, sin_ref, dkv_ref, down_ref, sum_ref, *, block
):
    rows = q_ref.shape[0]
    noisy = kn_ref.shape[0]
    width = dkv_ref.shape[1] // 2
    length = kc_ref.shape[0]
    here = pl.multiple_of(pl.program_id(0) * LANES, LANES)
    queries = head_parts(q_ref[...], SCALE)
    grads = head_parts(do_ref[...], 1.0)
    limit = limit_ref[0:1, :]
    product = do_ref[...].astype(F32) * o_ref[...].astype(F32)
    lane = lax.broadcasted_iota(jnp.int32, (8, LANES), 1)
    deltas = []
    for h in range(2):
        ones = jnp.where((lane < HEAD_DIM) == (h == 0), 1.0, 0.0)
        deltas.append(
            lax.dot_general(ones, product, NT, precision=lax.Precision.HIGHEST, preferred_element_type=F32)[0:1]
        )

    def fold(dq, keys, values, mask):
        keys_flipped = flipped(keys)
        dk = dv = None
        out = []
        for h in range(2):
            scores = nt_dot(keys, queries[h])
            probs = jnp.where(mask, jnp.exp(scores - log_ref[0, h : h + 1, :]), 0.0)
            inner = nt_dot(values, grads[h])
            slopes = (probs * (inner - deltas[h])).astype(BF16)
            dv_new = jnp.dot(probs.astype(BF16), grads[h], preferred_element_type=F32)
            dk_new = jnp.dot(slopes, queries[h], preferred_element_type=F32)
            dv = dv_new if dv is None else dv + dv_new
            dk = dk_new if dk is None else dk + dk_new
            out.append(
                dq[h]
                + jnp.dot(keys_flipped[h * HEAD_DIM : (h + 1) * HEAD_DIM], slopes, preferred_element_type=F32)
            )
        return tuple(out), dk, dv

    def unturn(grad, cos_tab, sin_tab):
        return grad * cos_tab - swap_halves(grad) * sin_tab

    def step(index, carry):
        dq, sum_k, sum_v = carry
        first = pl.multiple_of(index * block, block)
        where = pl.ds(first, block)
        at = lax.broadcasted_iota(jnp.int32, (block, rows), 0) + index * block
        dq, dk, dv = fold(dq, kc_ref[where, :], vc_ref[where, :], at < limit)
        dk = unturn(dk, cos_ref[where, :], sin_ref[where, :])
        dkv_ref[where, pl.ds(here, LANES)] = dk.astype(BF16)
        dkv_ref[where, pl.ds(width + here, LANES)] = dv.astype(BF16)
        return dq, sum_k + jnp.sum(dk, 0, keepdims=True), sum_v + jnp.sum(dv, 0, keepdims=True)

    zero_q = jnp.zeros((HEAD_DIM, rows), F32)
    zero_sum = jnp.zeros((1, LANES), F32)
    dq, sum_k, sum_v = lax.fori_loop(0, count_ref[0], step, ((zero_q, zero_q), zero_sum, zero_sum))

    def blank(index, carry):
        where = pl.ds(pl.multiple_of(index * block, block), block)
        dkv_ref[where, pl.ds(here, LANES)] = jnp.zeros((block, LANES), BF16)
        dkv_ref[where, pl.ds(width + here, LANES)] = jnp.zeros((block, LANES), BF16)
        return carry

    lax.fori_loop(count_ref[0], length // block, blank, 0)
    dq, dk, dv = fold(dq, kn_ref[...], vn_ref[...], own_mask(limit_ref, noisy, rows))
    dk = unturn(dk, cos_own_ref[:noisy, :], sin_own_ref[:noisy, :])
    dq = unturn(jnp.concatenate(dq, 0).T * SCALE, cos_own_ref[...], sin_own_ref[...])
    zeros = jnp.zeros((rows - noisy, LANES), BF16)
    for part, grad in enumerate((dq, dk, dv)):
        down_ref[: grad.shape[0], pl.ds(part * width + here, LANES)] = grad.astype(BF16)
        if part > 0:
            down_ref[noisy:, pl.ds(part * width + here, LANES)] = zeros
    sums = (
        jnp.sum(dq, 0, keepdims=True),
        sum_k + jnp.sum(dk, 0, keepdims=True),
        sum_v + jnp.sum(dv, 0, keepdims=True),
    )
    for part in range(3):
        sum_ref[:, pl.ds(part * width + here, LANES)] = jnp.broadcast_to(sums[part], (8, LANES))


def attend_back(count, own, clean, limits, attn, grad, log_total, cos_own, sin_own, cos_tab, sin_tab, block):
    rows = own.shape[0]
    length, both = clean.shape
    pairs = own.shape[1] // (3 * LANES)
    spec = pltpu.PrefetchScalarGridSpec(
        num_scalar_prefetch=1,
        grid=(pairs,),
        in_specs=[
            pl.BlockSpec((rows, LANES), lambda p, c: (0, p)),
            pl.BlockSpec((rows // 2, LANES), lambda p, c: (0, pairs + p)),
            pl.BlockSpec((rows // 2, LANES), lambda p, c: (0, 2 * pairs + p)),
            pl.BlockSpec((length, LANES), lambda p, c: (0, p)),
            pl.BlockSpec((length, LANES), lambda p, c: (0, pairs + p)),
            pl.BlockSpec((8, rows), lambda p, c: (0, 0)),
            pl.BlockSpec((rows, LANES), lambda p, c: (0, p)),
            pl.BlockSpec((rows, LANES), lambda p, c: (0, p)),
            pl.BlockSpec((1, 8, rows), lambda p, c: (p, 0, 0)),
            pl.BlockSpec((rows, LANES), lambda p, c: (0, 0)),
            pl.BlockSpec((rows, LANES), lambda p, c: (0, 0)),
            pl.BlockSpec((length, LANES), lambda p, c: (0, 0)),
            pl.BlockSpec((length, LANES), lambda p, c: (0, 0)),
        ],
        out_specs=[
            pl.BlockSpec((length, both), lambda p, c: (0, 0)),
            pl.BlockSpec((rows, own.shape[1]), lambda p, c: (0, 0)),
            pl.BlockSpec((8, own.shape[1]), lambda p, c: (0, 0)),
        ],
    )
    return pl.pallas_call(
        functools.partial(attend_back_kernel, block=block),
        grid_spec=spec,
        out_shape=[
            jax.ShapeDtypeStruct((length, both), BF16),
            jax.ShapeDtypeStruct(own.shape, BF16),
            jax.ShapeDtypeStruct((8, own.shape[1]), F32),
        ],
        compiler_params=pltpu.CompilerParams(vmem_limit_bytes=VMEM_LIMIT),
        cost_estimate=pl.CostEstimate(
            flops=pairs * rows * (length + rows // 2) * 5120,
            bytes_accessed=2 * pairs * LANES * (5 * length + 8 * rows),
            transcendentals=2 * pairs * rows * length,
        ),
        name="attend_back",
    )(count, own, own, own, clean, clean, limits, attn, grad, log_total, cos_own, sin_own, cos_tab, sin_tab)


def feed_forward_kernel(
    attn_ref, x_ref, top_ref, up_ref, down_ref, out_ref, vec_ref,
    block_out_ref, hidden_grad_ref, attn_grad_ref, weights_ref,
    hidden, unit, inverse, normed, normed_flipped, lowered, grad_normed,
    up_grads, down_grads, out_grads, vec_grads, sums, up_sems, down_sems, last_sems
):
    chunk = pl.program_id(0)
    chunks = pl.num_programs(0)
    width = x_ref.shape[1]

    @pl.when(chunk == 0)
    def _():
        value = (
            x_ref[...].astype(F32)
            + jnp.dot(attn_ref[...], out_ref[...], preferred_element_type=F32)
            + vec_ref[0:1, :]
        )
        hidden[...] = value
        center = value - jnp.mean(value, -1, keepdims=True)
        scale = lax.rsqrt(jnp.mean(center * center, -1, keepdims=True) + EPSILON)
        inverse[...] = scale
        unit[...] = center * scale
        scaled = unit[...] * vec_ref[1:2, :] + vec_ref[2:3, :]
        normed[...] = scaled.astype(BF16)
        normed_flipped[...] = scaled.T.astype(BF16)
        lowered[...] = jnp.zeros_like(lowered)
        grad_normed[...] = jnp.zeros_like(grad_normed)
        sums[...] = jnp.zeros_like(sums)

    upper = jnp.dot(normed[...], up_ref[...], preferred_element_type=F32) + vec_ref[pl.ds(4 + chunk, 1), :]
    grad_activ = nt_dot(top_ref[...], down_ref[...])
    inner = jnp.tanh(0.7978845608028654 * (upper + 0.044715 * upper * upper * upper))
    activ = 0.5 * upper * (1.0 + inner)
    slope = 0.5 * (1.0 + inner) + 0.5 * upper * (1.0 - inner * inner) * 0.7978845608028654 * (
        1.0 + 0.134145 * upper * upper
    )
    grad_upper = grad_activ * slope
    grad_low = grad_upper.astype(BF16)
    sums[pl.ds(4 + chunk, 1), :] = jnp.sum(grad_upper, 0, keepdims=True)
    lowered[...] += jnp.dot(activ.astype(BF16), down_ref[...], preferred_element_type=F32)
    grad_normed[...] += nt_dot(grad_low, up_ref[...])
    up_grads[chunk] = jnp.dot(normed_flipped[...], grad_low, preferred_element_type=F32).astype(BF16)
    down_grads[chunk] = jnp.dot(activ.T.astype(BF16), top_ref[...], preferred_element_type=F32).astype(BF16)

    def copy_up(index):
        columns = pl.ds(pl.multiple_of(index * width, width), width)
        return pltpu.make_async_copy(up_grads.at[index], weights_ref.at[:, columns], up_sems.at[index])

    def copy_down(index):
        columns = pl.ds(pl.multiple_of((chunks + index) * width, width), width)
        return pltpu.make_async_copy(down_grads.at[index], weights_ref.at[:, columns], down_sems.at[index])

    copy_up(chunk).start()
    copy_down(chunk).start()

    @pl.when(chunk == chunks - 1)
    def _():
        top = top_ref[...].astype(F32)
        block_out_ref[...] = (hidden[...] + lowered[...] + vec_ref[3:4, :]).astype(BF16)
        grad = grad_normed[...]
        rows_unit = unit[...]
        sums[1:2, :] = jnp.sum(grad * rows_unit, 0, keepdims=True)
        sums[2:3, :] = jnp.sum(grad, 0, keepdims=True)
        sums[3:4, :] = jnp.sum(top, 0, keepdims=True)
        grad = grad * vec_ref[1:2, :]
        grad = inverse[...] * (
            grad - jnp.mean(grad, -1, keepdims=True) - rows_unit * jnp.mean(grad * rows_unit, -1, keepdims=True)
        )
        grad = top + grad
        hidden_grad_ref[...] = grad
        sums[0:1, :] = jnp.sum(grad, 0, keepdims=True)
        low = grad.astype(BF16)
        attn_grad_ref[...] = nt_dot(low, out_ref[...]).astype(BF16)
        out_grads[...] = jnp.dot(
            attn_ref[...].astype(F32).T.astype(BF16), low, preferred_element_type=F32
        ).astype(BF16)
        vec_grads[...] = sums[...].T.astype(BF16)
        first = 2 * chunks * width
        copies = [
            pltpu.make_async_copy(out_grads, weights_ref.at[:, pl.ds(first, width)], last_sems.at[0]),
            pltpu.make_async_copy(vec_grads, weights_ref.at[:, pl.ds(first + width, LANES)], last_sems.at[1]),
        ]
        for copy in copies:
            copy.start()
        for index in range(up_grads.shape[0]):
            copy_up(index).wait()
            copy_down(index).wait()
        for copy in copies:
            copy.wait()


def feed_forward(attn, x, top, weights, vectors, chunks):
    rows, width = x.shape
    fixed = lambda b: (0, 0)
    whole = pl.BlockSpec((rows, width), fixed)
    return pl.pallas_call(
        feed_forward_kernel,
        grid=(chunks,),
        in_specs=[
            whole,
            whole,
            whole,
            pl.BlockSpec((width, width), lambda b: (0, b)),
            pl.BlockSpec((width, width), lambda b: (0, chunks + b)),
            pl.BlockSpec((width, width), lambda b: (0, 2 * chunks)),
            pl.BlockSpec(vectors.shape, fixed),
        ],
        out_specs=[whole, whole, whole, pl.BlockSpec(memory_space=pl.ANY)],
        out_shape=[
            jax.ShapeDtypeStruct((rows, width), BF16),
            jax.ShapeDtypeStruct((rows, width), F32),
            jax.ShapeDtypeStruct((rows, width), BF16),
            jax.ShapeDtypeStruct(weights.shape, BF16),
        ],
        scratch_shapes=[
            pltpu.VMEM((rows, width), F32),
            pltpu.VMEM((rows, width), F32),
            pltpu.VMEM((rows, 1), F32),
            pltpu.VMEM((rows, width), BF16),
            pltpu.VMEM((width, rows), BF16),
            pltpu.VMEM((rows, width), F32),
            pltpu.VMEM((rows, width), F32),
            pltpu.VMEM((chunks, width, width), BF16),
            pltpu.VMEM((chunks, width, width), BF16),
            pltpu.VMEM((width, width), BF16),
            pltpu.VMEM((width, LANES), BF16),
            pltpu.VMEM((LANES, width), F32),
            pltpu.SemaphoreType.DMA((chunks,)),
            pltpu.SemaphoreType.DMA((chunks,)),
            pltpu.SemaphoreType.DMA((2,)),
        ],
        compiler_params=pltpu.CompilerParams(vmem_limit_bytes=VMEM_LIMIT),
        cost_estimate=pl.CostEstimate(
            flops=2 * rows * width * width * (6 * chunks + 3),
            bytes_accessed=4 * width * weights.shape[1] + 12 * rows * width,
            transcendentals=rows * width * chunks,
        ),
        name="feed_forward",
    )(attn, x, top, weights, weights, weights, vectors)


def after(value, *others):
    return lax.optimization_barrier((value,) + others)[0]


def pick(array, index, axis=0):
    return lax.dynamic_index_in_dim(array, index, axis, keepdims=False)


def ordered(flag, own, other, axis):
    return jnp.stack([jnp.where(flag == 0, own, other), jnp.where(flag == 0, other, own)], axis)


class Links:
    def __init__(self):
        self.count = lax.axis_size("ctx")
        self.deep = self.count // 4
        at = lax.axis_index("ctx")
        self.x = lax.axis_index("batch")
        self.core = at % 2
        self.y = (at // 2) % 2
        self.z = at // 4
        self.chip = at // 2

    def over_core(self, array):
        return lax.ppermute(array, "ctx", [(i, i ^ 1) for i in range(self.count)])

    def over_y(self, array):
        return lax.ppermute(array, "ctx", [(i, i ^ 2) for i in range(self.count)])

    def over_x(self, array):
        return lax.ppermute(array, "batch", [(0, 1), (1, 0)])

    def along_z(self, array, hop):
        count = self.count
        return lax.ppermute(array, "ctx", [(i, (i + 4 * hop) % count) for i in range(count)])

    def around_z(self, piece):
        return [self.along_z(piece, hop) for hop in range(1, self.deep)]

    def column(self, piece, others):
        deep = self.deep
        whole = jnp.broadcast_to(piece[None], (deep,) + piece.shape)
        for hop, other in enumerate(others, 1):
            whole = lax.dynamic_update_index_in_dim(whole, other, (self.z - hop) % deep, 0)
        return whole

    def swap_z(self, parts):
        return [self.along_z(pick(parts, (self.z + hop) % self.deep), hop) for hop in range(1, self.deep)]

    def sum_z(self, parts, others):
        total = pick(parts, self.z).astype(F32)
        for other in others:
            total = total + other.astype(F32)
        return total


def unit_rows(values):
    center = values - jnp.mean(values, -1, keepdims=True)
    spread = jnp.mean(center * center, -1, keepdims=True)
    inverse = lax.rsqrt(spread + EPSILON)
    return center * inverse, inverse


def unit_back(grad, unit, inverse):
    return inverse * (
        grad - jnp.mean(grad, -1, keepdims=True) - unit * jnp.mean(grad * unit, -1, keepdims=True)
    )


def rotary_tables(positions):
    half_dim = HEAD_DIM // 2
    inverse = 1.0 / THETA ** (jnp.arange(half_dim, dtype=F32) / half_dim)
    angles = positions.astype(F32)[:, None] * jnp.tile(inverse, LANES // half_dim)[None, :]
    sign = jnp.where(jnp.arange(LANES) % HEAD_DIM < half_dim, -1.0, 1.0)
    return jnp.cos(angles), jnp.sin(angles) * sign[None, :]


def key_block(length, limit):
    sizes = [size for size in range(16, limit + 1, 16) if length % size == 0]
    return sizes[-1] if sizes else length


def row_block(rows):
    for block in (512, 384, 256, 128, 64, 32, 16):
        if rows % block == 0:
            return block
    return rows


def dot(a, b):
    return jnp.dot(a, b, preferred_element_type=F32)


def dot_left(a, b):
    return lax.dot_general(a, b, (((0,), (0,)), ((), ())), preferred_element_type=F32)


def on_device(
    layer_input, cotangent, prefix, block_size, ln1_gain, ln1_bias, qkv_weight, qkv_bias, out_weight, out_bias,
    ln2_gain, ln2_bias, up_weight, up_bias, down_weight, down_bias,
):
    links = Links()
    core = links.core
    seqs, _, pos_dev, width = layer_input.shape
    devices = 2 * links.count
    length = links.count * pos_dev
    half = width // 2
    rows = 4 * pos_dev
    shard = ln1_gain.shape[0]
    hidden_shard = up_bias.shape[0]

    split = qkv_weight.reshape(shard, 3, 2, half)
    vec_one = jnp.concatenate([ln1_gain, ln1_bias, qkv_bias])
    vec_piece = ordered(core, vec_one, links.over_core(vec_one), 0)
    qkv_piece = ordered(core, pick(split, core, 2), links.over_core(pick(split, 1 - core, 2)), 0)
    qkv_piece = qkv_piece.reshape(2 * shard, 3 * half)
    qkv_others = links.around_z(qkv_piece)
    qkv_column = links.column(qkv_piece, qkv_others)
    qkv_got = links.over_y(qkv_column)
    clean_piece = after(layer_input[0, 1], *qkv_others)
    clean_others = links.around_z(clean_piece)
    vec_piece = after(vec_piece, *qkv_others)
    vec_others = links.around_z(vec_piece)
    inputs_got = links.over_core(after(layer_input, *qkv_others))
    columns = [links.column(clean_piece, clean_others)]
    vec_column = links.column(vec_piece, vec_others)
    qkv_plane = ordered(links.y, qkv_column, qkv_got, 1)
    gate = (qkv_got,) + tuple(clean_others) + tuple(vec_others)
    weights_gate = gate
    vec_got = links.over_y(after(vec_column, *gate))
    vec_plane = ordered(links.y, vec_column, vec_got, 1)
    qkv_far = [links.over_x(qkv_plane[: links.deep // 2])]
    clean_inputs = []
    for s in range(seqs):
        row_got = links.over_y(after(columns[s], *gate))
        gate = (row_got,)
        if s == 0:
            gate = gate + (qkv_far[0], vec_got)
        if s + 1 < seqs:
            clean_piece = after(layer_input[s + 1, 1], qkv_got, *clean_others)
            clean_others = links.around_z(clean_piece)
            columns.append(links.column(clean_piece, clean_others))
            gate = gate + tuple(clean_others)
        if s == 0:
            qkv_far.append(links.over_x(after(qkv_plane[links.deep // 2 :], *gate)))
            vec_far = links.over_x(after(vec_plane, *gate))
        lane_rows = ordered(links.y, columns[s], row_got, 1)
        clean_inputs.append(ordered(core, lane_rows, links.over_core(lane_rows), 2).reshape(length, width))
    qkv_far = jnp.concatenate(qkv_far)
    qkv_mat = ordered(links.x, qkv_plane, qkv_far, 0).reshape(width, 3 * half)
    vec_one = ordered(links.x, vec_plane, vec_far, 0).reshape(devices, -1).astype(F32)
    gain_one = vec_one[:, :shard].reshape(1, width)
    bias_one = vec_one[:, shard : 2 * shard].reshape(1, width)
    qkv_add = pick(vec_one[:, 2 * shard :].reshape(3, 2, half), core, 1).reshape(1, 3 * half)

    folds = hidden_shard // shard
    up_piece = up_weight.reshape(shard, devices, folds, shard).transpose(0, 2, 1, 3).reshape(shard, -1)
    down_piece = down_weight.reshape(folds, shard, width).transpose(1, 0, 2).reshape(shard, -1)
    vec_piece = jnp.stack(
        [out_bias, ln2_gain, ln2_bias, down_bias] + [up_bias[i * shard : (i + 1) * shard] for i in range(folds)], 1
    )
    vec_piece = jnp.pad(vec_piece, ((0, 0), (0, LANES - vec_piece.shape[1])))
    packed = after(jnp.concatenate([up_piece, down_piece, out_weight, vec_piece], 1), *weights_gate)
    weights = lax.all_gather(packed, ("batch", "ctx"), axis=0, tiled=True)
    vectors = weights[:, -LANES:].T[: 4 + folds].astype(F32)

    inputs_pair = ordered(core, layer_input, inputs_got, 2).reshape(seqs, rows, width)

    cos_tab, sin_tab = rotary_tables(jnp.arange(length, dtype=jnp.int32))
    first_pos = links.chip * 2 * pos_dev
    cos_own = jnp.tile(lax.dynamic_slice_in_dim(cos_tab, first_pos, 2 * pos_dev, 0), (2, 1))
    sin_own = jnp.tile(lax.dynamic_slice_in_dim(sin_tab, first_pos, 2 * pos_dev, 0), (2, 1))
    block = key_block(length, 1536)
    at = jnp.arange(2 * pos_dev, dtype=jnp.int32)
    position = first_pos + at
    own_qkv, own_unit = project(
        inputs_pair.reshape(seqs * rows, width), gain_one, bias_one, qkv_mat, qkv_add,
        jnp.tile(cos_own, (seqs, 1)), jnp.tile(sin_own, (seqs, 1)), 0, width, row_block(rows),
    )
    own_qkv = own_qkv.reshape(seqs, rows, 3 * half)
    clean_kv, clean_unit, limit_list, counts, attn_list, log_list = ([] for _ in range(6))
    for s in range(seqs):
        near = (position // block_size[s]) * block_size[s]
        ends = near + block_size[s]
        noisy_limit = jnp.maximum(near, prefix[s])
        clean_limit = jnp.where(position < prefix[s], prefix[s], ends)
        limit = jnp.concatenate([noisy_limit, clean_limit])
        none = jnp.zeros_like(at)
        limits = jnp.stack(
            [limit, jnp.concatenate([near - first_pos, none]), jnp.concatenate([ends - first_pos, none])]
            + [jnp.zeros_like(limit)] * 5
        )
        count = jnp.minimum((jnp.max(limit) + block - 1) // block, length // block).reshape(1)
        clean, all_unit = project(
            clean_inputs[s], gain_one, bias_one, qkv_mat, qkv_add, cos_tab, sin_tab, half, half, row_block(length)
        )
        attn, log_total = attend(count, own_qkv[s], clean, limits, block)
        for kept, value in zip(
            (clean_kv, clean_unit, limit_list, counts, attn_list, log_list),
            (clean, all_unit, limits, count, attn, log_total),
        ):
            kept.append(value)

    attn_rows = jnp.stack(attn_list).reshape(seqs, 2, 2, pos_dev, half)
    attn_got = links.over_core(pick(attn_rows, 1 - core, 2))
    attn_low = ordered(core, pick(attn_rows, core, 2), attn_got, 3).reshape(-1, width)
    flat_inputs = layer_input.reshape(-1, width)
    output, grad_hidden, grad_attn, weight_grads = feed_forward(
        attn_low, flat_inputs, cotangent.reshape(-1, width), weights, vectors, folds
    )
    output = output.reshape(layer_input.shape)
    packed = lax.psum_scatter(weight_grads, ("batch", "ctx"), scatter_dimension=0, tiled=True).astype(F32)

    grad_split = grad_attn.reshape(-1, 2, half)
    grad_got = links.over_core(pick(grad_split, 1 - core, 1))
    grad_rows = ordered(
        core,
        pick(grad_split, core, 1).reshape(seqs, 2, pos_dev, half),
        grad_got.reshape(seqs, 2, pos_dev, half),
        2,
    ).reshape(seqs, rows, half)
    kv_mat = qkv_mat[:, half:]
    own_unit = own_unit.reshape(seqs, rows, width)
    unit_part = jnp.zeros((width, 3 * half), F32)
    kv_part = jnp.zeros((width, 2 * half), F32)
    column_sums = 0.0
    local_rows, mine_rows, sent = [], [], ()
    for s in range(seqs):
        clean_grad, own_grad, sums = attend_back(
            counts[s], own_qkv[s], clean_kv[s], limit_list[s], attn_list[s], after(grad_rows[s], *sent[:1]),
            log_list[s], cos_own, sin_own, cos_tab, sin_tab, block,
        )
        clean_grad = after(clean_grad, *sent[1:])
        spread = lax.dot_general(clean_grad, kv_mat, NT, preferred_element_type=F32).astype(BF16)
        local = lax.dot_general(own_grad, qkv_mat, NT, preferred_element_type=F32).astype(BF16)
        spread = spread.reshape(2 * links.deep, 2, pos_dev, width)
        local = local.reshape(2, 2, pos_dev, width)
        theirs = jnp.concatenate([pick(spread, 1 - core, 1), pick(local, 1 - core, 1)])
        got = links.over_core(theirs)
        own_grad = after(own_grad, theirs)
        clean_grad = after(clean_grad, theirs)
        unit_part = unit_part + dot_left(own_unit[s], own_grad)
        kv_part = kv_part + dot_left(clean_unit[s], clean_grad)
        column_sums = column_sums + sums[0]
        mine = pick(spread, core, 1).astype(F32) + got[: 2 * links.deep].astype(F32)
        mine = mine.astype(BF16).reshape(links.deep, 2, pos_dev, width)
        local_rows.append(pick(local, core, 1).astype(F32) + got[2 * links.deep :].astype(F32))
        theirs = pick(mine, 1 - links.y, 1)
        got = links.over_y(theirs)
        mine_rows.append((pick(mine, links.y, 1).astype(F32) + got.astype(F32)).astype(BF16))
        sent = (theirs, got)
    mine = jnp.stack(mine_rows, 1)
    others = links.swap_z(mine)
    total = links.sum_z(mine, others)
    own_rows = [jnp.stack([local_rows[s][0], local_rows[s][1] + total[s]]) for s in range(seqs)]
    gate = sent + tuple(others)

    grad_normed_one = jnp.stack(own_rows).reshape(-1, width)
    unit_one, inverse_one = unit_rows(flat_inputs.astype(F32))
    grad_input = grad_hidden + unit_back(grad_normed_one * gain_one, unit_one, inverse_one)
    grad_input = grad_input.astype(BF16).reshape(layer_input.shape)

    unit_part = lax.optimization_barrier(unit_part + jnp.pad(kv_part, ((0, 0), (half, 0))))
    wide = qkv_mat.astype(F32)
    gain_part = jnp.sum(wide * unit_part, -1)
    bias_part = jnp.sum(wide * column_sums[None, :], -1)
    qkv_part = gain_one.reshape(-1, 1) * unit_part + bias_one.reshape(-1, 1) * column_sums[None, :]
    column_sums = ordered(core, column_sums.reshape(3, half), jnp.zeros((3, half), F32), 1).reshape(3 * width)
    qk_part = column_sums[: 2 * width].reshape(devices, 2, shard).transpose(0, 2, 1).reshape(width, 2)
    vec_part = jnp.concatenate(
        [jnp.stack([gain_part, bias_part, column_sums[2 * width :]], 1), qk_part], 1
    )
    vec_part = jnp.pad(vec_part, ((0, 0), (0, LANES - vec_part.shape[1])))
    qkv_part = jnp.concatenate([qkv_part, vec_part], 1).astype(BF16)
    qkv_part = qkv_part.reshape(2, links.deep, 2, 2 * shard, -1)
    far = links.over_x(pick(qkv_part, 1 - links.x))
    qkv_part = (pick(qkv_part, links.x).astype(F32) + far.astype(F32)).astype(BF16)
    far = links.over_y(after(pick(qkv_part, 1 - links.y, 1), *gate[1:2]))
    qkv_part = (pick(qkv_part, links.y, 1).astype(F32) + far.astype(F32)).astype(BF16)
    qkv_part = after(qkv_part, *gate[2:])
    qkv_sum = links.sum_z(qkv_part, links.swap_z(qkv_part)).reshape(2, shard, -1)
    qkv_mine = pick(qkv_sum, core)
    qkv_got = links.over_core(pick(qkv_sum, 1 - core))
    grad_qkv = ordered(
        core, qkv_mine[:, : 3 * half].reshape(shard, 3, half), qkv_got[:, : 3 * half].reshape(shard, 3, half), 2
    ).reshape(shard, 3 * width)
    vec_sum = (qkv_mine[:, 3 * half :] + qkv_got[:, 3 * half :]).T

    hidden_width = devices * hidden_shard
    grad_up = packed[:, :hidden_width].reshape(shard, folds, devices, shard).transpose(0, 2, 1, 3)
    grad_up = grad_up.reshape(shard, hidden_width)
    grad_down = packed[:, hidden_width : hidden_width + folds * width].reshape(shard, folds, width)
    grad_down = grad_down.transpose(1, 0, 2).reshape(hidden_shard, width)
    grad_out = packed[:, hidden_width + folds * width : -LANES]
    late = packed[:, -LANES:].T

    return (
        output, grad_input, vec_sum[0], vec_sum[1], grad_qkv, vec_sum[3:5].reshape(-1), vec_sum[2], grad_out,
        late[0], late[1], late[2], grad_up, late[4 : 4 + folds].reshape(-1), grad_down, late[3],
    )


def solution(mesh):
    every = P(("batch", "ctx"))
    matrix = P(("batch", "ctx"), None)
    acts = P("batch", None, "ctx", None)
    return jax.shard_map(
        on_device,
        mesh=mesh,
        in_specs=(
            acts, acts, P("batch"), P("batch"), every, every, matrix, every, matrix, every, every, every, matrix,
            every, matrix, every,
        ),
        out_specs=(
            acts, acts, every, every, matrix, every, every, matrix, every, every, every, matrix, every, matrix, every,
        ),
        check_vma=False,
    )
```

```python
import functools

import jax
import jax.numpy as jnp
from jax import lax
from jax.experimental import pallas as pl
from jax.experimental.pallas import tpu as pltpu
from jax.sharding import PartitionSpec as P

HEADS = 12
HEAD_DIM = 64
SCALE = 0.125
NEGATIVE = -1e30
EPSILON = 1e-05
THETA = 10000.0
LANES = 128
BF16 = jnp.bfloat16
F32 = jnp.float32
VMEM_LIMIT = 56 * 1024 * 1024
NT = (((1,), (1,)), ((), ()))
LIGHT = pl.CostEstimate(flops=1, bytes_accessed=1, transcendentals=0)


def swap_halves(tile):
    lane = lax.broadcasted_iota(jnp.int32, tile.shape, 1)
    return jnp.where(lane % 64 < 32, pltpu.roll(tile, LANES - 32, 1), pltpu.roll(tile, 32, 1))


def project_kernel(x_ref, gain_ref, bias_ref, w_ref, add_ref, cos_ref, sin_ref, out_ref, unit_ref, *, start, turned):
    x = x_ref[...].astype(F32)
    center = x - jnp.mean(x, -1, keepdims=True)
    spread = jnp.mean(center * center, -1, keepdims=True)
    unit = center * lax.rsqrt(spread + EPSILON)
    unit_ref[...] = unit.astype(BF16)
    normed = (unit * gain_ref[...] + bias_ref[...]).astype(BF16)
    cos_tab, sin_tab = cos_ref[...], sin_ref[...]
    total = jnp.dot(normed, w_ref[:, start:], preferred_element_type=F32) + add_ref[:, start:]
    for tile in range(total.shape[1] // LANES):
        part = total[:, tile * LANES : (tile + 1) * LANES]
        if tile * LANES < turned:
            part = part * cos_tab + swap_halves(part) * sin_tab
        out_ref[:, tile * LANES : (tile + 1) * LANES] = part.astype(BF16)


def project(x, gain, bias, weight, add, cos_tab, sin_tab, start, turned, block):
    rows, width = x.shape
    columns = weight.shape[1] - start
    row_map = lambda i: (i, 0)
    fixed = lambda i: (0, 0)
    return pl.pallas_call(
        functools.partial(project_kernel, start=start, turned=turned),
        grid=(rows // block,),
        in_specs=[
            pl.BlockSpec((block, width), row_map),
            pl.BlockSpec((1, width), fixed),
            pl.BlockSpec((1, width), fixed),
            pl.BlockSpec(weight.shape, fixed),
            pl.BlockSpec((1, weight.shape[1]), fixed),
            pl.BlockSpec((block, LANES), row_map),
            pl.BlockSpec((block, LANES), row_map),
        ],
        out_specs=[pl.BlockSpec((block, columns), row_map), pl.BlockSpec((block, width), row_map)],
        out_shape=[jax.ShapeDtypeStruct((rows, columns), BF16), jax.ShapeDtypeStruct((rows, width), BF16)],
        compiler_params=pltpu.CompilerParams(vmem_limit_bytes=VMEM_LIMIT),
        cost_estimate=LIGHT,
        name="project",
    )(x, gain, bias, weight, add, cos_tab, sin_tab)


def place_kernel(where_ref, *refs, rows):
    *sources, out_ref = refs
    deep = sources[0].shape[0]
    for index in range(len(sources) * deep):
        first = pl.multiple_of(where_ref[index] * rows, rows)
        out_ref[pl.ds(first, rows), :] = sources[index // deep][index % deep, :rows, :]


def place(sources, where, rows):
    deep, _, width = sources[0].shape
    blocks = len(sources) * deep
    if rows % 16:
        out = jnp.concatenate([source[:, :rows] for source in sources])
        for index in range(blocks):
            block = sources[index // deep][index % deep, :rows]
            out = lax.dynamic_update_index_in_dim(out, block, where[index], 0)
        return out.reshape(blocks * rows, width)
    spec = pltpu.PrefetchScalarGridSpec(
        num_scalar_prefetch=1,
        grid=(1,),
        in_specs=[pl.BlockSpec(source.shape, lambda i, w: (0, 0, 0)) for source in sources],
        out_specs=pl.BlockSpec((blocks * rows, width), lambda i, w: (0, 0)),
    )
    return pl.pallas_call(
        functools.partial(place_kernel, rows=rows),
        grid_spec=spec,
        out_shape=jax.ShapeDtypeStruct((blocks * rows, width), sources[0].dtype),
        compiler_params=pltpu.CompilerParams(vmem_limit_bytes=VMEM_LIMIT),
        cost_estimate=LIGHT,
        name="place",
    )(where, *sources)


def head_parts(rows, factor):
    rows = rows.astype(F32) * factor
    lane = lax.broadcasted_iota(jnp.int32, rows.shape, 1)
    first = lane < HEAD_DIM
    return (jnp.where(first, rows, 0.0).astype(BF16), jnp.where(first, 0.0, rows).astype(BF16))


def flipped(tile):
    return tile.astype(F32).T.astype(BF16)


def nt_dot(a, b):
    return lax.dot_general(a, b, NT, preferred_element_type=F32)


def own_mask(limit_ref, noisy_rows, rows):
    at = lax.broadcasted_iota(jnp.int32, (noisy_rows, rows), 0)
    return (at >= limit_ref[1:2, :]) & (at < limit_ref[2:3, :])


def attend_kernel(count_ref, q_ref, kn_ref, vn_ref, kc_ref, vc_ref, limit_ref, o_ref, log_ref, *, block):
    rows = q_ref.shape[0]
    queries = head_parts(q_ref[...], SCALE)
    limit = limit_ref[0:1, :]

    def fold(state, parts):
        values = [flipped(part_values) for _, part_values, _ in parts]
        out = []
        for h in range(2):
            best, total, acc = state[h]
            heads = slice(h * HEAD_DIM, (h + 1) * HEAD_DIM)
            scores = [jnp.where(mask, nt_dot(keys, queries[h]), NEGATIVE) for keys, _, mask in parts]
            tops = [jnp.max(part, 0, keepdims=True) for part in scores]
            new_best = functools.reduce(jnp.maximum, tops, best)
            factor = jnp.exp(best - new_best)
            total = total * factor
            acc = acc * factor
            for part, part_values in zip(scores, values):
                weights = jnp.exp(part - new_best)
                total = total + jnp.sum(weights, 0, keepdims=True)
                acc = acc + jnp.dot(part_values[heads], weights.astype(BF16), preferred_element_type=F32)
            out.append((new_best, total, acc))
        return tuple(out)

    def clean_parts(index):
        parts = []
        for offset in range(0, block, piece):
            first = index * block + offset
            at = lax.broadcasted_iota(jnp.int32, (piece, rows), 0) + first
            if not isinstance(first, int):
                first = pl.multiple_of(first, piece)
            parts.append((kc_ref[pl.ds(first, piece), :], vc_ref[pl.ds(first, piece), :], at < limit))
        return parts

    piece = key_block(block, 512)
    own_part = (kn_ref[...], vn_ref[...], own_mask(limit_ref, kn_ref.shape[0], rows))
    start = (
        jnp.full((1, rows), NEGATIVE, F32),
        jnp.zeros((1, rows), F32),
        jnp.zeros((HEAD_DIM, rows), F32),
    )
    if block == kc_ref.shape[0]:
        state = fold((start, start), clean_parts(0) + [own_part])
    else:
        state = lax.fori_loop(0, count_ref[0], lambda i, state: fold(state, clean_parts(i)), (start, start))
        state = fold(state, [own_part])
    o_ref[...] = jnp.concatenate([acc / total for _, total, acc in state], 0).T.astype(BF16)
    for h in range(2):
        log_ref[0, h : h + 1, :] = state[h][0] + jnp.log(state[h][1])


def attend(count, own, clean, limits, block):
    rows = own.shape[0]
    length = clean.shape[0]
    pairs = own.shape[1] // (3 * LANES)
    spec = pltpu.PrefetchScalarGridSpec(
        num_scalar_prefetch=1,
        grid=(pairs,),
        in_specs=[
            pl.BlockSpec((rows, LANES), lambda p, c: (0, p)),
            pl.BlockSpec((rows // 2, LANES), lambda p, c: (0, pairs + p)),
            pl.BlockSpec((rows // 2, LANES), lambda p, c: (0, 2 * pairs + p)),
            pl.BlockSpec((length, LANES), lambda p, c: (0, p)),
            pl.BlockSpec((length, LANES), lambda p, c: (0, pairs + p)),
            pl.BlockSpec((8, rows), lambda p, c: (0, 0)),
        ],
        out_specs=[
            pl.BlockSpec((rows, LANES), lambda p, c: (0, p)),
            pl.BlockSpec((1, 8, rows), lambda p, c: (p, 0, 0)),
        ],
    )
    return pl.pallas_call(
        functools.partial(attend_kernel, block=block),
        grid_spec=spec,
        out_shape=[
            jax.ShapeDtypeStruct((rows, pairs * LANES), BF16),
            jax.ShapeDtypeStruct((pairs, 8, rows), F32),
        ],
        compiler_params=pltpu.CompilerParams(vmem_limit_bytes=VMEM_LIMIT),
        cost_estimate=LIGHT,
        name="attend",
    )(count, own, own, own, clean, clean, limits)


def attend_back_kernel(
    count_ref, q_ref, kn_ref, vn_ref, kc_ref, vc_ref, limit_ref, o_ref, do_ref, log_ref,
    cos_own_ref, sin_own_ref, cos_ref, sin_ref, dkv_ref, down_ref, sum_ref, *, block
):
    rows = q_ref.shape[0]
    noisy = kn_ref.shape[0]
    width = dkv_ref.shape[1] // 2
    length = kc_ref.shape[0]
    here = pl.multiple_of(pl.program_id(0) * LANES, LANES)
    queries = head_parts(q_ref[...], SCALE)
    grads = head_parts(do_ref[...], 1.0)
    limit = limit_ref[0:1, :]
    product = do_ref[...].astype(F32) * o_ref[...].astype(F32)
    lane = lax.broadcasted_iota(jnp.int32, (8, LANES), 1)
    deltas = []
    for h in range(2):
        ones = jnp.where((lane < HEAD_DIM) == (h == 0), 1.0, 0.0)
        deltas.append(
            lax.dot_general(ones, product, NT, precision=lax.Precision.HIGHEST, preferred_element_type=F32)[0:1]
        )

    def fold(dq, keys, values, mask):
        keys_flipped = flipped(keys)
        dk = dv = None
        out = []
        for h in range(2):
            scores = nt_dot(keys, queries[h])
            probs = jnp.where(mask, jnp.exp(scores - log_ref[0, h : h + 1, :]), 0.0)
            inner = nt_dot(values, grads[h])
            slopes = (probs * (inner - deltas[h])).astype(BF16)
            dv_new = jnp.dot(probs.astype(BF16), grads[h], preferred_element_type=F32)
            dk_new = jnp.dot(slopes, queries[h], preferred_element_type=F32)
            dv = dv_new if dv is None else dv + dv_new
            dk = dk_new if dk is None else dk + dk_new
            out.append(
                dq[h]
                + jnp.dot(keys_flipped[h * HEAD_DIM : (h + 1) * HEAD_DIM], slopes, preferred_element_type=F32)
            )
        return tuple(out), dk, dv

    def unturn(grad, cos_tab, sin_tab):
        return grad * cos_tab - swap_halves(grad) * sin_tab

    def step(index, carry):
        dq, sum_k, sum_v = carry
        first = pl.multiple_of(index * block, block)
        where = pl.ds(first, block)
        at = lax.broadcasted_iota(jnp.int32, (block, rows), 0) + index * block
        dq, dk, dv = fold(dq, kc_ref[where, :], vc_ref[where, :], at < limit)
        dk = unturn(dk, cos_ref[where, :], sin_ref[where, :])
        dkv_ref[where, pl.ds(here, LANES)] = dk.astype(BF16)
        dkv_ref[where, pl.ds(width + here, LANES)] = dv.astype(BF16)
        return dq, sum_k + jnp.sum(dk, 0, keepdims=True), sum_v + jnp.sum(dv, 0, keepdims=True)

    zero_q = jnp.zeros((HEAD_DIM, rows), F32)
    zero_sum = jnp.zeros((1, LANES), F32)
    dq, sum_k, sum_v = lax.fori_loop(0, count_ref[0], step, ((zero_q, zero_q), zero_sum, zero_sum))

    def blank(index, carry):
        where = pl.ds(pl.multiple_of(index * block, block), block)
        dkv_ref[where, pl.ds(here, LANES)] = jnp.zeros((block, LANES), BF16)
        dkv_ref[where, pl.ds(width + here, LANES)] = jnp.zeros((block, LANES), BF16)
        return carry

    lax.fori_loop(count_ref[0], length // block, blank, 0)
    dq, dk, dv = fold(dq, kn_ref[...], vn_ref[...], own_mask(limit_ref, noisy, rows))
    dk = unturn(dk, cos_own_ref[:noisy, :], sin_own_ref[:noisy, :])
    dq = unturn(jnp.concatenate(dq, 0).T * SCALE, cos_own_ref[...], sin_own_ref[...])
    zeros = jnp.zeros((rows - noisy, LANES), BF16)
    for part, grad in enumerate((dq, dk, dv)):
        down_ref[: grad.shape[0], pl.ds(part * width + here, LANES)] = grad.astype(BF16)
        if part > 0:
            down_ref[noisy:, pl.ds(part * width + here, LANES)] = zeros
    sums = (
        jnp.sum(dq, 0, keepdims=True),
        sum_k + jnp.sum(dk, 0, keepdims=True),
        sum_v + jnp.sum(dv, 0, keepdims=True),
    )
    for part in range(3):
        sum_ref[:, pl.ds(part * width + here, LANES)] = jnp.broadcast_to(sums[part], (8, LANES))


def attend_back(count, own, clean, limits, attn, grad, log_total, cos_own, sin_own, cos_tab, sin_tab, block):
    rows = own.shape[0]
    length, both = clean.shape
    pairs = own.shape[1] // (3 * LANES)
    spec = pltpu.PrefetchScalarGridSpec(
        num_scalar_prefetch=1,
        grid=(pairs,),
        in_specs=[
            pl.BlockSpec((rows, LANES), lambda p, c: (0, p)),
            pl.BlockSpec((rows // 2, LANES), lambda p, c: (0, pairs + p)),
            pl.BlockSpec((rows // 2, LANES), lambda p, c: (0, 2 * pairs + p)),
            pl.BlockSpec((length, LANES), lambda p, c: (0, p)),
            pl.BlockSpec((length, LANES), lambda p, c: (0, pairs + p)),
            pl.BlockSpec((8, rows), lambda p, c: (0, 0)),
            pl.BlockSpec((rows, LANES), lambda p, c: (0, p)),
            pl.BlockSpec((rows, LANES), lambda p, c: (0, p)),
            pl.BlockSpec((1, 8, rows), lambda p, c: (p, 0, 0)),
            pl.BlockSpec((rows, LANES), lambda p, c: (0, 0)),
            pl.BlockSpec((rows, LANES), lambda p, c: (0, 0)),
            pl.BlockSpec((length, LANES), lambda p, c: (0, 0)),
            pl.BlockSpec((length, LANES), lambda p, c: (0, 0)),
        ],
        out_specs=[
            pl.BlockSpec((length, both), lambda p, c: (0, 0)),
            pl.BlockSpec((rows, own.shape[1]), lambda p, c: (0, 0)),
            pl.BlockSpec((8, own.shape[1]), lambda p, c: (0, 0)),
        ],
    )
    return pl.pallas_call(
        functools.partial(attend_back_kernel, block=block),
        grid_spec=spec,
        out_shape=[
            jax.ShapeDtypeStruct((length, both), BF16),
            jax.ShapeDtypeStruct(own.shape, BF16),
            jax.ShapeDtypeStruct((8, own.shape[1]), F32),
        ],
        compiler_params=pltpu.CompilerParams(vmem_limit_bytes=VMEM_LIMIT),
        cost_estimate=LIGHT,
        name="attend_back",
    )(count, own, own, own, clean, clean, limits, attn, grad, log_total, cos_own, sin_own, cos_tab, sin_tab)


def feed_forward_kernel(
    core_ref, attn_ref, x_ref, top_ref, up_ref, down_ref, out_ref, vec_ref,
    block_out_ref, hidden_grad_ref, attn_grad_ref, weights_ref, mine_ref, theirs_ref,
    hidden, unit, inverse, normed, normed_flipped, lowered, grad_normed,
    up_grads, join_grads, down_grads, out_grads, vec_grads, sums, up_sems, join_sems, down_sems, last_sems,
    *, pairs, joined
):
    chunk = pl.program_id(0)
    chunks = pl.num_programs(0)
    width = x_ref.shape[1]

    @pl.when(chunk == 0)
    def _():
        value = (
            x_ref[...].astype(F32)
            + jnp.dot(attn_ref[...], out_ref[...], preferred_element_type=F32)
            + vec_ref[0:1, :]
        )
        hidden[...] = value
        center = value - jnp.mean(value, -1, keepdims=True)
        scale = lax.rsqrt(jnp.mean(center * center, -1, keepdims=True) + EPSILON)
        inverse[...] = scale
        unit[...] = center * scale
        scaled = unit[...] * vec_ref[1:2, :] + vec_ref[2:3, :]
        normed[...] = scaled.astype(BF16)
        normed_flipped[...] = scaled.T.astype(BF16)
        lowered[...] = jnp.zeros_like(lowered)
        grad_normed[...] = jnp.zeros_like(grad_normed)
        sums[...] = jnp.zeros_like(sums)

    upper = jnp.dot(normed[...], up_ref[...], preferred_element_type=F32) + vec_ref[pl.ds(4 + chunk, 1), :]
    grad_activ = nt_dot(top_ref[...], down_ref[...])
    inner = jnp.tanh(0.7978845608028654 * (upper + 0.044715 * upper * upper * upper))
    activ = 0.5 * upper * (1.0 + inner)
    slope = 0.5 * (1.0 + inner) + 0.5 * upper * (1.0 - inner * inner) * 0.7978845608028654 * (
        1.0 + 0.134145 * upper * upper
    )
    grad_upper = grad_activ * slope
    grad_low = grad_upper.astype(BF16)
    sums[pl.ds(4 + chunk, 1), :] = jnp.sum(grad_upper, 0, keepdims=True)
    lowered[...] += jnp.dot(activ.astype(BF16), down_ref[...], preferred_element_type=F32)
    grad_normed[...] += nt_dot(grad_low, up_ref[...])
    up_grads[chunk] = jnp.dot(normed_flipped[...], grad_low, preferred_element_type=F32).astype(BF16)
    down_grad = jnp.dot(activ.T.astype(BF16), top_ref[...], preferred_element_type=F32).astype(BF16)
    shard = width // (2 * pairs)

    @pl.when(chunk < joined)
    def _():
        join_grads[chunk] = down_grad

    @pl.when(chunk >= joined)
    def _():
        for pair in range(pairs):
            for core in range(2):
                first = (2 * pair + core) * shard
                down_grads[chunk - joined, core, pair * shard : (pair + 1) * shard, :] = down_grad[first : first + shard]

    def copy_up(index):
        columns = pl.ds(pl.multiple_of(index * width, width), width)
        return pltpu.make_async_copy(up_grads.at[index], weights_ref.at[:, columns], up_sems.at[index])

    def copy_join(index):
        columns = pl.ds(pl.multiple_of((chunks + index) * width, width), width)
        return pltpu.make_async_copy(join_grads.at[index], weights_ref.at[:, columns], join_sems.at[index])

    def copy_down(index):
        columns = pl.ds(pl.multiple_of(index * width, width), width)
        core = core_ref[0]
        return (
            pltpu.make_async_copy(down_grads.at[index, core], mine_ref.at[:, columns], down_sems.at[0, index]),
            pltpu.make_async_copy(down_grads.at[index, 1 - core], theirs_ref.at[:, columns], down_sems.at[1, index]),
        )

    copy_up(chunk).start()

    @pl.when(chunk < joined)
    def _():
        copy_join(chunk).start()

    @pl.when(chunk >= joined)
    def _():
        for copy in copy_down(chunk - joined):
            copy.start()

    @pl.when(chunk == chunks - 1)
    def _():
        top = top_ref[...].astype(F32)
        block_out_ref[...] = (hidden[...] + lowered[...] + vec_ref[3:4, :]).astype(BF16)
        grad = grad_normed[...]
        rows_unit = unit[...]
        sums[1:2, :] = jnp.sum(grad * rows_unit, 0, keepdims=True)
        sums[2:3, :] = jnp.sum(grad, 0, keepdims=True)
        sums[3:4, :] = jnp.sum(top, 0, keepdims=True)
        grad = grad * vec_ref[1:2, :]
        grad = inverse[...] * (
            grad - jnp.mean(grad, -1, keepdims=True) - rows_unit * jnp.mean(grad * rows_unit, -1, keepdims=True)
        )
        grad = top + grad
        hidden_grad_ref[...] = grad
        sums[0:1, :] = jnp.sum(grad, 0, keepdims=True)
        low = grad.astype(BF16)
        attn_grad_ref[...] = nt_dot(low, out_ref[...]).astype(BF16)
        out_grads[...] = jnp.dot(
            attn_ref[...].astype(F32).T.astype(BF16), low, preferred_element_type=F32
        ).astype(BF16)
        vec_grads[...] = sums[...].T.astype(BF16)
        first = (chunks + joined) * width
        copies = [
            pltpu.make_async_copy(out_grads, weights_ref.at[:, pl.ds(first, width)], last_sems.at[0]),
            pltpu.make_async_copy(vec_grads, weights_ref.at[:, pl.ds(first + width, LANES)], last_sems.at[1]),
        ]
        for copy in copies:
            copy.start()
        for index in range(up_grads.shape[0]):
            copy_up(index).wait()
        for index in range(joined):
            copy_join(index).wait()
        for index in range(down_grads.shape[0]):
            for copy in copy_down(index):
                copy.wait()
        for copy in copies:
            copy.wait()


def feed_forward(core, attn, x, top, weights, vectors, chunks, pairs, joined):
    rows, width = x.shape
    apart = chunks - joined
    fixed = lambda b, c: (0, 0)
    whole = pl.BlockSpec((rows, width), fixed)
    spec = pltpu.PrefetchScalarGridSpec(
        num_scalar_prefetch=1,
        grid=(chunks,),
        in_specs=[
            whole,
            whole,
            whole,
            pl.BlockSpec((width, width), lambda b, c: (0, b)),
            pl.BlockSpec((width, width), lambda b, c: (0, chunks + b)),
            pl.BlockSpec((width, width), lambda b, c: (0, 2 * chunks)),
            pl.BlockSpec(vectors.shape, fixed),
        ],
        out_specs=[whole, whole, whole] + [pl.BlockSpec(memory_space=pl.ANY)] * 3,
        scratch_shapes=[
            pltpu.VMEM((rows, width), F32),
            pltpu.VMEM((rows, width), F32),
            pltpu.VMEM((rows, 1), F32),
            pltpu.VMEM((rows, width), BF16),
            pltpu.VMEM((width, rows), BF16),
            pltpu.VMEM((rows, width), F32),
            pltpu.VMEM((rows, width), F32),
            pltpu.VMEM((chunks, width, width), BF16),
            pltpu.VMEM((joined, width, width), BF16),
            pltpu.VMEM((apart, 2, width // 2, width), BF16),
            pltpu.VMEM((width, width), BF16),
            pltpu.VMEM((width, LANES), BF16),
            pltpu.VMEM((LANES, width), F32),
            pltpu.SemaphoreType.DMA((chunks,)),
            pltpu.SemaphoreType.DMA((joined,)),
            pltpu.SemaphoreType.DMA((2, apart)),
            pltpu.SemaphoreType.DMA((2,)),
        ],
    )
    return pl.pallas_call(
        functools.partial(feed_forward_kernel, pairs=pairs, joined=joined),
        grid_spec=spec,
        out_shape=[
            jax.ShapeDtypeStruct((rows, width), BF16),
            jax.ShapeDtypeStruct((rows, width), F32),
            jax.ShapeDtypeStruct((rows, width), BF16),
            jax.ShapeDtypeStruct((width, weights.shape[1] - apart * width), BF16),
            jax.ShapeDtypeStruct((width // 2, apart * width), BF16),
            jax.ShapeDtypeStruct((width // 2, apart * width), BF16),
        ],
        compiler_params=pltpu.CompilerParams(vmem_limit_bytes=VMEM_LIMIT),
        cost_estimate=LIGHT,
        name="feed_forward",
    )(core.reshape(1), attn, x, top, weights, weights, weights, vectors)


def after(value, *others):
    return lax.optimization_barrier((value,) + others)[0]


def pick(array, index, axis=0):
    return lax.dynamic_index_in_dim(array, index, axis, keepdims=False)


def ordered(flag, own, other, axis):
    return jnp.stack([jnp.where(flag == 0, own, other), jnp.where(flag == 0, other, own)], axis)


class Links:
    def __init__(self):
        self.count = lax.axis_size("ctx")
        self.deep = self.count // 4
        at = lax.axis_index("ctx")
        self.x = lax.axis_index("batch")
        self.core = at % 2
        self.y = (at // 2) % 2
        self.z = at // 4
        self.chip = at // 2

    def over_core(self, array):
        return lax.ppermute(array, "ctx", [(i, i ^ 1) for i in range(self.count)])

    def over_y(self, array):
        return lax.ppermute(array, "ctx", [(i, i ^ 2) for i in range(self.count)])

    def over_x(self, array):
        return lax.ppermute(array, "batch", [(0, 1), (1, 0)])

    def along_z(self, array, hop):
        count = self.count
        return lax.ppermute(array, "ctx", [(i, (i + 4 * hop) % count) for i in range(count)])

    def around_z(self, piece):
        return [self.along_z(piece, hop) for hop in range(1, self.deep)]

    def column(self, piece, others):
        deep = self.deep
        whole = jnp.broadcast_to(piece[None], (deep,) + piece.shape)
        for hop, other in enumerate(others, 1):
            whole = lax.dynamic_update_index_in_dim(whole, other, (self.z - hop) % deep, 0)
        return whole

    def swap_z(self, parts):
        return [self.along_z(pick(parts, (self.z + hop) % self.deep), hop) for hop in range(1, self.deep)]

    def sum_z(self, parts, others):
        total = pick(parts, self.z).astype(F32)
        for other in others:
            total = total + other.astype(F32)
        return total


def unit_rows(values):
    center = values - jnp.mean(values, -1, keepdims=True)
    spread = jnp.mean(center * center, -1, keepdims=True)
    inverse = lax.rsqrt(spread + EPSILON)
    return center * inverse, inverse


def unit_back(grad, unit, inverse):
    return inverse * (
        grad - jnp.mean(grad, -1, keepdims=True) - unit * jnp.mean(grad * unit, -1, keepdims=True)
    )


def rotary_tables(positions):
    half_dim = HEAD_DIM // 2
    inverse = 1.0 / THETA ** (jnp.arange(half_dim, dtype=F32) / half_dim)
    angles = positions.astype(F32)[:, None] * jnp.tile(inverse, LANES // half_dim)[None, :]
    sign = jnp.where(jnp.arange(LANES) % HEAD_DIM < half_dim, -1.0, 1.0)
    return jnp.cos(angles), jnp.sin(angles) * sign[None, :]


def key_block(length, limit):
    sizes = [size for size in range(16, limit + 1, 16) if length % size == 0]
    return sizes[-1] if sizes else length


def row_block(rows):
    for block in (512, 384, 256, 128, 64, 32, 16):
        if rows % block == 0:
            return block
    return rows


def dot(a, b):
    return jnp.dot(a, b, preferred_element_type=F32)


def dot_left(a, b):
    return lax.dot_general(a, b, (((0,), (0,)), ((), ())), preferred_element_type=F32)


def on_device(
    layer_input, cotangent, prefix, block_size, ln1_gain, ln1_bias, qkv_weight, qkv_bias, out_weight, out_bias,
    ln2_gain, ln2_bias, up_weight, up_bias, down_weight, down_bias,
):
    links = Links()
    core = links.core
    seqs, _, pos_dev, width = layer_input.shape
    devices = 2 * links.count
    length = links.count * pos_dev
    half = width // 2
    rows = 4 * pos_dev
    shard = ln1_gain.shape[0]
    hidden_shard = up_bias.shape[0]

    split = qkv_weight.reshape(shard, 3, 2, half)
    vec_one = jnp.concatenate([ln1_gain, ln1_bias, qkv_bias])
    vec_one = ordered(core, vec_one, links.over_core(vec_one), 0).reshape(1, -1)
    vec_one = jnp.pad(vec_one, ((0, 7), (0, width - vec_one.shape[1])))
    qkv_piece = ordered(core, pick(split, core, 2), links.over_core(pick(split, 1 - core, 2)), 0)
    qkv_piece = qkv_piece.reshape(2 * shard, 3 * half)
    cos_tab, sin_tab = rotary_tables(after(jnp.arange(length, dtype=jnp.int32), qkv_piece))
    qkv_others = links.around_z(qkv_piece)
    inputs_got = links.over_core(layer_input)
    qkv_column = jnp.stack([qkv_piece] + qkv_others)
    qkv_got = links.over_y(qkv_column)
    qkv_far = links.over_x(qkv_column)
    clean_piece = jnp.concatenate([layer_input[0, 1], vec_one])
    clean_piece = after(clean_piece, cos_tab, sin_tab, inputs_got, *qkv_others)
    clean_others = links.around_z(clean_piece)
    gate = (qkv_got, qkv_far) + tuple(clean_others)
    weights_gate = gate
    qkv_last = links.over_x(after(qkv_got, *gate))
    hops = jnp.arange(links.deep, dtype=jnp.int32)
    levels = (links.z - hops) % links.deep
    arrived = []
    for s in range(seqs):
        column = after(jnp.stack([clean_piece] + clean_others), *gate)
        got = links.over_y(column)
        gate = (got,)
        if s + 1 < seqs:
            clean_piece = after(layer_input[s + 1, 1], column)
            clean_others = links.around_z(clean_piece)
            gate = gate + tuple(clean_others)
        if s == 0:
            vec_near = jnp.stack([column[:, pos_dev], got[:, pos_dev]])
            vec_far = links.over_x(vec_near)
            gate = gate + (qkv_last,)
        arrived.append((column, got, links.over_core(column)))
    where = jnp.concatenate(
        [(x * links.deep + levels) * 2 + y for x in (links.x, 1 - links.x) for y in (links.y, 1 - links.y)]
    )
    qkv_mat = place([qkv_column, qkv_got, qkv_far, qkv_last], where, 2 * shard)
    vec_one = jnp.concatenate([vec_near, vec_far]).reshape(where.shape[0], width).astype(F32)
    turn = (where[None, :] == jnp.arange(where.shape[0], dtype=jnp.int32)[:, None]).astype(F32)
    vec_one = jnp.dot(turn, vec_one[:, : 2 * (2 * shard + qkv_bias.shape[0])], precision=lax.Precision.HIGHEST)
    vec_one = vec_one.reshape(devices, -1)
    gain_one = vec_one[:, :shard].reshape(1, width)
    bias_one = vec_one[:, shard : 2 * shard].reshape(1, width)
    qkv_add = pick(vec_one[:, 2 * shard :].reshape(3, 2, half), core, 1).reshape(1, 3 * half)

    folds = hidden_shard // shard
    up_piece = up_weight.reshape(shard, devices, folds, shard).transpose(0, 2, 1, 3).reshape(shard, -1)
    down_piece = down_weight.reshape(folds, shard, width).transpose(1, 0, 2).reshape(shard, -1)
    vec_piece = jnp.stack(
        [out_bias, ln2_gain, ln2_bias, down_bias] + [up_bias[i * shard : (i + 1) * shard] for i in range(folds)], 1
    )
    vec_piece = jnp.pad(vec_piece, ((0, 0), (0, LANES - vec_piece.shape[1])))
    packed = after(jnp.concatenate([up_piece, down_piece, out_weight, vec_piece], 1), *weights_gate)
    weights = lax.all_gather(packed, ("batch", "ctx"), axis=0, tiled=True)
    vectors = weights[:, -LANES:].T[: 4 + folds].astype(F32)

    inputs_pair = ordered(core, layer_input, inputs_got, 2).reshape(seqs, rows, width)

    first_pos = links.chip * 2 * pos_dev
    cos_own = jnp.tile(lax.dynamic_slice_in_dim(cos_tab, first_pos, 2 * pos_dev, 0), (2, 1))
    sin_own = jnp.tile(lax.dynamic_slice_in_dim(sin_tab, first_pos, 2 * pos_dev, 0), (2, 1))
    block = key_block(length, 1536)
    at = after(jnp.arange(2 * pos_dev, dtype=jnp.int32), qkv_last)
    position = first_pos + at
    own_qkv, own_unit = project(
        inputs_pair.reshape(seqs * rows, width), gain_one, bias_one, qkv_mat, qkv_add,
        jnp.tile(cos_own, (seqs, 1)), jnp.tile(sin_own, (seqs, 1)), 0, width, row_block(rows),
    )
    own_qkv = own_qkv.reshape(seqs, rows, 3 * half)
    clean_kv, clean_unit, limit_list, counts, attn_list, log_list = ([] for _ in range(6))
    for s in range(seqs):
        near = jnp.floor((position.astype(F32) + 0.5) / block_size[s].astype(F32)).astype(jnp.int32) * block_size[s]
        ends = near + block_size[s]
        noisy_limit = jnp.maximum(near, prefix[s])
        clean_limit = jnp.where(position < prefix[s], prefix[s], ends)
        limit = jnp.concatenate([noisy_limit, clean_limit])
        none = jnp.zeros_like(at)
        limits = jnp.stack(
            [limit, jnp.concatenate([near - first_pos, none]), jnp.concatenate([ends - first_pos, none])]
            + [jnp.zeros_like(limit)] * 5
        )
        count = jnp.minimum((jnp.max(limit) + block - 1) // block, length // block).reshape(1)
        column, got, column_far = arrived[s]
        got = after(got, *([clean_kv[-1]] if s else [own_qkv]))
        where = jnp.concatenate(
            [(levels * 2 + y) * 2 + c for c in (core, 1 - core) for y in (links.y, 1 - links.y)]
        )
        clean_rows = place([column, got, column_far, links.over_core(got)], where, pos_dev)
        clean, all_unit = project(
            clean_rows, gain_one, bias_one, qkv_mat, qkv_add, cos_tab, sin_tab, half, half, row_block(length)
        )
        attn, log_total = attend(count, own_qkv[s], clean, limits, block)
        for kept, value in zip(
            (clean_kv, clean_unit, limit_list, counts, attn_list, log_list),
            (clean, all_unit, limits, count, attn, log_total),
        ):
            kept.append(value)

    attn_rows = jnp.stack(attn_list).reshape(seqs, 2, 2, pos_dev, half)
    attn_got = links.over_core(pick(attn_rows, 1 - core, 2))
    attn_low = ordered(core, pick(attn_rows, core, 2), attn_got, 3).reshape(-1, width)
    flat_inputs = layer_input.reshape(-1, width)
    joined = folds * 3 // 4
    apart = folds - joined
    output, grad_hidden, grad_attn, weight_grads, down_mine, down_theirs = feed_forward(
        core, attn_low, flat_inputs, cotangent.reshape(-1, width), weights, vectors, folds, links.count, joined
    )
    output = output.reshape(layer_input.shape)
    packed = lax.psum_scatter(weight_grads, ("batch", "ctx"), scatter_dimension=0, tiled=True)
    down_got = links.over_core(down_theirs)
    down_part = (down_mine.astype(F32) + down_got.astype(F32)).astype(BF16)
    down_part = down_part.reshape(2, links.deep, 2, shard * apart, width)
    down_sent = pick(down_part, 1 - links.x)
    down_got = links.over_x(down_sent)

    grad_split = grad_attn.reshape(-1, 2, half)
    grad_got = links.over_core(pick(grad_split, 1 - core, 1))
    grad_rows = ordered(
        core,
        pick(grad_split, core, 1).reshape(seqs, 2, pos_dev, half),
        grad_got.reshape(seqs, 2, pos_dev, half),
        2,
    ).reshape(seqs, rows, half)
    kv_mat = qkv_mat[:, half:]
    own_unit = own_unit.reshape(seqs, rows, width)
    unit_part = jnp.zeros((width, 3 * half), F32)
    kv_part = jnp.zeros((width, 2 * half), F32)
    column_sums = 0.0
    waiting, gate = [], ()
    for s in range(seqs):
        clean_grad, own_grad, sums = attend_back(
            counts[s], own_qkv[s], clean_kv[s], limit_list[s], attn_list[s], after(grad_rows[s], *gate),
            log_list[s], cos_own, sin_own, cos_tab, sin_tab, block,
        )
        spread = lax.dot_general(clean_grad, kv_mat, NT, preferred_element_type=F32).astype(BF16)
        local = lax.dot_general(own_grad, qkv_mat, NT, preferred_element_type=F32).astype(BF16)
        spread = spread.reshape(2 * links.deep, 2, pos_dev, width)
        local = local.reshape(2, 2, pos_dev, width)
        theirs = jnp.concatenate([pick(spread, 1 - core, 1), pick(local, 1 - core, 1)])
        got = links.over_core(theirs)
        gate = (theirs,)
        if s == seqs - 1:
            down_got = after(down_got, own_grad)
            down_part = (pick(down_part, links.x).astype(F32) + down_got.astype(F32)).astype(BF16)
            down_sent = pick(down_part, 1 - links.y, 1)
            down_got = links.over_y(down_sent)
            gate = (theirs, down_sent)
        unit_part = unit_part + dot_left(own_unit[s], after(own_grad, *gate))
        kv_part = kv_part + dot_left(clean_unit[s], after(clean_grad, *gate))
        column_sums = column_sums + sums[0]
        if s == seqs - 1:
            qkv_part = (unit_part + jnp.pad(kv_part, ((0, 0), (half, 0)))).astype(BF16)
            qkv_part = qkv_part.reshape(2, links.deep, 2, 2 * shard, 3 * half)
            far_part = pick(qkv_part, 1 - links.x)
            qkv_far = links.over_x(far_part)
        mine = pick(spread, core, 1).astype(F32) + got[: 2 * links.deep].astype(F32)
        mine = mine.astype(BF16).reshape(links.deep, 2, pos_dev, width)
        local = pick(local, core, 1).astype(F32) + got[2 * links.deep :].astype(F32)
        if s == seqs - 1:
            below = jnp.pad(column_sums, (0, 8 * width - 3 * half)).astype(BF16).reshape(1, 1, 8, width)
            mine = jnp.concatenate([mine, jnp.broadcast_to(below, (links.deep, 2, 8, width))], 2)
        theirs = pick(mine, 1 - links.y, 1)
        row_got = links.over_y(theirs)
        waiting.append((mine, local, row_got))
        gate = (theirs, down_sent)
    down_part = pick(after(down_part, far_part), links.y, 1).astype(F32)
    down_part = (down_part + down_got.astype(F32)).astype(BF16)
    summed = []
    for mine, _, row_got in waiting:
        mine = (pick(mine, links.y, 1).astype(F32) + after(row_got, far_part).astype(F32)).astype(BF16)
        summed.append(mine)
    first = jnp.concatenate(summed[:-1] + [down_part], 1)
    first_others = links.swap_z(first)
    others = links.swap_z(summed[-1])
    total = links.sum_z(summed[-1], others)
    first_others = after(tuple(first_others), summed[-1])
    first = links.sum_z(first, first_others)
    own_rows = [
        jnp.stack([local[0], local[1] + (first[s * pos_dev : (s + 1) * pos_dev] if s < seqs - 1 else total[:pos_dev])])
        for s, (_, local, _) in enumerate(waiting)
    ]
    down_sum = first[(seqs - 1) * pos_dev :]
    column_sums = total[pos_dev:].reshape(-1)[: 3 * half].reshape(3, half)
    column_sums = column_sums + links.over_x(column_sums)
    column_sums = ordered(core, column_sums, links.over_core(column_sums), 1).reshape(3 * width)

    grad_normed_one = jnp.stack(own_rows).reshape(-1, width)
    unit_one, inverse_one = unit_rows(after(flat_inputs, far_part).astype(F32))
    grad_input = grad_hidden + unit_back(grad_normed_one * gain_one, unit_one, inverse_one)
    grad_input = grad_input.astype(BF16).reshape(layer_input.shape)

    qkv_part = (pick(after(qkv_part, packed), links.x).astype(F32) + qkv_far.astype(F32)).astype(BF16)
    qkv_far = links.over_y(after(pick(qkv_part, 1 - links.y, 1), waiting[-1][2]))
    qkv_part = (pick(qkv_part, links.y, 1).astype(F32) + qkv_far.astype(F32)).astype(BF16)
    qkv_part = after(qkv_part, summed[-1])
    qkv_sum = links.sum_z(qkv_part, links.swap_z(qkv_part)).reshape(2, shard, 3, half)
    qkv_got = links.over_core(pick(qkv_sum, 1 - core))
    qkv_sum = ordered(core, pick(qkv_sum, core), qkv_got, 2).reshape(shard, 3 * width)
    grad_qkv = ln1_gain.astype(F32)[:, None] * qkv_sum + ln1_bias.astype(F32)[:, None] * column_sums[None, :]
    own_weight = qkv_weight.astype(F32)
    grad_gain_one = jnp.sum(own_weight * qkv_sum, -1)
    grad_bias_one = jnp.sum(own_weight * column_sums[None, :], -1)
    device = links.x * links.count + lax.axis_index("ctx")
    grad_qk_bias = lax.dynamic_slice_in_dim(column_sums[: 2 * width], device * 2 * shard, 2 * shard, 0)
    grad_value_bias = lax.dynamic_slice_in_dim(column_sums[2 * width :], device * shard, shard, 0)

    hidden_width = devices * hidden_shard
    packed = packed.astype(F32)
    grad_up = packed[:, :hidden_width].reshape(shard, folds, devices, shard).transpose(0, 2, 1, 3)
    grad_up = grad_up.reshape(shard, hidden_width)
    first_down = packed[:, hidden_width : hidden_width + joined * width].reshape(shard, joined, width)
    grad_down = jnp.concatenate([first_down, down_sum.reshape(shard, apart, width)], 1)
    grad_down = grad_down.transpose(1, 0, 2).reshape(hidden_shard, width)
    grad_out = packed[:, hidden_width + joined * width : -LANES]
    late = packed[:, -LANES:].T

    return (
        output, grad_input, grad_gain_one, grad_bias_one, grad_qkv, grad_qk_bias, grad_value_bias, grad_out,
        late[0], late[1], late[2], grad_up, late[4 : 4 + folds].reshape(-1), grad_down, late[3],
    )


def solution(mesh):
    every = P(("batch", "ctx"))
    matrix = P(("batch", "ctx"), None)
    acts = P("batch", None, "ctx", None)
    return jax.shard_map(
        on_device,
        mesh=mesh,
        in_specs=(
            acts, acts, P("batch"), P("batch"), every, every, matrix, every, matrix, every, every, every, matrix,
            every, matrix, every,
        ),
        out_specs=(
            acts, acts, every, every, matrix, every, every, matrix, every, every, every, matrix, every, matrix, every,
        ),
        check_vma=False,
    )
```

```python
import functools

import jax
import jax.numpy as jnp
from jax import lax
from jax.experimental import pallas as pl
from jax.experimental.pallas import tpu as pltpu
from jax.sharding import PartitionSpec as P

HEADS = 12
HEAD_DIM = 64
SCALE = 0.125
NEGATIVE = -1e30
EPSILON = 1e-05
THETA = 10000.0
LANES = 128
BF16 = jnp.bfloat16
F32 = jnp.float32
VMEM_LIMIT = 56 * 1024 * 1024
NT = (((1,), (1,)), ((), ()))
LIGHT = pl.CostEstimate(flops=1, bytes_accessed=1, transcendentals=0)


def swap_halves(tile):
    lane = lax.broadcasted_iota(jnp.int32, tile.shape, 1)
    return jnp.where(lane % 64 < 32, pltpu.roll(tile, LANES - 32, 1), pltpu.roll(tile, 32, 1))


def project_rows(x, gain_ref, bias_ref, w_ref, add_ref, cos_ref, sin_ref, out_ref, unit_ref, start, turned):
    x = x.astype(F32)
    center = x - jnp.mean(x, -1, keepdims=True)
    spread = jnp.mean(center * center, -1, keepdims=True)
    unit = center * lax.rsqrt(spread + EPSILON)
    unit_ref[...] = unit.astype(BF16)
    normed = (unit * gain_ref[...] + bias_ref[...]).astype(BF16)
    cos_tab, sin_tab = cos_ref[...], sin_ref[...]
    total = jnp.dot(normed, w_ref[:, start:], preferred_element_type=F32) + add_ref[:, start:]
    for tile in range(total.shape[1] // LANES):
        part = total[:, tile * LANES : (tile + 1) * LANES]
        if tile * LANES < turned:
            part = part * cos_tab + swap_halves(part) * sin_tab
        out_ref[:, tile * LANES : (tile + 1) * LANES] = part.astype(BF16)


def project_kernel(x_ref, *refs, start, turned):
    project_rows(x_ref[...], *refs, start, turned)


def project_parts_kernel(where_ref, a_ref, b_ref, c_ref, d_ref, *refs, start, turned):
    *refs, rows_ref = refs
    rows = rows_ref.shape[0] // 4
    for index, part in enumerate((a_ref, b_ref, c_ref, d_ref)):
        first = pl.multiple_of(where_ref[1 + index] * rows, rows)
        rows_ref[pl.ds(first, rows), :] = part[0, :rows, :]
    project_rows(rows_ref[...], *refs, start, turned)


def project_parts(where, parts, rows, gain, bias, weight, add, cos_tab, sin_tab, start, turned):
    deep, _, width = parts[0].shape
    columns = weight.shape[1] - start
    block = 4 * rows
    row_map = lambda i, w: (i, 0)
    fixed = lambda i, w: (0, 0)
    spec = pltpu.PrefetchScalarGridSpec(
        num_scalar_prefetch=1,
        grid=(deep,),
        in_specs=[
            pl.BlockSpec((1,) + part.shape[1:], lambda i, w: (lax.rem(w[0] - i + deep, deep), 0, 0)) for part in parts
        ]
        + [
            pl.BlockSpec((1, width), fixed),
            pl.BlockSpec((1, width), fixed),
            pl.BlockSpec(weight.shape, fixed),
            pl.BlockSpec((1, weight.shape[1]), fixed),
            pl.BlockSpec((block, LANES), row_map),
            pl.BlockSpec((block, LANES), row_map),
        ],
        out_specs=[pl.BlockSpec((block, columns), row_map), pl.BlockSpec((block, width), row_map)],
        scratch_shapes=[pltpu.VMEM((block, width), BF16)],
    )
    return pl.pallas_call(
        functools.partial(project_parts_kernel, start=start, turned=turned),
        grid_spec=spec,
        out_shape=[
            jax.ShapeDtypeStruct((deep * block, columns), BF16),
            jax.ShapeDtypeStruct((deep * block, width), BF16),
        ],
        compiler_params=pltpu.CompilerParams(vmem_limit_bytes=VMEM_LIMIT),
        cost_estimate=LIGHT,
        name="project_parts",
    )(where, *parts, gain, bias, weight, add, cos_tab, sin_tab)


def project(x, gain, bias, weight, add, cos_tab, sin_tab, start, turned, block):
    table_blocks = cos_tab.shape[0] // block
    rows, width = x.shape
    columns = weight.shape[1] - start
    row_map = lambda i: (i, 0)
    fixed = lambda i: (0, 0)
    return pl.pallas_call(
        functools.partial(project_kernel, start=start, turned=turned),
        grid=(rows // block,),
        in_specs=[
            pl.BlockSpec((block, width), row_map),
            pl.BlockSpec((1, width), fixed),
            pl.BlockSpec((1, width), fixed),
            pl.BlockSpec(weight.shape, fixed),
            pl.BlockSpec((1, weight.shape[1]), fixed),
            pl.BlockSpec((block, LANES), lambda i: (i % table_blocks, 0)),
            pl.BlockSpec((block, LANES), lambda i: (i % table_blocks, 0)),
        ],
        out_specs=[pl.BlockSpec((block, columns), row_map), pl.BlockSpec((block, width), row_map)],
        out_shape=[jax.ShapeDtypeStruct((rows, columns), BF16), jax.ShapeDtypeStruct((rows, width), BF16)],
        compiler_params=pltpu.CompilerParams(vmem_limit_bytes=VMEM_LIMIT),
        cost_estimate=LIGHT,
        name="project",
    )(x, gain, bias, weight, add, cos_tab, sin_tab)


def place_kernel(where_ref, *refs, rows):
    *sources, out_ref = refs
    deep = sources[0].shape[0]
    for index in range(len(sources) * deep):
        first = pl.multiple_of(where_ref[index] * rows, rows)
        out_ref[pl.ds(first, rows), :] = sources[index // deep][index % deep, :rows, :]


def place(sources, where, rows):
    deep, _, width = sources[0].shape
    blocks = len(sources) * deep
    if rows % 16:
        out = jnp.concatenate([source[:, :rows] for source in sources])
        for index in range(blocks):
            block = sources[index // deep][index % deep, :rows]
            out = lax.dynamic_update_index_in_dim(out, block, where[index], 0)
        return out.reshape(blocks * rows, width)
    spec = pltpu.PrefetchScalarGridSpec(
        num_scalar_prefetch=1,
        grid=(1,),
        in_specs=[pl.BlockSpec(source.shape, lambda i, w: (0, 0, 0)) for source in sources],
        out_specs=pl.BlockSpec((blocks * rows, width), lambda i, w: (0, 0)),
    )
    return pl.pallas_call(
        functools.partial(place_kernel, rows=rows),
        grid_spec=spec,
        out_shape=jax.ShapeDtypeStruct((blocks * rows, width), sources[0].dtype),
        compiler_params=pltpu.CompilerParams(vmem_limit_bytes=VMEM_LIMIT),
        cost_estimate=LIGHT,
        name="place",
    )(where, *sources)


def head_parts(rows, factor):
    rows = rows.astype(F32) * factor
    lane = lax.broadcasted_iota(jnp.int32, rows.shape, 1)
    first = lane < HEAD_DIM
    return (jnp.where(first, rows, 0.0).astype(BF16), jnp.where(first, 0.0, rows).astype(BF16))


def flipped(tile):
    return tile.astype(F32).T.astype(BF16)


def nt_dot(a, b):
    return lax.dot_general(a, b, NT, preferred_element_type=F32)


def sight(scalars_ref, rows):
    prefix, size, first = scalars_ref[0], scalars_ref[1], scalars_ref[2]
    row = lax.broadcasted_iota(jnp.int32, (1, rows), 1)
    noisy = row < rows // 2
    position = first + jnp.where(noisy, row, row - rows // 2)
    near = jnp.floor((position.astype(F32) + 0.5) / size.astype(F32)).astype(jnp.int32) * size
    clean_limit = jnp.where(position < prefix, prefix, near + size)
    limit = jnp.where(noisy, jnp.maximum(near, prefix), clean_limit)
    low = near - first
    return limit, low, jnp.where(noisy, low + size, low)


def own_mask(low, high, noisy_rows):
    at = lax.broadcasted_iota(jnp.int32, (noisy_rows, low.shape[1]), 0)
    return (at >= low) & (at < high)


def attend_kernel(scalars_ref, q_ref, kn_ref, vn_ref, kc_ref, vc_ref, o_ref, log_ref, *, block):
    rows = q_ref.shape[0]
    queries = head_parts(q_ref[...], SCALE)
    limit, low, high = sight(scalars_ref, rows)

    def fold(state, parts):
        values = [flipped(part_values) for _, part_values, _ in parts]
        out = []
        for h in range(2):
            best, total, acc = state[h]
            heads = slice(h * HEAD_DIM, (h + 1) * HEAD_DIM)
            scores = [jnp.where(mask, nt_dot(keys, queries[h]), NEGATIVE) for keys, _, mask in parts]
            tops = [jnp.max(part, 0, keepdims=True) for part in scores]
            new_best = functools.reduce(jnp.maximum, tops, best)
            factor = jnp.exp(best - new_best)
            total = total * factor
            acc = acc * factor
            for part, part_values in zip(scores, values):
                weights = jnp.exp(part - new_best)
                total = total + jnp.sum(weights, 0, keepdims=True)
                acc = acc + jnp.dot(part_values[heads], weights.astype(BF16), preferred_element_type=F32)
            out.append((new_best, total, acc))
        return tuple(out)

    def clean_parts(index):
        parts = []
        for offset in range(0, block, piece):
            first = index * block + offset
            at = lax.broadcasted_iota(jnp.int32, (piece, rows), 0) + first
            if not isinstance(first, int):
                first = pl.multiple_of(first, piece)
            parts.append((kc_ref[pl.ds(first, piece), :], vc_ref[pl.ds(first, piece), :], at < limit))
        return parts

    piece = key_block(block, 512)
    own_part = (kn_ref[...], vn_ref[...], own_mask(low, high, kn_ref.shape[0]))
    start = (
        jnp.full((1, rows), NEGATIVE, F32),
        jnp.zeros((1, rows), F32),
        jnp.zeros((HEAD_DIM, rows), F32),
    )
    if block == kc_ref.shape[0]:
        state = fold((start, start), clean_parts(0) + [own_part])
    else:
        state = lax.fori_loop(0, kc_ref.shape[0] // block, lambda i, state: fold(state, clean_parts(i)), (start, start))
        state = fold(state, [own_part])
    o_ref[...] = jnp.concatenate([acc / total for _, total, acc in state], 0).T.astype(BF16)
    for h in range(2):
        log_ref[0, h : h + 1, :] = state[h][0] + jnp.log(state[h][1])


def attend(scalars, own, s, seqs, clean, block):
    rows = own.shape[0] // seqs
    length = clean.shape[0]
    pairs = own.shape[1] // (3 * LANES)
    spec = pltpu.PrefetchScalarGridSpec(
        num_scalar_prefetch=1,
        grid=(pairs,),
        in_specs=[
            pl.BlockSpec((rows, LANES), lambda p, c: (s, p)),
            pl.BlockSpec((rows // 2, LANES), lambda p, c: (2 * s, pairs + p)),
            pl.BlockSpec((rows // 2, LANES), lambda p, c: (2 * s, 2 * pairs + p)),
            pl.BlockSpec((length, LANES), lambda p, c: (0, p)),
            pl.BlockSpec((length, LANES), lambda p, c: (0, pairs + p)),
        ],
        out_specs=[
            pl.BlockSpec((rows, LANES), lambda p, c: (0, p)),
            pl.BlockSpec((1, 8, rows), lambda p, c: (p, 0, 0)),
        ],
    )
    return pl.pallas_call(
        functools.partial(attend_kernel, block=block),
        grid_spec=spec,
        out_shape=[
            jax.ShapeDtypeStruct((rows, pairs * LANES), BF16),
            jax.ShapeDtypeStruct((pairs, 8, rows), F32),
        ],
        compiler_params=pltpu.CompilerParams(vmem_limit_bytes=VMEM_LIMIT),
        cost_estimate=LIGHT,
        name="attend",
    )(scalars, own, own, own, clean, clean)


def attend_back_kernel(
    scalars_ref, q_ref, kn_ref, vn_ref, kc_ref, vc_ref, o_ref, do_ref, log_ref,
    cos_own_ref, sin_own_ref, cos_ref, sin_ref, dkv_ref, down_ref, sum_ref, *, block
):
    rows = q_ref.shape[0]
    noisy = kn_ref.shape[0]
    width = dkv_ref.shape[1] // 2
    length = kc_ref.shape[0]
    here = pl.multiple_of(pl.program_id(0) * LANES, LANES)
    queries = head_parts(q_ref[...], SCALE)
    grads = head_parts(do_ref[...], 1.0)
    limit, low, high = sight(scalars_ref, rows)
    product = do_ref[...].astype(F32) * o_ref[...].astype(F32)
    lane = lax.broadcasted_iota(jnp.int32, (8, LANES), 1)
    deltas = []
    for h in range(2):
        ones = jnp.where((lane < HEAD_DIM) == (h == 0), 1.0, 0.0)
        deltas.append(
            lax.dot_general(ones, product, NT, precision=lax.Precision.HIGHEST, preferred_element_type=F32)[0:1]
        )

    def fold(dq, keys, values, mask):
        keys_flipped = flipped(keys)
        dk = dv = None
        out = []
        for h in range(2):
            scores = nt_dot(keys, queries[h])
            probs = jnp.where(mask, jnp.exp(scores - log_ref[0, h : h + 1, :]), 0.0)
            inner = nt_dot(values, grads[h])
            slopes = (probs * (inner - deltas[h])).astype(BF16)
            dv_new = jnp.dot(probs.astype(BF16), grads[h], preferred_element_type=F32)
            dk_new = jnp.dot(slopes, queries[h], preferred_element_type=F32)
            dv = dv_new if dv is None else dv + dv_new
            dk = dk_new if dk is None else dk + dk_new
            out.append(
                dq[h]
                + jnp.dot(keys_flipped[h * HEAD_DIM : (h + 1) * HEAD_DIM], slopes, preferred_element_type=F32)
            )
        return tuple(out), dk, dv

    def unturn(grad, cos_tab, sin_tab):
        return grad * cos_tab - swap_halves(grad) * sin_tab

    def step(index, carry):
        dq, sum_k, sum_v = carry
        first = pl.multiple_of(index * block, block)
        where = pl.ds(first, block)
        at = lax.broadcasted_iota(jnp.int32, (block, rows), 0) + index * block
        dq, dk, dv = fold(dq, kc_ref[where, :], vc_ref[where, :], at < limit)
        dk = unturn(dk, cos_ref[where, :], sin_ref[where, :])
        dkv_ref[where, pl.ds(here, LANES)] = dk.astype(BF16)
        dkv_ref[where, pl.ds(width + here, LANES)] = dv.astype(BF16)
        return dq, sum_k + jnp.sum(dk, 0, keepdims=True), sum_v + jnp.sum(dv, 0, keepdims=True)

    zero_q = jnp.zeros((HEAD_DIM, rows), F32)
    zero_sum = jnp.zeros((1, LANES), F32)
    dq, sum_k, sum_v = lax.fori_loop(0, length // block, step, ((zero_q, zero_q), zero_sum, zero_sum))

    dq, dk, dv = fold(dq, kn_ref[...], vn_ref[...], own_mask(low, high, noisy))
    dk = unturn(dk, cos_own_ref[:noisy, :], sin_own_ref[:noisy, :])
    dq = unturn(jnp.concatenate(dq, 0).T * SCALE, cos_own_ref[...], sin_own_ref[...])
    zeros = jnp.zeros((rows - noisy, LANES), BF16)
    for part, grad in enumerate((dq, dk, dv)):
        down_ref[: grad.shape[0], pl.ds(part * width + here, LANES)] = grad.astype(BF16)
        if part > 0:
            down_ref[noisy:, pl.ds(part * width + here, LANES)] = zeros
    sums = (
        jnp.sum(dq, 0, keepdims=True),
        sum_k + jnp.sum(dk, 0, keepdims=True),
        sum_v + jnp.sum(dv, 0, keepdims=True),
    )
    for part in range(3):
        sum_ref[:, pl.ds(part * width + here, LANES)] = jnp.broadcast_to(sums[part], (8, LANES))


def attend_back(scalars, own, s, seqs, clean, attn, grad, log_total, cos_own, sin_own, cos_tab, sin_tab, block):
    rows = own.shape[0] // seqs
    length, both = clean.shape
    pairs = own.shape[1] // (3 * LANES)
    spec = pltpu.PrefetchScalarGridSpec(
        num_scalar_prefetch=1,
        grid=(pairs,),
        in_specs=[
            pl.BlockSpec((rows, LANES), lambda p, c: (s, p)),
            pl.BlockSpec((rows // 2, LANES), lambda p, c: (2 * s, pairs + p)),
            pl.BlockSpec((rows // 2, LANES), lambda p, c: (2 * s, 2 * pairs + p)),
            pl.BlockSpec((length, LANES), lambda p, c: (0, p)),
            pl.BlockSpec((length, LANES), lambda p, c: (0, pairs + p)),
            pl.BlockSpec((rows, LANES), lambda p, c: (0, p)),
            pl.BlockSpec((rows, LANES), lambda p, c: (0, p)),
            pl.BlockSpec((1, 8, rows), lambda p, c: (p, 0, 0)),
            pl.BlockSpec((rows, LANES), lambda p, c: (0, 0)),
            pl.BlockSpec((rows, LANES), lambda p, c: (0, 0)),
            pl.BlockSpec((length, LANES), lambda p, c: (0, 0)),
            pl.BlockSpec((length, LANES), lambda p, c: (0, 0)),
        ],
        out_specs=[
            pl.BlockSpec((length, both), lambda p, c: (0, 0)),
            pl.BlockSpec((rows, own.shape[1]), lambda p, c: (0, 0)),
            pl.BlockSpec((8, own.shape[1]), lambda p, c: (0, 0)),
        ],
    )
    return pl.pallas_call(
        functools.partial(attend_back_kernel, block=block),
        grid_spec=spec,
        out_shape=[
            jax.ShapeDtypeStruct((length, both), BF16),
            jax.ShapeDtypeStruct((rows, own.shape[1]), BF16),
            jax.ShapeDtypeStruct((8, own.shape[1]), F32),
        ],
        compiler_params=pltpu.CompilerParams(vmem_limit_bytes=VMEM_LIMIT),
        cost_estimate=LIGHT,
        name="attend_back",
    )(scalars, own, own, own, clean, clean, attn, grad, log_total, cos_own, sin_own, cos_tab, sin_tab)


def feed_forward_kernel(
    core_ref, attn_ref, x_ref, top_ref, up_ref, down_ref, out_ref, vec_ref,
    block_out_ref, hidden_grad_ref, attn_grad_ref, weights_ref, mine_ref, theirs_ref,
    hidden, unit, inverse, normed, normed_flipped, lowered, grad_normed,
    up_grads, join_grads, down_grads, out_grads, vec_grads, sums, up_sems, join_sems, down_sems, last_sems,
    *, pairs, joined
):
    chunk = pl.program_id(0)
    chunks = pl.num_programs(0)
    width = x_ref.shape[1]

    @pl.when(chunk == 0)
    def _():
        value = (
            x_ref[...].astype(F32)
            + jnp.dot(attn_ref[...], out_ref[...], preferred_element_type=F32)
            + vec_ref[0:1, :]
        )
        hidden[...] = value
        center = value - jnp.mean(value, -1, keepdims=True)
        scale = lax.rsqrt(jnp.mean(center * center, -1, keepdims=True) + EPSILON)
        inverse[...] = scale
        unit[...] = center * scale
        scaled = unit[...] * vec_ref[1:2, :] + vec_ref[2:3, :]
        normed[...] = scaled.astype(BF16)
        normed_flipped[...] = scaled.T.astype(BF16)
        lowered[...] = jnp.zeros_like(lowered)
        grad_normed[...] = jnp.zeros_like(grad_normed)
        sums[...] = jnp.zeros_like(sums)

    upper = jnp.dot(normed[...], up_ref[...], preferred_element_type=F32) + vec_ref[pl.ds(4 + chunk, 1), :]
    grad_activ = nt_dot(top_ref[...], down_ref[...])
    square = upper * upper
    half = 0.5 + 0.5 * jnp.tanh(upper * (0.7978845608028654 + 0.035677408136300125 * square))
    activ = upper * half
    slope = half + activ * (1.0 - half) * (1.5957691216057308 + 0.21406444881780075 * square)
    grad_upper = grad_activ * slope
    grad_low = grad_upper.astype(BF16)
    sums[pl.ds(4 + chunk, 1), :] = jnp.sum(grad_upper, 0, keepdims=True)
    lowered[...] += jnp.dot(activ.astype(BF16), down_ref[...], preferred_element_type=F32)
    grad_normed[...] += nt_dot(grad_low, up_ref[...])
    up_grads[chunk] = jnp.dot(normed_flipped[...], grad_low, preferred_element_type=F32).astype(BF16)
    down_grad = jnp.dot(activ.T.astype(BF16), top_ref[...], preferred_element_type=F32).astype(BF16)
    shard = width // (2 * pairs)

    @pl.when(chunk < joined)
    def _():
        join_grads[chunk] = down_grad

    @pl.when(chunk >= joined)
    def _():
        for pair in range(pairs):
            for core in range(2):
                first = (2 * pair + core) * shard
                down_grads[chunk - joined, core, pair * shard : (pair + 1) * shard, :] = down_grad[first : first + shard]

    def copy_up(index):
        columns = pl.ds(pl.multiple_of(index * width, width), width)
        return pltpu.make_async_copy(up_grads.at[index], weights_ref.at[:, columns], up_sems.at[index])

    def copy_join(index):
        columns = pl.ds(pl.multiple_of((chunks + index) * width, width), width)
        return pltpu.make_async_copy(join_grads.at[index], weights_ref.at[:, columns], join_sems.at[index])

    def copy_down(index):
        columns = pl.ds(pl.multiple_of(index * width, width), width)
        core = core_ref[0]
        return (
            pltpu.make_async_copy(down_grads.at[index, core], mine_ref.at[:, columns], down_sems.at[0, index]),
            pltpu.make_async_copy(down_grads.at[index, 1 - core], theirs_ref.at[:, columns], down_sems.at[1, index]),
        )

    copy_up(chunk).start()

    @pl.when(chunk < joined)
    def _():
        copy_join(chunk).start()

    @pl.when(chunk >= joined)
    def _():
        for copy in copy_down(chunk - joined):
            copy.start()

    @pl.when(chunk == chunks - 1)
    def _():
        top = top_ref[...].astype(F32)
        block_out_ref[...] = (hidden[...] + lowered[...] + vec_ref[3:4, :]).astype(BF16)
        grad = grad_normed[...]
        rows_unit = unit[...]
        sums[1:2, :] = jnp.sum(grad * rows_unit, 0, keepdims=True)
        sums[2:3, :] = jnp.sum(grad, 0, keepdims=True)
        sums[3:4, :] = jnp.sum(top, 0, keepdims=True)
        grad = grad * vec_ref[1:2, :]
        grad = inverse[...] * (
            grad - jnp.mean(grad, -1, keepdims=True) - rows_unit * jnp.mean(grad * rows_unit, -1, keepdims=True)
        )
        grad = top + grad
        hidden_grad_ref[...] = grad
        sums[0:1, :] = jnp.sum(grad, 0, keepdims=True)
        low = grad.astype(BF16)
        attn_grad_ref[...] = nt_dot(low, out_ref[...]).astype(BF16)
        out_grads[...] = jnp.dot(
            attn_ref[...].astype(F32).T.astype(BF16), low, preferred_element_type=F32
        ).astype(BF16)
        vec_grads[...] = sums[...].T.astype(BF16)
        first = (chunks + joined) * width
        copies = [
            pltpu.make_async_copy(out_grads, weights_ref.at[:, pl.ds(first, width)], last_sems.at[0]),
            pltpu.make_async_copy(vec_grads, weights_ref.at[:, pl.ds(first + width, LANES)], last_sems.at[1]),
        ]
        for copy in copies:
            copy.start()
        for index in range(up_grads.shape[0]):
            copy_up(index).wait()
        for index in range(joined):
            copy_join(index).wait()
        for index in range(down_grads.shape[0]):
            for copy in copy_down(index):
                copy.wait()
        for copy in copies:
            copy.wait()


def feed_forward(core, attn, x, top, weights, vectors, chunks, pairs, joined):
    rows, width = x.shape
    apart = chunks - joined
    fixed = lambda b, c: (0, 0)
    whole = pl.BlockSpec((rows, width), fixed)
    spec = pltpu.PrefetchScalarGridSpec(
        num_scalar_prefetch=1,
        grid=(chunks,),
        in_specs=[
            whole,
            whole,
            whole,
            pl.BlockSpec((width, width), lambda b, c: (0, b)),
            pl.BlockSpec((width, width), lambda b, c: (0, chunks + b)),
            pl.BlockSpec((width, width), lambda b, c: (0, 2 * chunks)),
            pl.BlockSpec(vectors.shape, fixed),
        ],
        out_specs=[whole, whole, whole] + [pl.BlockSpec(memory_space=pl.ANY)] * 3,
        scratch_shapes=[
            pltpu.VMEM((rows, width), F32),
            pltpu.VMEM((rows, width), F32),
            pltpu.VMEM((rows, 1), F32),
            pltpu.VMEM((rows, width), BF16),
            pltpu.VMEM((width, rows), BF16),
            pltpu.VMEM((rows, width), F32),
            pltpu.VMEM((rows, width), F32),
            pltpu.VMEM((chunks, width, width), BF16),
            pltpu.VMEM((joined, width, width), BF16),
            pltpu.VMEM((apart, 2, width // 2, width), BF16),
            pltpu.VMEM((width, width), BF16),
            pltpu.VMEM((width, LANES), BF16),
            pltpu.VMEM((LANES, width), F32),
            pltpu.SemaphoreType.DMA((chunks,)),
            pltpu.SemaphoreType.DMA((joined,)),
            pltpu.SemaphoreType.DMA((2, apart)),
            pltpu.SemaphoreType.DMA((2,)),
        ],
    )
    return pl.pallas_call(
        functools.partial(feed_forward_kernel, pairs=pairs, joined=joined),
        grid_spec=spec,
        out_shape=[
            jax.ShapeDtypeStruct((rows, width), BF16),
            jax.ShapeDtypeStruct((rows, width), F32),
            jax.ShapeDtypeStruct((rows, width), BF16),
            jax.ShapeDtypeStruct((width, weights.shape[1] - apart * width), BF16),
            jax.ShapeDtypeStruct((width // 2, apart * width), BF16),
            jax.ShapeDtypeStruct((width // 2, apart * width), BF16),
        ],
        compiler_params=pltpu.CompilerParams(vmem_limit_bytes=VMEM_LIMIT),
        cost_estimate=LIGHT,
        name="feed_forward",
    )(core.reshape(1), attn, x, top, weights, weights, weights, vectors)


def after(value, *others):
    return lax.optimization_barrier((value,) + others)[0]


def pick(array, index, axis=0):
    return lax.dynamic_index_in_dim(array, index, axis, keepdims=False)


def ordered(flag, own, other, axis):
    return jnp.stack([jnp.where(flag == 0, own, other), jnp.where(flag == 0, other, own)], axis)


class Links:
    def __init__(self):
        self.count = lax.axis_size("ctx")
        self.deep = self.count // 4
        at = lax.axis_index("ctx")
        self.x = lax.axis_index("batch")
        self.core = at % 2
        self.y = (at // 2) % 2
        self.z = at // 4
        self.chip = at // 2

    def over_core(self, array):
        return lax.ppermute(array, "ctx", [(i, i ^ 1) for i in range(self.count)])

    def over_y(self, array):
        return lax.ppermute(array, "ctx", [(i, i ^ 2) for i in range(self.count)])

    def over_x(self, array):
        return lax.ppermute(array, "batch", [(0, 1), (1, 0)])

    def along_z(self, array, hop):
        count = self.count
        return lax.ppermute(array, "ctx", [(i, (i + 4 * hop) % count) for i in range(count)])

    def around_z(self, piece):
        return [self.along_z(piece, hop) for hop in range(1, self.deep)]

    def column(self, piece, others):
        deep = self.deep
        whole = jnp.broadcast_to(piece[None], (deep,) + piece.shape)
        for hop, other in enumerate(others, 1):
            whole = lax.dynamic_update_index_in_dim(whole, other, (self.z - hop) % deep, 0)
        return whole

    def swap_z(self, parts):
        return [self.along_z(pick(parts, (self.z + hop) % self.deep), hop) for hop in range(1, self.deep)]

    def sum_z(self, parts, others):
        total = pick(parts, self.z).astype(F32)
        for other in others:
            total = total + other.astype(F32)
        return total


def unit_rows(values):
    center = values - jnp.mean(values, -1, keepdims=True)
    spread = jnp.mean(center * center, -1, keepdims=True)
    inverse = lax.rsqrt(spread + EPSILON)
    return center * inverse, inverse


def unit_back(grad, unit, inverse):
    return inverse * (
        grad - jnp.mean(grad, -1, keepdims=True) - unit * jnp.mean(grad * unit, -1, keepdims=True)
    )


def rotary_tables(positions):
    half_dim = HEAD_DIM // 2
    inverse = 1.0 / THETA ** (jnp.arange(half_dim, dtype=F32) / half_dim)
    angles = positions.astype(F32)[:, None] * jnp.tile(inverse, LANES // half_dim)[None, :]
    sign = jnp.where(jnp.arange(LANES) % HEAD_DIM < half_dim, -1.0, 1.0)
    return jnp.cos(angles), jnp.sin(angles) * sign[None, :]


def key_block(length, limit):
    sizes = [size for size in range(16, limit + 1, 16) if length % size == 0]
    return sizes[-1] if sizes else length


def row_block(rows):
    for block in (512, 384, 256, 128, 64, 32, 16):
        if rows % block == 0:
            return block
    return rows


def dot(a, b):
    return jnp.dot(a, b, preferred_element_type=F32)


def dot_left(a, b):
    return lax.dot_general(a, b, (((0,), (0,)), ((), ())), preferred_element_type=F32)


def on_device(
    layer_input, cotangent, prefix, block_size, ln1_gain, ln1_bias, qkv_weight, qkv_bias, out_weight, out_bias,
    ln2_gain, ln2_bias, up_weight, up_bias, down_weight, down_bias,
):
    links = Links()
    core = links.core
    seqs, _, pos_dev, width = layer_input.shape
    devices = 2 * links.count
    length = links.count * pos_dev
    half = width // 2
    rows = 4 * pos_dev
    shard = ln1_gain.shape[0]
    hidden_shard = up_bias.shape[0]

    split = qkv_weight.reshape(shard, 3, 2, half)
    vec_one = jnp.concatenate([ln1_gain, ln1_bias, qkv_bias])
    vec_one = ordered(core, vec_one, links.over_core(vec_one), 0).reshape(1, -1)
    vec_one = jnp.pad(vec_one, ((0, 7), (0, width - vec_one.shape[1])))
    qkv_piece = ordered(core, pick(split, core, 2), links.over_core(pick(split, 1 - core, 2)), 0)
    qkv_piece = qkv_piece.reshape(2 * shard, 3 * half)
    cos_tab, sin_tab = rotary_tables(after(jnp.arange(length, dtype=jnp.int32), qkv_piece))
    first_pos = links.chip * 2 * pos_dev
    cos_own = jnp.tile(lax.dynamic_slice_in_dim(cos_tab, first_pos, 2 * pos_dev, 0), (2, 1))
    sin_own = jnp.tile(lax.dynamic_slice_in_dim(sin_tab, first_pos, 2 * pos_dev, 0), (2, 1))
    block = key_block(length, 1536)
    scalars = [jnp.stack([prefix[s], block_size[s], first_pos]) for s in range(seqs)]
    qkv_others = links.around_z(qkv_piece)
    inputs_got = links.over_core(layer_input)
    qkv_column = jnp.stack([qkv_piece] + qkv_others)
    qkv_got = links.over_y(qkv_column)
    qkv_far = links.over_x(qkv_column)
    clean_piece = jnp.concatenate([layer_input[0, 1], vec_one])
    clean_piece = after(clean_piece, cos_tab, sin_tab, inputs_got, *qkv_others)
    clean_others = links.around_z(clean_piece)
    gate = (qkv_got, qkv_far) + tuple(clean_others)
    weights_gate = gate
    qkv_last = links.over_x(after(qkv_got, *gate))
    hops = jnp.arange(links.deep, dtype=jnp.int32)
    levels = (links.z - hops) % links.deep
    arrived = []
    for s in range(seqs):
        column = after(jnp.stack([clean_piece] + clean_others), *gate)
        got = links.over_y(column)
        gate = (got,)
        if s + 1 < seqs:
            clean_piece = after(layer_input[s + 1, 1], column)
            clean_others = links.around_z(clean_piece)
            gate = gate + tuple(clean_others)
        if s == 0:
            vec_near = jnp.stack([column[:, pos_dev], got[:, pos_dev]])
            vec_far = links.over_x(after(vec_near, *gate[1:]))
            gate = gate + (qkv_last,)
        arrived.append((column, got, links.over_core(column)))
    where = jnp.concatenate(
        [(x * links.deep + levels) * 2 + y for x in (links.x, 1 - links.x) for y in (links.y, 1 - links.y)]
    )
    qkv_mat = place([qkv_column, qkv_got, qkv_far, qkv_last], where, 2 * shard)
    vec_one = jnp.concatenate([vec_near, vec_far]).reshape(where.shape[0], width).astype(F32)
    turn = (where[None, :] == jnp.arange(where.shape[0], dtype=jnp.int32)[:, None]).astype(F32)
    vec_one = jnp.dot(turn, vec_one[:, : 2 * (2 * shard + qkv_bias.shape[0])], precision=lax.Precision.HIGHEST)
    vec_one = vec_one.reshape(devices, -1)
    gain_one = vec_one[:, :shard].reshape(1, width)
    bias_one = vec_one[:, shard : 2 * shard].reshape(1, width)
    qkv_add = pick(vec_one[:, 2 * shard :].reshape(3, 2, half), core, 1).reshape(1, 3 * half)

    folds = hidden_shard // shard
    up_piece = up_weight.reshape(shard, devices, folds, shard).transpose(0, 2, 1, 3).reshape(shard, -1)
    down_piece = down_weight.reshape(folds, shard, width).transpose(1, 0, 2).reshape(shard, -1)
    vec_piece = jnp.stack(
        [out_bias, ln2_gain, ln2_bias, down_bias] + [up_bias[i * shard : (i + 1) * shard] for i in range(folds)], 1
    )
    vec_piece = jnp.pad(vec_piece, ((0, 0), (0, LANES - vec_piece.shape[1])))
    packed = after(jnp.concatenate([up_piece, down_piece, out_weight, vec_piece], 1), *weights_gate)
    weights = lax.all_gather(packed, ("batch", "ctx"), axis=0, tiled=True)
    vectors = weights[:, -LANES:].T[: 4 + folds].astype(F32)

    inputs_pair = ordered(core, layer_input, inputs_got, 2).reshape(seqs, rows, width)

    own_qkv, own_unit = project(
        inputs_pair.reshape(seqs * rows, width), gain_one, bias_one, qkv_mat, qkv_add,
        cos_own, sin_own, 0, width, row_block(rows),
    )
    clean_kv, clean_unit, attn_list, log_list = ([] for _ in range(4))
    for s in range(seqs):
        column, got, column_far = arrived[s]
        got = after(got, *([clean_kv[-1]] if s else [own_qkv]))
        where = jnp.stack([links.z] + [y * 2 + c for c in (core, 1 - core) for y in (links.y, 1 - links.y)])
        clean, all_unit = project_parts(
            where, [column, got, column_far, links.over_core(got)], pos_dev,
            gain_one, bias_one, qkv_mat, qkv_add, cos_tab, sin_tab, half, half,
        )
        attn, log_total = attend(scalars[s], own_qkv, s, seqs, clean, block)
        for kept, value in zip(
            (clean_kv, clean_unit, attn_list, log_list),
            (clean, all_unit, attn, log_total),
        ):
            kept.append(value)

    attn_rows = jnp.stack(attn_list).reshape(seqs, 2, 2, pos_dev, half)
    attn_got = links.over_core(pick(attn_rows, 1 - core, 2))
    attn_low = ordered(core, pick(attn_rows, core, 2), attn_got, 3).reshape(-1, width)
    flat_inputs = layer_input.reshape(-1, width)
    joined = folds * 3 // 4
    apart = folds - joined
    output, grad_hidden, grad_attn, weight_grads, down_mine, down_theirs = feed_forward(
        core, attn_low, flat_inputs, cotangent.reshape(-1, width), weights, vectors, folds, links.count, joined
    )
    output = output.reshape(layer_input.shape)
    packed = lax.psum_scatter(weight_grads, ("batch", "ctx"), scatter_dimension=0, tiled=True)
    down_got = links.over_core(down_theirs)
    down_part = (down_mine.astype(F32) + down_got.astype(F32)).astype(BF16)
    down_part = down_part.reshape(2, links.deep, 2, shard * apart, width)
    down_sent = pick(down_part, 1 - links.x)
    down_got = links.over_x(down_sent)

    grad_split = grad_attn.reshape(-1, 2, half)
    grad_got = links.over_core(pick(grad_split, 1 - core, 1))
    grad_rows = ordered(
        core,
        pick(grad_split, core, 1).reshape(seqs, 2, pos_dev, half),
        grad_got.reshape(seqs, 2, pos_dev, half),
        2,
    ).reshape(seqs, rows, half)
    kv_mat = qkv_mat[:, half:]
    own_unit = own_unit.reshape(seqs, rows, width)
    unit_part = jnp.zeros((width, 3 * half), F32)
    kv_part = jnp.zeros((width, 2 * half), F32)
    column_sums = 0.0
    waiting, gate = [], ()
    for s in range(seqs):
        clean_grad, own_grad, sums = attend_back(
            scalars[s], own_qkv, s, seqs, clean_kv[s], attn_list[s], after(grad_rows[s], *gate),
            log_list[s], cos_own, sin_own, cos_tab, sin_tab, block,
        )
        spread = lax.dot_general(clean_grad, kv_mat, NT, preferred_element_type=F32).astype(BF16)
        local = lax.dot_general(own_grad, qkv_mat, NT, preferred_element_type=F32).astype(BF16)
        spread = spread.reshape(2 * links.deep, 2, pos_dev, width)
        local = local.reshape(2, 2, pos_dev, width)
        theirs = jnp.concatenate([pick(spread, 1 - core, 1), pick(local, 1 - core, 1)])
        got = links.over_core(theirs)
        gate = (theirs,)
        if s == seqs - 1:
            down_got = after(down_got, own_grad)
            down_part = (pick(down_part, links.x).astype(F32) + down_got.astype(F32)).astype(BF16)
            down_sent = pick(down_part, 1 - links.y, 1)
            down_got = links.over_y(down_sent)
            gate = (theirs, down_sent)
        unit_part = unit_part + dot_left(own_unit[s], after(own_grad, *gate))
        kv_part = kv_part + dot_left(clean_unit[s], after(clean_grad, *gate))
        column_sums = column_sums + sums[0]
        if s == seqs - 1:
            qkv_part = (unit_part + jnp.pad(kv_part, ((0, 0), (half, 0)))).astype(BF16)
            qkv_part = qkv_part.reshape(2, links.deep, 2, 2 * shard, 3 * half)
            far_part = pick(qkv_part, 1 - links.x)
            qkv_far = links.over_x(far_part)
        mine = pick(spread, core, 1).astype(F32) + got[: 2 * links.deep].astype(F32)
        mine = mine.astype(BF16).reshape(links.deep, 2, pos_dev, width)
        local = pick(local, core, 1).astype(F32) + got[2 * links.deep :].astype(F32)
        if s == seqs - 1:
            below = jnp.pad(column_sums, (0, 8 * width - 3 * half)).astype(BF16).reshape(1, 1, 8, width)
            mine = jnp.concatenate([mine, jnp.broadcast_to(below, (links.deep, 2, 8, width))], 2)
        theirs = pick(mine, 1 - links.y, 1)
        row_got = links.over_y(theirs)
        waiting.append((mine, local, row_got))
        gate = (theirs, down_sent)
    down_part = pick(after(down_part, far_part), links.y, 1).astype(F32)
    down_part = (down_part + down_got.astype(F32)).astype(BF16)
    summed = []
    for mine, _, row_got in waiting:
        mine = (pick(mine, links.y, 1).astype(F32) + after(row_got, far_part).astype(F32)).astype(BF16)
        summed.append(mine)
    first = jnp.concatenate(summed[:-1] + [down_part], 1)
    first_others = links.swap_z(first)
    others = links.swap_z(summed[-1])
    total = links.sum_z(summed[-1], others)
    first_others = after(tuple(first_others), summed[-1])
    first = links.sum_z(first, first_others)
    own_rows = [
        jnp.stack([local[0], local[1] + (first[s * pos_dev : (s + 1) * pos_dev] if s < seqs - 1 else total[:pos_dev])])
        for s, (_, local, _) in enumerate(waiting)
    ]
    down_sum = first[(seqs - 1) * pos_dev :]
    column_sums = total[pos_dev:].reshape(-1)[: 3 * half].reshape(3, half)
    column_sums = column_sums + links.over_x(column_sums)
    column_sums = ordered(core, column_sums, links.over_core(column_sums), 1).reshape(3 * width)

    grad_normed_one = jnp.stack(own_rows).reshape(-1, width)
    unit_one, inverse_one = unit_rows(after(flat_inputs, far_part).astype(F32))
    grad_input = grad_hidden + unit_back(grad_normed_one * gain_one, unit_one, inverse_one)
    grad_input = grad_input.astype(BF16).reshape(layer_input.shape)

    qkv_part = (pick(after(qkv_part, packed), links.x).astype(F32) + qkv_far.astype(F32)).astype(BF16)
    qkv_far = links.over_y(after(pick(qkv_part, 1 - links.y, 1), waiting[-1][2]))
    qkv_part = (pick(qkv_part, links.y, 1).astype(F32) + qkv_far.astype(F32)).astype(BF16)
    qkv_part = after(qkv_part, summed[-1])
    qkv_sum = links.sum_z(qkv_part, links.swap_z(qkv_part)).reshape(2, shard, 3, half)
    qkv_got = links.over_core(pick(qkv_sum, 1 - core))
    qkv_sum = ordered(core, pick(qkv_sum, core), qkv_got, 2).reshape(shard, 3 * width)
    grad_qkv = ln1_gain.astype(F32)[:, None] * qkv_sum + ln1_bias.astype(F32)[:, None] * column_sums[None, :]
    own_weight = qkv_weight.astype(F32)
    grad_gain_one = jnp.sum(own_weight * qkv_sum, -1)
    grad_bias_one = jnp.sum(own_weight * column_sums[None, :], -1)
    device = links.x * links.count + lax.axis_index("ctx")
    grad_qk_bias = lax.dynamic_slice_in_dim(column_sums[: 2 * width], device * 2 * shard, 2 * shard, 0)
    grad_value_bias = lax.dynamic_slice_in_dim(column_sums[2 * width :], device * shard, shard, 0)

    hidden_width = devices * hidden_shard
    packed = packed.astype(F32)
    grad_up = packed[:, :hidden_width].reshape(shard, folds, devices, shard).transpose(0, 2, 1, 3)
    grad_up = grad_up.reshape(shard, hidden_width)
    first_down = packed[:, hidden_width : hidden_width + joined * width].reshape(shard, joined, width)
    grad_down = jnp.concatenate([first_down, down_sum.reshape(shard, apart, width)], 1)
    grad_down = grad_down.transpose(1, 0, 2).reshape(hidden_shard, width)
    grad_out = packed[:, hidden_width + joined * width : -LANES]
    late = packed[:, -LANES:].T

    return (
        output, grad_input, grad_gain_one, grad_bias_one, grad_qkv, grad_qk_bias, grad_value_bias, grad_out,
        late[0], late[1], late[2], grad_up, late[4 : 4 + folds].reshape(-1), grad_down, late[3],
    )


def solution(mesh):
    every = P(("batch", "ctx"))
    matrix = P(("batch", "ctx"), None)
    acts = P("batch", None, "ctx", None)
    return jax.shard_map(
        on_device,
        mesh=mesh,
        in_specs=(
            acts, acts, P("batch"), P("batch"), every, every, matrix, every, matrix, every, every, every, matrix,
            every, matrix, every,
        ),
        out_specs=(
            acts, acts, every, every, matrix, every, every, matrix, every, every, every, matrix, every, matrix, every,
        ),
        check_vma=False,
    )
```

```python
import functools

import jax
import jax.numpy as jnp
from jax import lax
from jax.experimental import pallas as pl
from jax.experimental.pallas import tpu as pltpu
from jax.sharding import PartitionSpec as P

HEADS = 12
HEAD_DIM = 64
SCALE = 0.125
NEGATIVE = -1e30
EPSILON = 1e-05
THETA = 10000.0
LANES = 128
BF16 = jnp.bfloat16
F32 = jnp.float32
VMEM_LIMIT = 56 * 1024 * 1024
NT = (((1,), (1,)), ((), ()))
LIGHT = pl.CostEstimate(flops=1, bytes_accessed=1, transcendentals=0)


def swap_halves(tile):
    lane = lax.broadcasted_iota(jnp.int32, tile.shape, 1)
    return jnp.where(lane % 64 < 32, pltpu.roll(tile, LANES - 32, 1), pltpu.roll(tile, 32, 1))


def project_rows(x, gain_ref, bias_ref, w_ref, add_ref, cos_ref, sin_ref, out_ref, unit_ref, start, turned):
    x = x.astype(F32)
    center = x - jnp.mean(x, -1, keepdims=True)
    spread = jnp.mean(center * center, -1, keepdims=True)
    unit = center * lax.rsqrt(spread + EPSILON)
    unit_ref[...] = unit.astype(BF16)
    normed = (unit * gain_ref[...] + bias_ref[...]).astype(BF16)
    cos_tab, sin_tab = cos_ref[...], sin_ref[...]
    total = jnp.dot(normed, w_ref[:, start:], preferred_element_type=F32) + add_ref[:, start:]
    for tile in range(total.shape[1] // LANES):
        part = total[:, tile * LANES : (tile + 1) * LANES]
        if tile * LANES < turned:
            part = part * cos_tab + swap_halves(part) * sin_tab
        out_ref[:, tile * LANES : (tile + 1) * LANES] = part.astype(BF16)


def project_kernel(x_ref, *refs, start, turned):
    project_rows(x_ref[...], *refs, start, turned)


def project_parts_kernel(where_ref, a_ref, b_ref, c_ref, d_ref, *refs, start, turned):
    *refs, rows_ref = refs
    rows = rows_ref.shape[0] // 4
    for index, part in enumerate((a_ref, b_ref, c_ref, d_ref)):
        first = pl.multiple_of(where_ref[1 + index] * rows, rows)
        rows_ref[pl.ds(first, rows), :] = part[0, :rows, :]
    project_rows(rows_ref[...], *refs, start, turned)


def project_parts(where, parts, rows, gain, bias, weight, add, cos_tab, sin_tab, start, turned):
    deep, _, width = parts[0].shape
    columns = weight.shape[1] - start
    block = 4 * rows
    row_map = lambda i, w: (i, 0)
    fixed = lambda i, w: (0, 0)
    spec = pltpu.PrefetchScalarGridSpec(
        num_scalar_prefetch=1,
        grid=(deep,),
        in_specs=[
            pl.BlockSpec((1,) + part.shape[1:], lambda i, w: (lax.rem(w[0] - i + deep, deep), 0, 0)) for part in parts
        ]
        + [
            pl.BlockSpec((1, width), fixed),
            pl.BlockSpec((1, width), fixed),
            pl.BlockSpec(weight.shape, fixed),
            pl.BlockSpec((1, weight.shape[1]), fixed),
            pl.BlockSpec((block, LANES), row_map),
            pl.BlockSpec((block, LANES), row_map),
        ],
        out_specs=[pl.BlockSpec((block, columns), row_map), pl.BlockSpec((block, width), row_map)],
        scratch_shapes=[pltpu.VMEM((block, width), BF16)],
    )
    return pl.pallas_call(
        functools.partial(project_parts_kernel, start=start, turned=turned),
        grid_spec=spec,
        out_shape=[
            jax.ShapeDtypeStruct((deep * block, columns), BF16),
            jax.ShapeDtypeStruct((deep * block, width), BF16),
        ],
        compiler_params=pltpu.CompilerParams(vmem_limit_bytes=VMEM_LIMIT),
        cost_estimate=LIGHT,
        name="project_parts",
    )(where, *parts, gain, bias, weight, add, cos_tab, sin_tab)


def project(x, gain, bias, weight, add, cos_tab, sin_tab, start, turned, block):
    table_blocks = cos_tab.shape[0] // block
    rows, width = x.shape
    columns = weight.shape[1] - start
    row_map = lambda i: (i, 0)
    fixed = lambda i: (0, 0)
    return pl.pallas_call(
        functools.partial(project_kernel, start=start, turned=turned),
        grid=(rows // block,),
        in_specs=[
            pl.BlockSpec((block, width), row_map),
            pl.BlockSpec((1, width), fixed),
            pl.BlockSpec((1, width), fixed),
            pl.BlockSpec(weight.shape, fixed),
            pl.BlockSpec((1, weight.shape[1]), fixed),
            pl.BlockSpec((block, LANES), lambda i: (i % table_blocks, 0)),
            pl.BlockSpec((block, LANES), lambda i: (i % table_blocks, 0)),
        ],
        out_specs=[pl.BlockSpec((block, columns), row_map), pl.BlockSpec((block, width), row_map)],
        out_shape=[jax.ShapeDtypeStruct((rows, columns), BF16), jax.ShapeDtypeStruct((rows, width), BF16)],
        compiler_params=pltpu.CompilerParams(vmem_limit_bytes=VMEM_LIMIT),
        cost_estimate=LIGHT,
        name="project",
    )(x, gain, bias, weight, add, cos_tab, sin_tab)


def place_kernel(where_ref, *refs, rows):
    *sources, out_ref = refs
    deep = sources[0].shape[0]
    for index in range(len(sources) * deep):
        first = pl.multiple_of(where_ref[index] * rows, rows)
        out_ref[pl.ds(first, rows), :] = sources[index // deep][index % deep, :rows, :]


def place(sources, where, rows):
    deep, _, width = sources[0].shape
    blocks = len(sources) * deep
    if rows % 16:
        out = jnp.concatenate([source[:, :rows] for source in sources])
        for index in range(blocks):
            block = sources[index // deep][index % deep, :rows]
            out = lax.dynamic_update_index_in_dim(out, block, where[index], 0)
        return out.reshape(blocks * rows, width)
    spec = pltpu.PrefetchScalarGridSpec(
        num_scalar_prefetch=1,
        grid=(1,),
        in_specs=[pl.BlockSpec(source.shape, lambda i, w: (0, 0, 0)) for source in sources],
        out_specs=pl.BlockSpec((blocks * rows, width), lambda i, w: (0, 0)),
    )
    return pl.pallas_call(
        functools.partial(place_kernel, rows=rows),
        grid_spec=spec,
        out_shape=jax.ShapeDtypeStruct((blocks * rows, width), sources[0].dtype),
        compiler_params=pltpu.CompilerParams(vmem_limit_bytes=VMEM_LIMIT),
        cost_estimate=LIGHT,
        name="place",
    )(where, *sources)


def head_parts(rows, factor):
    rows = rows.astype(F32) * factor
    lane = lax.broadcasted_iota(jnp.int32, rows.shape, 1)
    first = lane < HEAD_DIM
    return (jnp.where(first, rows, 0.0).astype(BF16), jnp.where(first, 0.0, rows).astype(BF16))


def flipped(tile):
    return tile.astype(F32).T.astype(BF16)


def nt_dot(a, b):
    return lax.dot_general(a, b, NT, preferred_element_type=F32)


def sight(scalars_ref, rows):
    prefix, size, first = scalars_ref[0], scalars_ref[1], scalars_ref[2]
    row = lax.broadcasted_iota(jnp.int32, (1, rows), 1)
    noisy = row < rows // 2
    position = first + jnp.where(noisy, row, row - rows // 2)
    near = jnp.floor((position.astype(F32) + 0.5) / size.astype(F32)).astype(jnp.int32) * size
    clean_limit = jnp.where(position < prefix, prefix, near + size)
    limit = jnp.where(noisy, jnp.maximum(near, prefix), clean_limit)
    low = near - first
    return limit, low, jnp.where(noisy, low + size, low)


def own_mask(low, high, noisy_rows):
    at = lax.broadcasted_iota(jnp.int32, (noisy_rows, low.shape[1]), 0)
    return (at >= low) & (at < high)


def attend_kernel(scalars_ref, q_ref, kn_ref, vn_ref, kc_ref, vc_ref, o_ref, log_ref, *, block):
    rows = q_ref.shape[0]
    queries = head_parts(q_ref[...], SCALE)
    limit, low, high = sight(scalars_ref, rows)

    def fold(state, parts):
        values = [flipped(part_values) for _, part_values, _ in parts]
        out = []
        for h in range(2):
            best, total, acc = state[h]
            heads = slice(h * HEAD_DIM, (h + 1) * HEAD_DIM)
            scores = [jnp.where(mask, nt_dot(keys, queries[h]), NEGATIVE) for keys, _, mask in parts]
            tops = [jnp.max(part, 0, keepdims=True) for part in scores]
            new_best = functools.reduce(jnp.maximum, tops, best)
            factor = jnp.exp(best - new_best)
            total = total * factor
            acc = acc * factor
            for part, part_values in zip(scores, values):
                weights = jnp.exp(part - new_best)
                total = total + jnp.sum(weights, 0, keepdims=True)
                acc = acc + jnp.dot(part_values[heads], weights.astype(BF16), preferred_element_type=F32)
            out.append((new_best, total, acc))
        return tuple(out)

    def clean_parts(index):
        parts = []
        for offset in range(0, block, piece):
            first = index * block + offset
            at = lax.broadcasted_iota(jnp.int32, (piece, rows), 0) + first
            if not isinstance(first, int):
                first = pl.multiple_of(first, piece)
            parts.append((kc_ref[pl.ds(first, piece), :], vc_ref[pl.ds(first, piece), :], at < limit))
        return parts

    piece = key_block(block, 512)
    own_part = (kn_ref[...], vn_ref[...], own_mask(low, high, kn_ref.shape[0]))
    start = (
        jnp.full((1, rows), NEGATIVE, F32),
        jnp.zeros((1, rows), F32),
        jnp.zeros((HEAD_DIM, rows), F32),
    )
    if block == kc_ref.shape[0]:
        state = fold((start, start), clean_parts(0) + [own_part])
    else:
        state = lax.fori_loop(0, kc_ref.shape[0] // block, lambda i, state: fold(state, clean_parts(i)), (start, start))
        state = fold(state, [own_part])
    o_ref[...] = jnp.concatenate([acc / total for _, total, acc in state], 0).T.astype(BF16)
    for h in range(2):
        log_ref[0, h : h + 1, :] = state[h][0] + jnp.log(state[h][1])


def attend(scalars, own, s, seqs, clean, block):
    rows = own.shape[0] // seqs
    length = clean.shape[0]
    pairs = own.shape[1] // (3 * LANES)
    spec = pltpu.PrefetchScalarGridSpec(
        num_scalar_prefetch=1,
        grid=(pairs,),
        in_specs=[
            pl.BlockSpec((rows, LANES), lambda p, c: (s, p)),
            pl.BlockSpec((rows // 2, LANES), lambda p, c: (2 * s, pairs + p)),
            pl.BlockSpec((rows // 2, LANES), lambda p, c: (2 * s, 2 * pairs + p)),
            pl.BlockSpec((length, LANES), lambda p, c: (0, p)),
            pl.BlockSpec((length, LANES), lambda p, c: (0, pairs + p)),
        ],
        out_specs=[
            pl.BlockSpec((rows, LANES), lambda p, c: (0, p)),
            pl.BlockSpec((1, 8, rows), lambda p, c: (p, 0, 0)),
        ],
    )
    return pl.pallas_call(
        functools.partial(attend_kernel, block=block),
        grid_spec=spec,
        out_shape=[
            jax.ShapeDtypeStruct((rows, pairs * LANES), BF16),
            jax.ShapeDtypeStruct((pairs, 8, rows), F32),
        ],
        compiler_params=pltpu.CompilerParams(vmem_limit_bytes=VMEM_LIMIT),
        cost_estimate=LIGHT,
        name="attend",
    )(scalars, own, own, own, clean, clean)


def attend_back_kernel(
    scalars_ref, q_ref, kn_ref, vn_ref, kc_ref, vc_ref, o_ref, do_ref, log_ref,
    cos_own_ref, sin_own_ref, cos_ref, sin_ref, dkv_ref, down_ref, sum_ref, *, block
):
    rows = q_ref.shape[0]
    noisy = kn_ref.shape[0]
    width = dkv_ref.shape[1] // 2
    length = kc_ref.shape[0]
    here = pl.multiple_of(pl.program_id(0) * LANES, LANES)
    queries = head_parts(q_ref[...], SCALE)
    grads = head_parts(do_ref[...], 1.0)
    limit, low, high = sight(scalars_ref, rows)
    product = do_ref[...].astype(F32) * o_ref[...].astype(F32)
    lane = lax.broadcasted_iota(jnp.int32, (8, LANES), 1)
    deltas = []
    for h in range(2):
        ones = jnp.where((lane < HEAD_DIM) == (h == 0), 1.0, 0.0)
        deltas.append(
            lax.dot_general(ones, product, NT, precision=lax.Precision.HIGHEST, preferred_element_type=F32)[0:1]
        )

    def fold(dq, keys, values, mask):
        keys_flipped = flipped(keys)
        dk = dv = None
        out = []
        for h in range(2):
            scores = nt_dot(keys, queries[h])
            probs = jnp.where(mask, jnp.exp(scores - log_ref[0, h : h + 1, :]), 0.0)
            inner = nt_dot(values, grads[h])
            slopes = (probs * (inner - deltas[h])).astype(BF16)
            dv_new = jnp.dot(probs.astype(BF16), grads[h], preferred_element_type=F32)
            dk_new = jnp.dot(slopes, queries[h], preferred_element_type=F32)
            dv = dv_new if dv is None else dv + dv_new
            dk = dk_new if dk is None else dk + dk_new
            out.append(
                dq[h]
                + jnp.dot(keys_flipped[h * HEAD_DIM : (h + 1) * HEAD_DIM], slopes, preferred_element_type=F32)
            )
        return tuple(out), dk, dv

    def unturn(grad, cos_tab, sin_tab):
        return grad * cos_tab - swap_halves(grad) * sin_tab

    def step(index, carry):
        dq, sum_k, sum_v = carry
        first = pl.multiple_of(index * block, block)
        where = pl.ds(first, block)
        at = lax.broadcasted_iota(jnp.int32, (block, rows), 0) + index * block
        dq, dk, dv = fold(dq, kc_ref[where, :], vc_ref[where, :], at < limit)
        dk = unturn(dk, cos_ref[where, :], sin_ref[where, :])
        dkv_ref[where, pl.ds(here, LANES)] = dk.astype(BF16)
        dkv_ref[where, pl.ds(width + here, LANES)] = dv.astype(BF16)
        return dq, sum_k + jnp.sum(dk, 0, keepdims=True), sum_v + jnp.sum(dv, 0, keepdims=True)

    zero_q = jnp.zeros((HEAD_DIM, rows), F32)
    zero_sum = jnp.zeros((1, LANES), F32)
    dq, sum_k, sum_v = lax.fori_loop(0, length // block, step, ((zero_q, zero_q), zero_sum, zero_sum))

    dq, dk, dv = fold(dq, kn_ref[...], vn_ref[...], own_mask(low, high, noisy))
    dk = unturn(dk, cos_own_ref[:noisy, :], sin_own_ref[:noisy, :])
    dq = unturn(jnp.concatenate(dq, 0).T * SCALE, cos_own_ref[...], sin_own_ref[...])
    zeros = jnp.zeros((rows - noisy, LANES), BF16)
    for part, grad in enumerate((dq, dk, dv)):
        down_ref[: grad.shape[0], pl.ds(part * width + here, LANES)] = grad.astype(BF16)
        if part > 0:
            down_ref[noisy:, pl.ds(part * width + here, LANES)] = zeros
    sums = (
        jnp.sum(dq, 0, keepdims=True),
        sum_k + jnp.sum(dk, 0, keepdims=True),
        sum_v + jnp.sum(dv, 0, keepdims=True),
    )
    for part in range(3):
        sum_ref[:, pl.ds(part * width + here, LANES)] = jnp.broadcast_to(sums[part], (8, LANES))


def attend_back(scalars, own, s, seqs, clean, attn, grad, log_total, cos_own, sin_own, cos_tab, sin_tab, block):
    rows = own.shape[0] // seqs
    length, both = clean.shape
    pairs = own.shape[1] // (3 * LANES)
    spec = pltpu.PrefetchScalarGridSpec(
        num_scalar_prefetch=1,
        grid=(pairs,),
        in_specs=[
            pl.BlockSpec((rows, LANES), lambda p, c: (s, p)),
            pl.BlockSpec((rows // 2, LANES), lambda p, c: (2 * s, pairs + p)),
            pl.BlockSpec((rows // 2, LANES), lambda p, c: (2 * s, 2 * pairs + p)),
            pl.BlockSpec((length, LANES), lambda p, c: (0, p)),
            pl.BlockSpec((length, LANES), lambda p, c: (0, pairs + p)),
            pl.BlockSpec((rows, LANES), lambda p, c: (0, p)),
            pl.BlockSpec((rows, LANES), lambda p, c: (0, p)),
            pl.BlockSpec((1, 8, rows), lambda p, c: (p, 0, 0)),
            pl.BlockSpec((rows, LANES), lambda p, c: (0, 0)),
            pl.BlockSpec((rows, LANES), lambda p, c: (0, 0)),
            pl.BlockSpec((length, LANES), lambda p, c: (0, 0)),
            pl.BlockSpec((length, LANES), lambda p, c: (0, 0)),
        ],
        out_specs=[
            pl.BlockSpec((length, both), lambda p, c: (0, 0)),
            pl.BlockSpec((rows, own.shape[1]), lambda p, c: (0, 0)),
            pl.BlockSpec((8, own.shape[1]), lambda p, c: (0, 0)),
        ],
    )
    return pl.pallas_call(
        functools.partial(attend_back_kernel, block=block),
        grid_spec=spec,
        out_shape=[
            jax.ShapeDtypeStruct((length, both), BF16),
            jax.ShapeDtypeStruct((rows, own.shape[1]), BF16),
            jax.ShapeDtypeStruct((8, own.shape[1]), F32),
        ],
        compiler_params=pltpu.CompilerParams(vmem_limit_bytes=VMEM_LIMIT),
        cost_estimate=LIGHT,
        name="attend_back",
    )(scalars, own, own, own, clean, clean, attn, grad, log_total, cos_own, sin_own, cos_tab, sin_tab)


def feed_forward_kernel(
    core_ref, attn_ref, x_ref, top_ref, up_ref, down_ref, out_ref, tile_ref,
    block_out_ref, hidden_grad_ref, own_grad_ref, far_grad_ref, weights_ref, mine_ref, theirs_ref,
    vec_ref, hidden, unit, inverse, normed, normed_flipped, lowered, grad_normed,
    up_grads, join_grads, down_grads, out_grads, vec_grads, sums, up_sems, join_sems, down_sems, last_sems,
    *, pairs, joined
):
    chunk = pl.program_id(0)
    chunks = pl.num_programs(0)
    width = x_ref.shape[1]

    @pl.when(chunk == 0)
    def _():
        vec_ref[...] = tile_ref[...].astype(F32).T
        value = (
            x_ref[...].astype(F32)
            + jnp.dot(attn_ref[...], out_ref[...], preferred_element_type=F32)
            + vec_ref[0:1, :]
        )
        hidden[...] = value
        center = value - jnp.mean(value, -1, keepdims=True)
        scale = lax.rsqrt(jnp.mean(center * center, -1, keepdims=True) + EPSILON)
        inverse[...] = scale
        unit[...] = center * scale
        scaled = unit[...] * vec_ref[1:2, :] + vec_ref[2:3, :]
        normed[...] = scaled.astype(BF16)
        normed_flipped[...] = scaled.T.astype(BF16)
        lowered[...] = jnp.zeros_like(lowered)
        grad_normed[...] = jnp.zeros_like(grad_normed)
        sums[...] = jnp.zeros_like(sums)

    upper = jnp.dot(normed[...], up_ref[...], preferred_element_type=F32) + vec_ref[pl.ds(4 + chunk, 1), :]
    grad_activ = nt_dot(top_ref[...], down_ref[...])
    square = upper * upper
    half = 0.5 + 0.5 * jnp.tanh(upper * (0.7978845608028654 + 0.035677408136300125 * square))
    activ = upper * half
    slope = half + activ * (1.0 - half) * (1.5957691216057308 + 0.21406444881780075 * square)
    grad_upper = grad_activ * slope
    grad_low = grad_upper.astype(BF16)
    sums[pl.ds(4 + chunk, 1), :] = jnp.sum(grad_upper, 0, keepdims=True)
    lowered[...] += jnp.dot(activ.astype(BF16), down_ref[...], preferred_element_type=F32)
    grad_normed[...] += nt_dot(grad_low, up_ref[...])
    up_grads[chunk] = jnp.dot(normed_flipped[...], grad_low, preferred_element_type=F32).astype(BF16)
    down_grad = jnp.dot(activ.T.astype(BF16), top_ref[...], preferred_element_type=F32).astype(BF16)
    shard = width // (2 * pairs)

    @pl.when(chunk < joined)
    def _():
        join_grads[chunk] = down_grad

    @pl.when(chunk >= joined)
    def _():
        for pair in range(pairs):
            for core in range(2):
                first = (2 * pair + core) * shard
                down_grads[chunk - joined, core, pair * shard : (pair + 1) * shard, :] = down_grad[first : first + shard]

    def copy_up(index):
        columns = pl.ds(pl.multiple_of(index * width, width), width)
        return pltpu.make_async_copy(up_grads.at[index], weights_ref.at[:, columns], up_sems.at[index])

    def copy_join(index):
        columns = pl.ds(pl.multiple_of((chunks + index) * width, width), width)
        return pltpu.make_async_copy(join_grads.at[index], weights_ref.at[:, columns], join_sems.at[index])

    def copy_down(index):
        columns = pl.ds(pl.multiple_of(index * width, width), width)
        core = core_ref[0]
        return (
            pltpu.make_async_copy(down_grads.at[index, core], mine_ref.at[:, columns], down_sems.at[0, index]),
            pltpu.make_async_copy(down_grads.at[index, 1 - core], theirs_ref.at[:, columns], down_sems.at[1, index]),
        )

    copy_up(chunk).start()

    @pl.when(chunk < joined)
    def _():
        copy_join(chunk).start()

    @pl.when(chunk >= joined)
    def _():
        for copy in copy_down(chunk - joined):
            copy.start()

    @pl.when(chunk == chunks - 1)
    def _():
        top = top_ref[...].astype(F32)
        block_out_ref[...] = (hidden[...] + lowered[...] + vec_ref[3:4, :]).astype(BF16)
        grad = grad_normed[...]
        rows_unit = unit[...]
        sums[1:2, :] = jnp.sum(grad * rows_unit, 0, keepdims=True)
        sums[2:3, :] = jnp.sum(grad, 0, keepdims=True)
        sums[3:4, :] = jnp.sum(top, 0, keepdims=True)
        grad = grad * vec_ref[1:2, :]
        grad = inverse[...] * (
            grad - jnp.mean(grad, -1, keepdims=True) - rows_unit * jnp.mean(grad * rows_unit, -1, keepdims=True)
        )
        grad = top + grad
        hidden_grad_ref[...] = grad
        sums[0:1, :] = jnp.sum(grad, 0, keepdims=True)
        low = grad.astype(BF16)
        attn_grad = nt_dot(low, out_ref[...]).astype(BF16)
        for core in range(2):
            own, far = core * (width // 2), (1 - core) * (width // 2)

            @pl.when(core_ref[0] == core)
            def _():
                own_grad_ref[...] = attn_grad[:, own : own + width // 2]
                far_grad_ref[...] = attn_grad[:, far : far + width // 2]

        out_grads[...] = jnp.dot(
            attn_ref[...].astype(F32).T.astype(BF16), low, preferred_element_type=F32
        ).astype(BF16)
        vec_grads[...] = sums[...].T.astype(BF16)
        first = (chunks + joined) * width
        copies = [
            pltpu.make_async_copy(out_grads, weights_ref.at[:, pl.ds(first, width)], last_sems.at[0]),
            pltpu.make_async_copy(vec_grads, weights_ref.at[:, pl.ds(first + width, LANES)], last_sems.at[1]),
        ]
        for copy in copies:
            copy.start()
        for index in range(up_grads.shape[0]):
            copy_up(index).wait()
        for index in range(joined):
            copy_join(index).wait()
        for index in range(down_grads.shape[0]):
            for copy in copy_down(index):
                copy.wait()
        for copy in copies:
            copy.wait()


def feed_forward(core, attn, x, top, weights, chunks, pairs, joined):
    rows, width = x.shape
    apart = chunks - joined
    fixed = lambda b, c: (0, 0)
    whole = pl.BlockSpec((rows, width), fixed)
    halved = pl.BlockSpec((rows, width // 2), fixed)
    spec = pltpu.PrefetchScalarGridSpec(
        num_scalar_prefetch=1,
        grid=(chunks,),
        in_specs=[
            whole,
            whole,
            whole,
            pl.BlockSpec((width, width), lambda b, c: (0, b)),
            pl.BlockSpec((width, width), lambda b, c: (0, chunks + b)),
            pl.BlockSpec((width, width), lambda b, c: (0, 2 * chunks)),
            pl.BlockSpec((width, LANES), lambda b, c: (0, weights.shape[1] // LANES - 1)),
        ],
        out_specs=[whole, whole, halved, halved] + [pl.BlockSpec(memory_space=pl.ANY)] * 3,
        scratch_shapes=[
            pltpu.VMEM((LANES, width), F32),
            pltpu.VMEM((rows, width), F32),
            pltpu.VMEM((rows, width), F32),
            pltpu.VMEM((rows, 1), F32),
            pltpu.VMEM((rows, width), BF16),
            pltpu.VMEM((width, rows), BF16),
            pltpu.VMEM((rows, width), F32),
            pltpu.VMEM((rows, width), F32),
            pltpu.VMEM((chunks, width, width), BF16),
            pltpu.VMEM((joined, width, width), BF16),
            pltpu.VMEM((apart, 2, width // 2, width), BF16),
            pltpu.VMEM((width, width), BF16),
            pltpu.VMEM((width, LANES), BF16),
            pltpu.VMEM((LANES, width), F32),
            pltpu.SemaphoreType.DMA((chunks,)),
            pltpu.SemaphoreType.DMA((joined,)),
            pltpu.SemaphoreType.DMA((2, apart)),
            pltpu.SemaphoreType.DMA((2,)),
        ],
    )
    return pl.pallas_call(
        functools.partial(feed_forward_kernel, pairs=pairs, joined=joined),
        grid_spec=spec,
        out_shape=[
            jax.ShapeDtypeStruct((rows, width), BF16),
            jax.ShapeDtypeStruct((rows, width), F32),
            jax.ShapeDtypeStruct((rows, width // 2), BF16),
            jax.ShapeDtypeStruct((rows, width // 2), BF16),
            jax.ShapeDtypeStruct((width, weights.shape[1] - apart * width), BF16),
            jax.ShapeDtypeStruct((width // 2, apart * width), BF16),
            jax.ShapeDtypeStruct((width // 2, apart * width), BF16),
        ],
        compiler_params=pltpu.CompilerParams(vmem_limit_bytes=VMEM_LIMIT),
        cost_estimate=LIGHT,
        name="feed_forward",
    )(core.reshape(1), attn, x, top, weights, weights, weights, weights)


def after(value, *others):
    return lax.optimization_barrier((value,) + others)[0]


def pick(array, index, axis=0):
    return lax.dynamic_index_in_dim(array, index, axis, keepdims=False)


def ordered(flag, own, other, axis):
    return jnp.stack([jnp.where(flag == 0, own, other), jnp.where(flag == 0, other, own)], axis)


class Links:
    def __init__(self):
        self.count = lax.axis_size("ctx")
        self.deep = self.count // 4
        at = lax.axis_index("ctx")
        self.x = lax.axis_index("batch")
        self.core = at % 2
        self.y = (at // 2) % 2
        self.z = at // 4
        self.chip = at // 2

    def over_core(self, array):
        return lax.ppermute(array, "ctx", [(i, i ^ 1) for i in range(self.count)])

    def over_y(self, array):
        return lax.ppermute(array, "ctx", [(i, i ^ 2) for i in range(self.count)])

    def over_x(self, array):
        return lax.ppermute(array, "batch", [(0, 1), (1, 0)])

    def along_z(self, array, hop):
        count = self.count
        return lax.ppermute(array, "ctx", [(i, (i + 4 * hop) % count) for i in range(count)])

    def around_z(self, piece):
        return [self.along_z(piece, hop) for hop in range(1, self.deep)]

    def column(self, piece, others):
        deep = self.deep
        whole = jnp.broadcast_to(piece[None], (deep,) + piece.shape)
        for hop, other in enumerate(others, 1):
            whole = lax.dynamic_update_index_in_dim(whole, other, (self.z - hop) % deep, 0)
        return whole

    def swap_z(self, parts):
        return [self.along_z(pick(parts, (self.z + hop) % self.deep), hop) for hop in range(1, self.deep)]

    def sum_z(self, parts, others):
        total = pick(parts, self.z).astype(F32)
        for other in others:
            total = total + other.astype(F32)
        return total


def unit_rows(values):
    center = values - jnp.mean(values, -1, keepdims=True)
    spread = jnp.mean(center * center, -1, keepdims=True)
    inverse = lax.rsqrt(spread + EPSILON)
    return center * inverse, inverse


def unit_back(grad, unit, inverse):
    return inverse * (
        grad - jnp.mean(grad, -1, keepdims=True) - unit * jnp.mean(grad * unit, -1, keepdims=True)
    )


def rotary_tables(positions):
    half_dim = HEAD_DIM // 2
    inverse = 1.0 / THETA ** (jnp.arange(half_dim, dtype=F32) / half_dim)
    angles = positions.astype(F32)[:, None] * jnp.tile(inverse, LANES // half_dim)[None, :]
    sign = jnp.where(jnp.arange(LANES) % HEAD_DIM < half_dim, -1.0, 1.0)
    return jnp.cos(angles), jnp.sin(angles) * sign[None, :]


def key_block(length, limit):
    sizes = [size for size in range(16, limit + 1, 16) if length % size == 0]
    return sizes[-1] if sizes else length


def row_block(rows):
    for block in (512, 384, 256, 128, 64, 32, 16):
        if rows % block == 0:
            return block
    return rows


def dot(a, b):
    return jnp.dot(a, b, preferred_element_type=F32)


def dot_left(a, b):
    return lax.dot_general(a, b, (((0,), (0,)), ((), ())), preferred_element_type=F32)


def on_device(
    layer_input, cotangent, prefix, block_size, ln1_gain, ln1_bias, qkv_weight, qkv_bias, out_weight, out_bias,
    ln2_gain, ln2_bias, up_weight, up_bias, down_weight, down_bias,
):
    links = Links()
    core = links.core
    seqs, _, pos_dev, width = layer_input.shape
    devices = 2 * links.count
    length = links.count * pos_dev
    half = width // 2
    rows = 4 * pos_dev
    shard = ln1_gain.shape[0]
    hidden_shard = up_bias.shape[0]

    split = qkv_weight.reshape(shard, 3, 2, half)
    vec_one = jnp.concatenate([ln1_gain, ln1_bias, qkv_bias])
    vec_one = ordered(core, vec_one, links.over_core(vec_one), 0).reshape(1, -1)
    vec_one = jnp.pad(vec_one, ((0, 7), (0, width - vec_one.shape[1])))
    qkv_piece = ordered(core, pick(split, core, 2), links.over_core(pick(split, 1 - core, 2)), 0)
    qkv_piece = qkv_piece.reshape(2 * shard, 3 * half)
    cos_tab, sin_tab = rotary_tables(after(jnp.arange(length, dtype=jnp.int32), qkv_piece))
    first_pos = links.chip * 2 * pos_dev
    cos_own = jnp.tile(lax.dynamic_slice_in_dim(cos_tab, first_pos, 2 * pos_dev, 0), (2, 1))
    sin_own = jnp.tile(lax.dynamic_slice_in_dim(sin_tab, first_pos, 2 * pos_dev, 0), (2, 1))
    block = key_block(length, 1536)
    scalars = [jnp.stack([prefix[s], block_size[s], first_pos]) for s in range(seqs)]
    qkv_others = links.around_z(qkv_piece)
    inputs_got = links.over_core(layer_input)
    qkv_column = jnp.stack([qkv_piece] + qkv_others)
    qkv_got = links.over_y(qkv_column)
    qkv_far = links.over_x(qkv_column)
    clean_piece = jnp.concatenate([layer_input[0, 1], vec_one])
    clean_piece = after(clean_piece, cos_tab, sin_tab, inputs_got, *qkv_others)
    clean_others = links.around_z(clean_piece)
    gate = (qkv_got, qkv_far) + tuple(clean_others)
    weights_gate = gate
    qkv_last = links.over_x(after(qkv_got, *gate))
    hops = jnp.arange(links.deep, dtype=jnp.int32)
    levels = (links.z - hops) % links.deep
    arrived = []
    for s in range(seqs):
        column = after(jnp.stack([clean_piece] + clean_others), *gate)
        got = links.over_y(column)
        gate = (got,)
        if s + 1 < seqs:
            clean_piece = after(layer_input[s + 1, 1], column)
            clean_others = links.around_z(clean_piece)
            gate = gate + tuple(clean_others)
        if s == 0:
            vec_near = jnp.stack([column[:, pos_dev], got[:, pos_dev]])
            vec_far = links.over_x(after(vec_near, *gate[1:]))
            gate = gate + (qkv_last,)
        arrived.append((column, got, links.over_core(column)))
    where = jnp.concatenate(
        [(x * links.deep + levels) * 2 + y for x in (links.x, 1 - links.x) for y in (links.y, 1 - links.y)]
    )
    qkv_mat = place([qkv_column, qkv_got, qkv_far, qkv_last], where, 2 * shard)
    vec_one = jnp.concatenate([vec_near, vec_far]).reshape(where.shape[0], width).astype(F32)
    turn = (where[None, :] == jnp.arange(where.shape[0], dtype=jnp.int32)[:, None]).astype(F32)
    vec_one = jnp.dot(turn, vec_one[:, : 2 * (2 * shard + qkv_bias.shape[0])], precision=lax.Precision.HIGHEST)
    vec_one = vec_one.reshape(devices, -1)
    gain_one = vec_one[:, :shard].reshape(1, width)
    bias_one = vec_one[:, shard : 2 * shard].reshape(1, width)
    qkv_add = pick(vec_one[:, 2 * shard :].reshape(3, 2, half), core, 1).reshape(1, 3 * half)

    folds = hidden_shard // shard
    up_piece = up_weight.reshape(shard, devices, folds, shard).transpose(0, 2, 1, 3).reshape(shard, -1)
    down_piece = down_weight.reshape(folds, shard, width).transpose(1, 0, 2).reshape(shard, -1)
    vec_piece = jnp.stack(
        [out_bias, ln2_gain, ln2_bias, down_bias] + [up_bias[i * shard : (i + 1) * shard] for i in range(folds)], 1
    )
    vec_piece = jnp.pad(vec_piece, ((0, 0), (0, LANES - vec_piece.shape[1])))
    packed = after(jnp.concatenate([up_piece, down_piece, out_weight, vec_piece], 1), *weights_gate)
    weights = lax.all_gather(packed, ("batch", "ctx"), axis=0, tiled=True)

    inputs_pair = ordered(core, layer_input, inputs_got, 2).reshape(seqs, rows, width)

    own_qkv, own_unit = project(
        inputs_pair.reshape(seqs * rows, width), gain_one, bias_one, qkv_mat, qkv_add,
        cos_own, sin_own, 0, width, row_block(rows),
    )
    clean_kv, clean_unit, attn_list, log_list = ([] for _ in range(4))
    for s in range(seqs):
        column, got, column_far = arrived[s]
        got = after(got, *([clean_kv[-1]] if s else [own_qkv]))
        where = jnp.stack([links.z] + [y * 2 + c for c in (core, 1 - core) for y in (links.y, 1 - links.y)])
        clean, all_unit = project_parts(
            where, [column, got, column_far, links.over_core(got)], pos_dev,
            gain_one, bias_one, qkv_mat, qkv_add, cos_tab, sin_tab, half, half,
        )
        attn, log_total = attend(scalars[s], own_qkv, s, seqs, clean, block)
        for kept, value in zip(
            (clean_kv, clean_unit, attn_list, log_list),
            (clean, all_unit, attn, log_total),
        ):
            kept.append(value)

    attn_rows = jnp.stack(attn_list).reshape(seqs, 2, 2, pos_dev, half)
    attn_got = links.over_core(pick(attn_rows, 1 - core, 2))
    attn_low = ordered(core, pick(attn_rows, core, 2), attn_got, 3).reshape(-1, width)
    flat_inputs = layer_input.reshape(-1, width)
    joined = folds * 3 // 4
    apart = folds - joined
    output, grad_hidden, grad_mine, grad_theirs, weight_grads, down_mine, down_theirs = feed_forward(
        core, attn_low, flat_inputs, cotangent.reshape(-1, width), weights, folds, links.count, joined
    )
    output = output.reshape(layer_input.shape)
    packed = lax.psum_scatter(weight_grads, ("batch", "ctx"), scatter_dimension=0, tiled=True)
    down_got = links.over_core(down_theirs)
    down_part = (down_mine.astype(F32) + down_got.astype(F32)).astype(BF16)
    down_part = down_part.reshape(2, links.deep, 2, shard * apart, width)
    down_sent = pick(down_part, 1 - links.x)
    down_got = links.over_x(down_sent)

    grad_got = links.over_core(grad_theirs)
    grad_rows = ordered(
        core,
        grad_mine.reshape(seqs, 2, pos_dev, half),
        grad_got.reshape(seqs, 2, pos_dev, half),
        2,
    ).reshape(seqs, rows, half)
    kv_mat = qkv_mat[:, half:]
    own_unit = own_unit.reshape(seqs, rows, width)
    unit_part = jnp.zeros((width, 3 * half), F32)
    kv_part = jnp.zeros((width, 2 * half), F32)
    column_sums = 0.0
    waiting, gate = [], ()
    for s in range(seqs):
        clean_grad, own_grad, sums = attend_back(
            scalars[s], own_qkv, s, seqs, clean_kv[s], attn_list[s], after(grad_rows[s], *gate),
            log_list[s], cos_own, sin_own, cos_tab, sin_tab, block,
        )
        spread = lax.dot_general(clean_grad, kv_mat, NT, preferred_element_type=F32).astype(BF16)
        local = lax.dot_general(own_grad, qkv_mat, NT, preferred_element_type=F32).astype(BF16)
        spread = spread.reshape(2 * links.deep, 2, pos_dev, width)
        local = local.reshape(2, 2, pos_dev, width)
        theirs = jnp.concatenate([pick(spread, 1 - core, 1), pick(local, 1 - core, 1)])
        got = links.over_core(theirs)
        gate = (theirs,)
        if s == seqs - 1:
            down_got = after(down_got, own_grad)
            down_part = (pick(down_part, links.x).astype(F32) + down_got.astype(F32)).astype(BF16)
            down_sent = pick(down_part, 1 - links.y, 1)
            down_got = links.over_y(down_sent)
            gate = (theirs, down_sent)
        unit_part = unit_part + dot_left(own_unit[s], after(own_grad, *gate))
        kv_part = kv_part + dot_left(clean_unit[s], after(clean_grad, *gate))
        column_sums = column_sums + sums[0]
        if s == seqs - 1:
            qkv_part = (unit_part + jnp.pad(kv_part, ((0, 0), (half, 0)))).astype(BF16)
            qkv_part = qkv_part.reshape(2, links.deep, 2, 2 * shard, 3 * half)
            far_part = pick(qkv_part, 1 - links.x)
            qkv_far = links.over_x(far_part)
        mine = pick(spread, core, 1).astype(F32) + got[: 2 * links.deep].astype(F32)
        mine = mine.astype(BF16).reshape(links.deep, 2, pos_dev, width)
        local = pick(local, core, 1).astype(F32) + got[2 * links.deep :].astype(F32)
        if s == seqs - 1:
            below = jnp.pad(column_sums, (0, 8 * width - 3 * half)).astype(BF16).reshape(1, 1, 8, width)
            mine = jnp.concatenate([mine, jnp.broadcast_to(below, (links.deep, 2, 8, width))], 2)
        theirs = pick(mine, 1 - links.y, 1)
        row_got = links.over_y(theirs)
        waiting.append((mine, local, row_got))
        gate = (theirs, down_sent)
    down_part = pick(after(down_part, far_part), links.y, 1).astype(F32)
    down_part = (down_part + down_got.astype(F32)).astype(BF16)
    summed = []
    for mine, _, row_got in waiting:
        mine = (pick(mine, links.y, 1).astype(F32) + after(row_got, far_part).astype(F32)).astype(BF16)
        summed.append(mine)
    first = jnp.concatenate(summed[:-1] + [down_part], 1)
    first_others = links.swap_z(first)
    others = links.swap_z(summed[-1])
    total = links.sum_z(summed[-1], others)
    first_others = after(tuple(first_others), summed[-1])
    first = links.sum_z(first, first_others)
    own_rows = [
        jnp.stack([local[0], local[1] + (first[s * pos_dev : (s + 1) * pos_dev] if s < seqs - 1 else total[:pos_dev])])
        for s, (_, local, _) in enumerate(waiting)
    ]
    down_sum = first[(seqs - 1) * pos_dev :]
    column_sums = total[pos_dev:].reshape(-1)[: 3 * half].reshape(3, half)
    column_sums = column_sums + links.over_x(column_sums)
    column_sums = ordered(core, column_sums, links.over_core(column_sums), 1).reshape(3 * width)

    grad_normed_one = jnp.stack(own_rows).reshape(-1, width)
    unit_one, inverse_one = unit_rows(after(flat_inputs, far_part).astype(F32))
    grad_input = grad_hidden + unit_back(grad_normed_one * gain_one, unit_one, inverse_one)
    grad_input = grad_input.astype(BF16).reshape(layer_input.shape)

    qkv_part = (pick(after(qkv_part, packed), links.x).astype(F32) + qkv_far.astype(F32)).astype(BF16)
    qkv_far = links.over_y(after(pick(qkv_part, 1 - links.y, 1), waiting[-1][2]))
    qkv_part = (pick(qkv_part, links.y, 1).astype(F32) + qkv_far.astype(F32)).astype(BF16)
    qkv_part = after(qkv_part, summed[-1])
    qkv_sum = links.sum_z(qkv_part, links.swap_z(qkv_part)).reshape(2, shard, 3, half)
    qkv_got = links.over_core(pick(qkv_sum, 1 - core))
    qkv_sum = ordered(core, pick(qkv_sum, core), qkv_got, 2).reshape(shard, 3 * width)
    grad_qkv = ln1_gain.astype(F32)[:, None] * qkv_sum + ln1_bias.astype(F32)[:, None] * column_sums[None, :]
    own_weight = qkv_weight.astype(F32)
    grad_gain_one = jnp.sum(own_weight * qkv_sum, -1)
    grad_bias_one = jnp.sum(own_weight * column_sums[None, :], -1)
    device = links.x * links.count + lax.axis_index("ctx")
    grad_qk_bias = lax.dynamic_slice_in_dim(column_sums[: 2 * width], device * 2 * shard, 2 * shard, 0)
    grad_value_bias = lax.dynamic_slice_in_dim(column_sums[2 * width :], device * shard, shard, 0)

    hidden_width = devices * hidden_shard
    packed = packed.astype(F32)
    grad_up = packed[:, :hidden_width].reshape(shard, folds, devices, shard).transpose(0, 2, 1, 3)
    grad_up = grad_up.reshape(shard, hidden_width)
    first_down = packed[:, hidden_width : hidden_width + joined * width].reshape(shard, joined, width)
    grad_down = jnp.concatenate([first_down, down_sum.reshape(shard, apart, width)], 1)
    grad_down = grad_down.transpose(1, 0, 2).reshape(hidden_shard, width)
    grad_out = packed[:, hidden_width + joined * width : -LANES]
    late = packed[:, -LANES:].T

    return (
        output, grad_input, grad_gain_one, grad_bias_one, grad_qkv, grad_qk_bias, grad_value_bias, grad_out,
        late[0], late[1], late[2], grad_up, late[4 : 4 + folds].reshape(-1), grad_down, late[3],
    )


def solution(mesh):
    every = P(("batch", "ctx"))
    matrix = P(("batch", "ctx"), None)
    acts = P("batch", None, "ctx", None)
    return jax.shard_map(
        on_device,
        mesh=mesh,
        in_specs=(
            acts, acts, P("batch"), P("batch"), every, every, matrix, every, matrix, every, every, every, matrix,
            every, matrix, every,
        ),
        out_specs=(
            acts, acts, every, every, matrix, every, every, matrix, every, every, every, matrix, every, matrix, every,
        ),
        check_vma=False,
    )
```
